128 devices in a mesh: slab: 4 (over z), grp: 32 (over y, x, core).
Axes of the slice: x: 4, y: 4, z: 4, core: 2. Of those that a mesh axis runs over, the one named last changes fastest.
Arguments:
- samples: float32 [131072, 6, 128], P(('slab', 'grp')), as said below
- block_ids: int32 [131072], P(('slab', 'grp')), may hold values from 0 to 131071, as said below
- tile_counts: int32 [131072], P(('slab', 'grp')), may hold values from 0 to 128
- occupied: int32 [8, 64, 256], P('slab', 'grp'), may hold values 0 or 1
- coupling: float32 [27, 64, 64], replicated, may hold values from -0.06 to 0.06
Outputs:
- solution_field: float32 [64, 8, 64, 256], P(None, 'slab', 'grp')
- residual: float32 [64, 8, 64, 256], P(None, 'slab', 'grp')
The draws below stay inside these ranges and needn't reach their ends.
Inputs may be any that keep to these rules, and one draw needn't show every extreme that they name: `samples`: the first three components of every sample lie in [0, 1). `block_ids`: slot j * 8 + c of a device's slots (c below 8) carries a block whose x // 2 is the slab index and y // 2 the grp index of the device of linear index j over slab then grp; ids number blocks as (x * 64 + y) * 256 + z; every block is named by exactly one slot over all devices.
All inputs are finite; a program needn't handle non-finite values. No bound on the sum of `occupied` on one device may be relied on, other than what follows from the above.
Results may differ from the reference program's by a relative error of at most 0.0003.
Values sent between devices are 32-bit elements; how exact they have to be, the bound alone decides.
No kernel may reach another device: no remote copies, remote signals or barrier semaphores. Data moves between devices by JAX's collectives and lax.ppermute only.
A program may use at most 128 MiB of HBM per device.

```python
import jax
import jax.numpy as jnp
from jax import lax

NODES = 64
TILE = 128
BX = 2
BY = 2
BZ = 256
ITERS = 3
GX = 8
GY = 64
CAP = 8
SLOTS = 131072
N_SLAB = 4
N_GRP = 32


def draw_samples(key, part):
    key_pos, key_dir = jax.random.split(key, 2)
    position = jax.random.uniform(key_pos, (SLOTS, 3, TILE), jnp.float32, 0.0, 0.999)
    normals = jnp.clip(jax.random.normal(key_dir, (SLOTS, 3, TILE), jnp.float32), -4.0, 4.0)
    return jnp.concatenate([position, normals], axis=1)


def draw_block_ids(key, part):
    per_slab = GY // BY
    devs = GX // BX * per_slab
    blocks = BX * BY * BZ
    keys = jax.random.split(key, devs)
    orders = jax.vmap(lambda single: jax.random.permutation(single, blocks))(keys).astype(jnp.int32)
    position = jnp.arange(SLOTS, dtype=jnp.int32)
    source = position // (CAP * devs)
    target = position // CAP % devs
    lane = position % CAP
    local = orders[target, source * CAP + lane]
    block_x = target // per_slab * BX + local // (BY * BZ)
    block_y = target % per_slab * BY + local // BZ % BY
    block_z = local % BZ
    return (block_x * GY + block_y) * BZ + block_z


def draw_tile_counts(key, part):
    raw = jax.random.randint(key, (SLOTS,), 0, 2 * TILE, jnp.int32)
    counts = jnp.minimum(raw, TILE)
    return counts.at[0].set(TILE).at[SLOTS - 1].set(0)


def place_ends(result, rng, least, largest):
    extent = result.shape
    spot = [jax.random.randint(jax.random.fold_in(rng, axis), (), 0, extent[axis]) for axis in range(len(extent))]
    result = result.at[tuple(spot)].set(least)
    longest = extent.index(max(extent))
    spot[longest] = (spot[longest] + 1) % extent[longest]
    return result.at[tuple(spot)].set(largest)


def scatter_about(stream_key, extent, spread, reach, kind=jnp.bfloat16):
    return jnp.clip(spread * jax.random.normal(stream_key, extent, jnp.float32), -reach, reach).astype(kind)


def setup_inputs(seed: int = 0) -> dict:
    seeds = jax.random.split(jax.random.key(seed), 6)
    samples = draw_samples(jax.random.fold_in(seeds[5], 71), 0)
    block_ids = draw_block_ids(jax.random.fold_in(seeds[5], 71), 0)
    tile_counts = draw_tile_counts(jax.random.fold_in(seeds[5], 71), 0)
    occupied = place_ends((jax.random.randint(seeds[3], (GX, GY, BZ), 0, 10) < 7).astype(jnp.int32), jax.random.fold_in(seeds[3], 1), 0, 1)
    coupling = scatter_about(seeds[4], (27, NODES, NODES), 0.01, 0.06, jnp.float32)
    return {"samples": samples, "block_ids": block_ids, "tile_counts": tile_counts, "occupied": occupied, "coupling": coupling}


HIGH = lax.Precision.HIGHEST


def bspline_value(diff):
    mag = jnp.abs(diff)
    return jnp.where(mag < 0.5, 0.75 - mag * mag, jnp.where(mag < 1.5, 0.5 * (1.5 - mag) ** 2, 0.0))


def bspline_slope(diff):
    mag = jnp.abs(diff)
    outer = -(1.5 - mag) * diff / jnp.maximum(mag, 0.5)
    return jnp.where(mag < 0.5, -2.0 * diff, jnp.where(mag < 1.5, outer, 0.0))


def splat_tiles(tile_data, counts):
    slots = tile_data.shape[0]
    width = tile_data.shape[2]
    lanes = jnp.arange(width, dtype=jnp.int32)[None, :]
    valid = (lanes < counts[:, None]).astype(jnp.float32)
    centres = jnp.arange(4, dtype=jnp.float32) + 0.5
    diff = 4.0 * tile_data[:, 0:3, :][:, :, None, :] - centres[None, None, :, None]
    values = bspline_value(diff)
    slopes = 4.0 * bspline_slope(diff)
    normals = tile_data[:, 3:6, :] * valid[:, None, :]
    pair_val = (values[:, 1][:, :, None, :] * values[:, 2][:, None, :, :]).reshape(slots, 16, width)
    pair_dy = (slopes[:, 1][:, :, None, :] * values[:, 2][:, None, :, :]).reshape(slots, 16, width)
    pair_dz = (values[:, 1][:, :, None, :] * slopes[:, 2][:, None, :, :]).reshape(slots, 16, width)
    term_x = jnp.einsum('tis,tks->tik', slopes[:, 0] * normals[:, 0][:, None, :], pair_val, precision=HIGH)
    term_y = jnp.einsum('tis,tks->tik', values[:, 0] * normals[:, 1][:, None, :], pair_dy, precision=HIGH)
    term_z = jnp.einsum('tis,tks->tik', values[:, 0] * normals[:, 2][:, None, :], pair_dz, precision=HIGH)
    dens = jnp.einsum('tis,tks->tik', values[:, 0] * valid[:, None, :], pair_val, precision=HIGH)
    rhs = (term_x + term_y + term_z).reshape(slots, 64)
    return jnp.concatenate([rhs, dens.reshape(slots, 64)], axis=1)


def symmetric_blocks(coupling):
    coupled = 0.5 * (coupling + jnp.transpose(jnp.flip(coupling, 0), (0, 2, 1)))
    rowabs = jnp.sum(jnp.abs(coupled), axis=(0, 2))
    return coupled, rowabs


def apply_stiffness(field, padded, coupled, diag, mask):
    nodes, size_x, size_y, size_z = field.shape
    total = jnp.zeros((nodes, size_x * size_y * size_z), jnp.float32)
    for offset in range(27):
        shift_x = offset // 9
        shift_y = offset // 3 % 3
        shift_z = offset % 3
        piece = padded[:, shift_x:shift_x + size_x, shift_y:shift_y + size_y, shift_z:shift_z + size_z]
        total = total + jnp.dot(coupled[offset], piece.reshape(nodes, -1), precision=HIGH)
    return diag * field - mask * total.reshape(field.shape)


def reference(samples, block_ids, tile_counts, occupied, coupling):
    devs = N_SLAB * N_GRP
    grouped = samples.reshape(devs, SLOTS // devs, 6, TILE)
    grouped_counts = tile_counts.reshape(devs, SLOTS // devs)
    contrib = lax.map(lambda pair: splat_tiles(pair[0], pair[1]), (grouped, grouped_counts))
    contrib = contrib.reshape(SLOTS, 128)
    summed = jax.ops.segment_sum(contrib, block_ids, num_segments=GX * GY * BZ)
    grid = summed.T.reshape(2, 64, GX, GY, BZ)
    right_side = grid[0]
    density = grid[1]
    coupled, rowabs = symmetric_blocks(coupling)
    diag = rowabs[:, None, None, None] + 0.5 + 4.0 * density
    mask = occupied.astype(jnp.float32)[None]

    def operate(field):
        padded = jnp.pad(field * mask, ((0, 0), (1, 1), (1, 1), (1, 1)))
        return apply_stiffness(field, padded, coupled, diag, mask)

    solution_field = jnp.zeros_like(right_side)
    residual = right_side
    direction = right_side
    norm_now = jnp.sum(residual * residual)
    for step in range(ITERS):
        image = operate(direction)
        alpha = norm_now / jnp.sum(direction * image)
        solution_field = solution_field + alpha * direction
        residual = residual - alpha * image
        norm_next = jnp.sum(residual * residual)
        direction = residual + (norm_next / norm_now) * direction
        norm_now = norm_next
    return solution_field, residual
```

```python
import functools

import jax
import jax.numpy as jnp
from jax import lax
from jax.experimental import pallas as pl
from jax.experimental.pallas import tpu as pltpu
from jax.sharding import PartitionSpec as P

AXES = ("slab", "grp")
F32 = jnp.float32
BF16 = jnp.bfloat16
N_COLS = 4
BZ = 256
NODES = 64
SENDERS = 128
CAP = 8
ROWS = CAP + 1


def lane_iota(shape):
    return lax.broadcasted_iota(jnp.int32, shape, len(shape) - 1)


def row_iota(shape):
    return lax.broadcasted_iota(jnp.int32, shape, 0)


def basis_of(pos):
    u = 4.0 * pos
    cell = jnp.floor(u)
    w = u - cell
    rest = 1.0 - w
    low = 0.5 * (rest * rest)
    high = 0.5 * (w * w)
    off = w - 0.5
    mid = 0.75 - off * off
    slow = -4.0 * rest
    shigh = 4.0 * w
    smid = -8.0 * off
    at = [cell == float(i) for i in range(4)]
    zero = jnp.zeros_like(u)
    values, slopes = [], []
    for i in range(4):
        val, slo = zero, zero
        if i + 1 < 4:
            val = jnp.where(at[i + 1], low, val)
            slo = jnp.where(at[i + 1], slow, slo)
        if i - 1 >= 0:
            val = jnp.where(at[i - 1], high, val)
            slo = jnp.where(at[i - 1], shigh, slo)
        values.append(jnp.where(at[i], mid, val))
        slopes.append(jnp.where(at[i], smid, slo))
    return values, slopes


def splat_kernel(samp_ref, cnt_ref, ids_ref, out_ref, flip, basis, acc, stats):
    step = pl.program_id(0)
    last = pl.num_programs(0) - 1

    @pl.when(step == 0)
    def _():
        stats[...] = jnp.zeros_like(stats)

    for k in range(6):
        flip[k] = samp_ref[k].T
    counts = cnt_ref[pl.ds(step, 1), :]

    def evaluate(group, carry):
        rows = pl.ds(pl.multiple_of(group * 8, 8), 8)
        valid = (row_iota((8, 128)) + group * 8 < counts).astype(F32)
        n0 = flip[3, rows, :] * valid
        n1 = flip[4, rows, :] * valid
        n2 = flip[5, rows, :] * valid
        val, slo = basis_of(flip[0, rows, :])
        for i in range(4):
            basis[i, rows, :] = slo[i] * n0
            basis[4 + i, rows, :] = val[i] * n1
            basis[8 + i, rows, :] = val[i] * n2
            basis[12 + i, rows, :] = val[i] * valid
        for d in (1, 2):
            val, slo = basis_of(flip[d, rows, :])
            for i in range(4):
                basis[8 + 8 * d + i, rows, :] = val[i]
                basis[12 + 8 * d + i, rows, :] = slo[i]
        return carry

    lax.fori_loop(0, 16, evaluate, 0, unroll=2)

    for i in range(4):
        def add_group(group, sums, i=i):
            rows = pl.ds(pl.multiple_of(group * 8, 8), 8)
            a = basis[i, rows, :]
            b = basis[4 + i, rows, :]
            c = basis[8 + i, rows, :]
            d = basis[12 + i, rows, :]
            v2 = [basis[24 + l, rows, :] for l in range(4)]
            s2 = [basis[28 + l, rows, :] for l in range(4)]
            out = list(sums)
            for j in range(4):
                v1 = basis[16 + j, rows, :]
                s1 = basis[20 + j, rows, :]
                first = a * v1 + b * s1
                second = c * v1
                dens = d * v1
                for l in range(4):
                    at = j * 4 + l
                    out[at] = out[at] + (first * v2[l] + second * s2[l])
                    out[16 + at] = out[16 + at] + dens * v2[l]
            return tuple(out)

        zero = jnp.zeros((8, 128), F32)
        sums = lax.fori_loop(0, 16, add_group, (zero,) * 32, unroll=2)
        for at in range(16):
            acc[pl.ds((i * 16 + at) * 8, 8), :] = sums[at]
            acc[pl.ds((64 + i * 16 + at) * 8, 8), :] = sums[16 + at]

    total = acc[pl.ds(0, 128, stride=8), :]
    for s in range(1, 8):
        total = total + acc[pl.ds(s, 128, stride=8), :]
    square = total[:64] * total[:64]
    weighted = total[64:] * square
    part, wpart = square[:8], weighted[:8]
    for k in range(1, 8):
        part = part + square[8 * k : 8 * k + 8]
        wpart = wpart + weighted[8 * k : 8 * k + 8]
    stats[0] = stats[0] + part
    stats[1] = stats[1] + wpart
    by_tile = total.T
    for d in range(16):
        out_ref[step, pl.ds(ROWS * d, 8), :] = by_tile[8 * d : 8 * d + 8]

    @pl.when(step == last)
    def _():
        ids = ids_ref[...]
        local = ((ids >> 14) & 1) * 512 + ((ids >> 8) & 1) * 256 + (ids & 255)
        local = local.astype(F32)
        sum0 = jnp.sum(stats[0], keepdims=True)
        sum1 = jnp.sum(stats[1], keepdims=True)
        lanes = lane_iota((1, 128))
        both = jnp.where(lanes % 2 == 0, sum0, sum1)
        for g in range(8):
            for d in range(16):
                row = jnp.where(lanes // 8 == d, local[g : g + 1], both)
                out_ref[g, pl.ds(ROWS * d + CAP, 1), :] = row


def splat(samples, counts, ids):
    tiles = samples.shape[0]
    groups = tiles // 128
    return pl.pallas_call(
        splat_kernel,
        name="splat",
        grid=(groups,),
        in_specs=[
            pl.BlockSpec((6, 128, 128), lambda g: (0, g, 0)),
            pl.BlockSpec((groups, 128), lambda g: (0, 0)),
            pl.BlockSpec((groups, 128), lambda g: (0, 0)),
        ],
        out_specs=pl.BlockSpec((groups, 16 * ROWS, 128), lambda g: (0, 0, 0)),
        out_shape=jax.ShapeDtypeStruct((groups, 16 * ROWS, 128), F32),
        scratch_shapes=[
            pltpu.VMEM((6, 128, 128), F32),
            pltpu.VMEM((32, 128, 128), F32),
            pltpu.VMEM((1024, 128), F32),
            pltpu.VMEM((2, 8, 128), F32),
        ],
    )(jnp.transpose(samples, (1, 0, 2)), counts.reshape(groups, 128), ids.reshape(groups, 128))


def assemble_kernel(seat_ref, recv_ref, mask_ref, rowabs_ref, v_ref, mv_ref, diag_ref, maskc_ref, c_ref, turned):
    seat = seat_ref[0]
    turned[...] = recv_ref[pl.ds(CAP, SENDERS, stride=ROWS), :].T
    where = turned[pl.ds(pl.multiple_of(seat * 8, 8), 8), :].astype(jnp.int32)
    other = lax.rem(seat + 1, 16)
    sums = turned[pl.ds(pl.multiple_of(other * 8, 8), 8), :]
    sum0 = jnp.sum(sums[0:1, :], keepdims=True)
    sum1 = jnp.sum(sums[1:2, :], keepdims=True)
    rowabs = rowabs_ref[...]
    mean = jnp.sum(rowabs[:, 0:1], keepdims=True) * (1.0 / NODES)
    centre = mean + 0.5 + 4.0 * (sum1 / sum0)
    inverse = 1.0 / centre
    c_ref[...] = jnp.broadcast_to(centre, (8, 128))
    tiles = []
    for c in range(CAP):
        block = recv_ref[pl.ds(c, SENDERS, stride=ROWS), :]
        high = block.astype(BF16)
        low = (block - high.astype(F32)).astype(BF16)
        tiles.append(jnp.concatenate([high, low], axis=1))
    table = jnp.concatenate(tiles, axis=0)
    for col in range(N_COLS):
        picks = []
        for c in range(CAP):
            hit = row_iota((BZ, SENDERS)) + col * BZ == where[c : c + 1, :]
            picks.append(hit.astype(F32).astype(BF16))
        pick = jnp.concatenate(picks, axis=1)
        both = jnp.dot(pick, table, preferred_element_type=F32)
        ordered = (both[:, :128] + both[:, 128:]).T
        rhs = ordered[:NODES]
        dens = ordered[NODES:]
        lanes = pl.ds(col * BZ, BZ)
        mask = mask_ref[0:1, lanes]
        v_ref[:, lanes] = rhs
        mv_ref[:, lanes] = rhs * mask
        diag = rowabs[:, 0:1] + 0.5 + 4.0 * dens
        diag_ref[:, lanes] = (diag - centre) * inverse
        maskc_ref[:, lanes] = jnp.broadcast_to(mask * inverse, (8, BZ))


def assemble(seat, recv, mask, rowabs):
    blocks = N_COLS * BZ
    field = jax.ShapeDtypeStruct((NODES, blocks), F32)
    return pl.pallas_call(
        assemble_kernel,
        name="assemble",
        in_specs=[pl.BlockSpec(memory_space=pltpu.SMEM)] + [pl.BlockSpec(memory_space=pltpu.VMEM)] * 3,
        out_specs=[pl.BlockSpec(memory_space=pltpu.VMEM)] * 5,
        out_shape=[field, field, field, jax.ShapeDtypeStruct((8, blocks), F32), jax.ShapeDtypeStruct((8, 128), F32)],
        scratch_shapes=[pltpu.VMEM((128, 128), F32)],
    )(seat, recv, mask, rowabs)


def apply_kernel(first, flag_ref, v_ref, mv_ref, diag_ref, mask_ref, maskc_ref, xl_ref, xh_ref, yl_ref, yh_ref,
                 w_ref, mom_ref, o_ref, mo_ref, mo_mom_ref, high, low):
    edges = [flag_ref[k] for k in range(4)]
    for px in range(4):
        for py in range(4):
            if py in (0, 3):
                src = (yl_ref if py == 0 else yh_ref)[:, pl.ds(px * BZ, BZ)]
                src = src * edges[2 if py == 0 else 3]
            elif px in (0, 3):
                src = (xl_ref if px == 0 else xh_ref)[:, pl.ds((py - 1) * BZ, BZ)]
            else:
                src = mv_ref[:, pl.ds(((px - 1) * 2 + py - 1) * BZ, BZ)]
            if px in (0, 3):
                src = src * edges[0 if px == 0 else 1]
            top = src.astype(BF16)
            rows = pl.ds((px * 4 + py) * NODES, NODES)
            high[rows, :] = top
            low[rows, :] = (src - top.astype(F32)).astype(BF16)
    lanes = lane_iota((NODES, BZ))
    sq = jnp.zeros((NODES, BZ), F32)
    cross = jnp.zeros((NODES, BZ), F32)
    for ox in range(2):
        for oy in range(2):
            full = jnp.zeros((6 * NODES, BZ), F32)
            half = jnp.zeros((3 * NODES, BZ), F32)
            for dx in range(3):
                rows = pl.ds(((ox + dx) * 4 + oy) * NODES, 3 * NODES)
                cols = pl.ds(dx * 3 * NODES, 3 * NODES)
                full = full + jnp.dot(w_ref[dx], high[rows, :], preferred_element_type=F32)
                half = half + jnp.dot(w_ref[dx, 0 : 3 * NODES, :], low[rows, :], preferred_element_type=F32)
            part = full[: 3 * NODES] + full[3 * NODES :] + half
            before = jnp.where(lanes == 0, 0.0, pltpu.roll(part[:NODES], 1, 1))
            after = jnp.where(lanes == BZ - 1, 0.0, pltpu.roll(part[2 * NODES :], BZ - 1, 1))
            total = part[NODES : 2 * NODES] + before + after
            at = pl.ds((ox * 2 + oy) * BZ, BZ)
            v = v_ref[:, at]
            new = diag_ref[:, at] * v - maskc_ref[0:1, at] * total
            o_ref[:, at] = new
            mo_ref[:, at] = new * mask_ref[0:1, at]
            sq = sq + v * v
            cross = cross + v * new
    sq = jnp.sum(sq, keepdims=True)
    cross = jnp.sum(cross, keepdims=True)
    spot = lane_iota((1, 128))
    mom = jnp.where(spot == first, sq, jnp.where(spot == first + 1, cross, mom_ref[0:1, :]))
    mo_mom_ref[...] = jnp.broadcast_to(mom, mo_mom_ref.shape)


def apply_stiffness(order, flags, v, mv, diag, mask, maskc, halos, weights, moments):
    blocks = N_COLS * BZ
    field = jax.ShapeDtypeStruct((NODES, blocks), F32)
    moment_rows = SENDERS if order == 2 else 8
    return pl.pallas_call(
        functools.partial(apply_kernel, 2 * order),
        name="stiffness",
        in_specs=[pl.BlockSpec(memory_space=pltpu.SMEM)] + [pl.BlockSpec(memory_space=pltpu.VMEM)] * 11,
        out_specs=[pl.BlockSpec(memory_space=pltpu.VMEM)] * 3,
        out_shape=[field, field, jax.ShapeDtypeStruct((moment_rows, 128), F32)],
        scratch_shapes=[pltpu.VMEM((16 * NODES, BZ), BF16), pltpu.VMEM((16 * NODES, BZ), BF16)],
    )(flags, v, mv, diag, mask, maskc, *halos, weights, moments)


def finish_kernel(mom_ref, c_ref, v0_ref, v1_ref, v2_ref, v3_ref, x_ref, r_ref):
    row = jnp.sum(mom_ref[...], axis=0, keepdims=True)
    lanes = lane_iota((1, 128))
    m = [jnp.sum(jnp.where(lanes == k, row, 0.0), keepdims=True) for k in range(6)]
    zero = jnp.zeros((1, 1), F32)
    one = jnp.ones((1, 1), F32)

    def inner(f, g):
        total = zero
        for i, a in enumerate(f):
            for j, b in enumerate(g):
                if a is not None and b is not None:
                    total = total + a * b * m[i + j]
        return total

    r = [one, None, None, None]
    p = [one, None, None, None]
    x = [None, None, None]
    norm = m[0]

    def plus(a, b):
        if a is None:
            return b
        return a if b is None else a + b

    for step in range(3):
        image = [plus(p[k], p[k - 1] if k else None) for k in range(4)]
        alpha = norm / inner(p, image)
        for k in range(3):
            if p[k] is not None:
                x[k] = plus(x[k], alpha * p[k])
        for k in range(4):
            if image[k] is not None:
                r[k] = plus(r[k], -(alpha * image[k]))
        if step < 2:
            new = inner(r, r)
            beta = new / norm
            p = [plus(r[k], None if p[k] is None else beta * p[k]) for k in range(4)]
            norm = new
    inverse = 1.0 / c_ref[0:1, 0:1]
    x = [value * inverse for value in x]
    for chunk in range(8):
        bx, by, zt = chunk // 4, chunk // 2 % 2, chunk % 2
        spot = bx * 4 + zt * 2 + by
        at = pl.ds(chunk * 128, 128)
        v0, v1, v2, v3 = v0_ref[:, at], v1_ref[:, at], v2_ref[:, at], v3_ref[:, at]
        x_ref[:, spot, :] = x[0] * v0 + x[1] * v1 + x[2] * v2
        r_ref[:, spot, :] = r[0] * v0 + r[1] * v1 + r[2] * v2 + r[3] * v3


def finish(moments, centre, fields):
    out = jax.ShapeDtypeStruct((NODES, 8, 128), F32)
    return pl.pallas_call(
        finish_kernel,
        name="finish",
        in_specs=[pl.BlockSpec(memory_space=pltpu.VMEM)] * 6,
        out_specs=[pl.BlockSpec(memory_space=pltpu.VMEM)] * 2,
        out_shape=[out, out],
    )(moments, centre, *fields)


def stencil_weights(coupling):
    coupled = 0.5 * (coupling + jnp.transpose(jnp.flip(coupling, 0), (0, 2, 1)))
    rowabs = jnp.sum(jnp.abs(coupled), axis=(0, 2))
    stacked = jnp.transpose(coupled.reshape(3, 3, 3, NODES, NODES), (0, 2, 3, 1, 4))
    stacked = stacked.reshape(3, 3 * NODES, 3 * NODES)
    high = lax.reduce_precision(stacked, 8, 7)
    both = jnp.concatenate([high, stacked - high], axis=1).astype(BF16)
    return both, jnp.broadcast_to(rowabs[:, None], (NODES, 128))


def ring(axis, move):
    count = lax.axis_size(axis)
    return [(i, (i + move) % count) for i in range(count)]


def exchange(field):
    half = field.shape[1] // 2
    xl = lax.ppermute(field[:, half:], "slab", ring("slab", 1))
    xh = lax.ppermute(field[:, :half], "slab", ring("slab", -1))
    first = jnp.concatenate([xl[:, :BZ], field[:, :BZ], field[:, half : half + BZ], xh[:, :BZ]], axis=1)
    final = jnp.concatenate([xl[:, BZ:], field[:, BZ:half], field[:, half + BZ :], xh[:, BZ:]], axis=1)
    yh = lax.ppermute(first, "grp", ring("grp", -1))
    yl = lax.ppermute(final, "grp", ring("grp", 1))
    return xl, xh, yl, yh


def on_device(samples, block_ids, tile_counts, occupied, coupling):
    slab, grp = lax.axis_index("slab"), lax.axis_index("grp")
    payload = splat(samples, tile_counts, block_ids)
    recv = lax.all_to_all(payload.reshape(SENDERS, 1, ROWS * 128), AXES, split_axis=0, concat_axis=0, tiled=True)
    weights, rowabs = stencil_weights(coupling)
    mask = jnp.broadcast_to(occupied.astype(F32).reshape(1, N_COLS * BZ), (8, N_COLS * BZ))
    flags = jnp.stack([slab > 0, slab < lax.axis_size("slab") - 1, grp > 0, grp < lax.axis_size("grp") - 1]).astype(F32)
    seat = (grp % 16).astype(jnp.int32).reshape(1)
    v, mv, diag, maskc, centre = assemble(seat, recv.reshape(SENDERS * ROWS, 128), mask, rowabs)
    fields = [v]
    moments = jnp.zeros((8, 128), F32)
    for order in range(3):
        v, mv, moments = apply_stiffness(order, flags, v, mv, diag, mask, maskc, exchange(mv), weights, moments)
        fields.append(v)
    shared = lax.all_to_all(moments.reshape(SENDERS, 1, 128), AXES, split_axis=0, concat_axis=0, tiled=True)
    outs = finish(shared.reshape(SENDERS, 128), centre, fields)

    def place(out):
        out = out.reshape(NODES, 2, 2, 2, 128)
        return jnp.transpose(out, (0, 1, 3, 2, 4)).reshape(NODES, 2, 2, BZ)

    return place(outs[0]), place(outs[1])


def solution(mesh):
    placed = (P(AXES, None, None), P(AXES), P(AXES), P("slab", "grp", None), P())
    return jax.shard_map(
        on_device,
        mesh=mesh,
        in_specs=placed,
        out_specs=(P(None, "slab", "grp", None), P(None, "slab", "grp", None)),
        check_vma=False,
    )
```

```python
import functools

import jax
import jax.numpy as jnp
from jax import lax
from jax.experimental import pallas as pl
from jax.experimental.pallas import tpu as pltpu
from jax.sharding import PartitionSpec as P

AXES = ("slab", "grp")
F32 = jnp.float32
BF16 = jnp.bfloat16
N_COLS = 4
BZ = 256
NODES = 64
SENDERS = 128
CAP = 8
ROWS = CAP + 1


def lane_iota(shape):
    return lax.broadcasted_iota(jnp.int32, shape, len(shape) - 1)


def row_iota(shape):
    return lax.broadcasted_iota(jnp.int32, shape, 0)


def basis_of(pos):
    u = 4.0 * pos
    cell = jnp.floor(u)
    w = u - cell
    rest = 1.0 - w
    low = 0.5 * (rest * rest)
    high = 0.5 * (w * w)
    off = w - 0.5
    mid = 0.75 - off * off
    slow = -4.0 * rest
    shigh = 4.0 * w
    smid = -8.0 * off
    at = [cell == float(i) for i in range(4)]
    zero = jnp.zeros_like(u)
    values, slopes = [], []
    for i in range(4):
        val, slo = zero, zero
        if i + 1 < 4:
            val = jnp.where(at[i + 1], low, val)
            slo = jnp.where(at[i + 1], slow, slo)
        if i - 1 >= 0:
            val = jnp.where(at[i - 1], high, val)
            slo = jnp.where(at[i - 1], shigh, slo)
        values.append(jnp.where(at[i], mid, val))
        slopes.append(jnp.where(at[i], smid, slo))
    return values, slopes


def splat_kernel(samp_ref, cnt_ref, ids_ref, out_ref, flip, basis, acc, stats):
    step = pl.program_id(0)
    last = pl.num_programs(0) - 1

    @pl.when(step == 0)
    def _():
        stats[...] = jnp.zeros_like(stats)

    for k in range(6):
        flip[k] = samp_ref[k].T
    counts = cnt_ref[pl.ds(step, 1), :]

    def evaluate(group, carry):
        rows = pl.ds(pl.multiple_of(group * 8, 8), 8)
        valid = (row_iota((8, 128)) + group * 8 < counts).astype(F32)
        n0 = flip[3, rows, :] * valid
        n1 = flip[4, rows, :] * valid
        n2 = flip[5, rows, :] * valid
        val, slo = basis_of(flip[0, rows, :])
        for i in range(4):
            basis[i, rows, :] = slo[i] * n0
            basis[4 + i, rows, :] = val[i] * n1
            basis[8 + i, rows, :] = val[i] * n2
            basis[12 + i, rows, :] = val[i] * valid
        for d in (1, 2):
            val, slo = basis_of(flip[d, rows, :])
            for i in range(4):
                basis[8 + 8 * d + i, rows, :] = val[i]
                basis[12 + 8 * d + i, rows, :] = slo[i]
        return carry

    lax.fori_loop(0, 16, evaluate, 0, unroll=2)

    for i in range(4):
        def add_group(group, sums, i=i):
            rows = pl.ds(group * 8, 8)
            a = basis[i, rows, :]
            b = basis[4 + i, rows, :]
            c = basis[8 + i, rows, :]
            d = basis[12 + i, rows, :]
            v2 = [basis[24 + l, rows, :] for l in range(4)]
            s2 = [basis[28 + l, rows, :] for l in range(4)]
            out = list(sums)
            for j in range(4):
                v1 = basis[16 + j, rows, :]
                s1 = basis[20 + j, rows, :]
                first = a * v1 + b * s1
                second = c * v1
                dens = d * v1
                for l in range(4):
                    at = j * 4 + l
                    out[at] = out[at] + (first * v2[l] + second * s2[l])
                    out[16 + at] = out[16 + at] + dens * v2[l]
            return tuple(out)

        zero = jnp.zeros((8, 128), F32)
        sums = (zero,) * 32
        for group in range(16):
            sums = add_group(group, sums)
        for at in range(16):
            acc[pl.ds((i * 16 + at) * 8, 8), :] = sums[at]
            acc[pl.ds((64 + i * 16 + at) * 8, 8), :] = sums[16 + at]

    total = acc[pl.ds(0, 128, stride=8), :]
    for s in range(1, 8):
        total = total + acc[pl.ds(s, 128, stride=8), :]
    square = total[:64] * total[:64]
    weighted = total[64:] * square
    part, wpart = square[:8], weighted[:8]
    for k in range(1, 8):
        part = part + square[8 * k : 8 * k + 8]
        wpart = wpart + weighted[8 * k : 8 * k + 8]
    stats[0] = stats[0] + part
    stats[1] = stats[1] + wpart
    by_tile = total.T
    for d in range(16):
        out_ref[step, pl.ds(ROWS * d, 8), :] = by_tile[8 * d : 8 * d + 8]

    @pl.when(step == last)
    def _():
        ids = ids_ref[...]
        local = ((ids >> 14) & 1) * 512 + ((ids >> 8) & 1) * 256 + (ids & 255)
        local = local.astype(F32)
        sum0 = jnp.sum(stats[0], keepdims=True)
        sum1 = jnp.sum(stats[1], keepdims=True)
        lanes = lane_iota((1, 128))
        both = jnp.where(lanes % 2 == 0, sum0, sum1)
        for g in range(8):
            for d in range(16):
                row = jnp.where(lanes // 8 == d, local[g : g + 1], both)
                out_ref[g, pl.ds(ROWS * d + CAP, 1), :] = row


def splat(samples, counts, ids):
    tiles = samples.shape[0]
    groups = tiles // 128
    return pl.pallas_call(
        splat_kernel,
        name="splat",
        grid=(groups,),
        in_specs=[
            pl.BlockSpec((6, 128, 128), lambda g: (0, g, 0)),
            pl.BlockSpec((groups, 128), lambda g: (0, 0)),
            pl.BlockSpec((groups, 128), lambda g: (0, 0)),
        ],
        out_specs=pl.BlockSpec((groups, 16 * ROWS, 128), lambda g: (0, 0, 0)),
        out_shape=jax.ShapeDtypeStruct((groups, 16 * ROWS, 128), F32),
        scratch_shapes=[
            pltpu.VMEM((6, 128, 128), F32),
            pltpu.VMEM((32, 128, 128), F32),
            pltpu.VMEM((1024, 128), F32),
            pltpu.VMEM((2, 8, 128), F32),
        ],
    )(jnp.transpose(samples, (1, 0, 2)), counts.reshape(groups, 128), ids.reshape(groups, 128))


def vmem(x):
    return pltpu.with_memory_space_constraint(x, pltpu.VMEM)


def parity_weights(place_ref):
    slab, grp = place_ref[0], place_ref[1]
    slabs, grps = place_ref[2], place_ref[3]

    def pick(cond):
        return jnp.where(cond, 1.0, 0.0).astype(F32)

    def sides(at, count):
        odd = at % 2 == 1
        low = (pick(odd), pick(jnp.logical_and(jnp.logical_not(odd), at > 0)))
        high = (pick(jnp.logical_not(odd)), pick(jnp.logical_and(odd, at < count - 1)))
        return low, high

    return sides(slab, slabs), sides(grp, grps)


def blend(pair, a, b):
    return a * pair[0] + b * pair[1]


def column(x, y):
    return pl.ds((x * 2 + y) * BZ, BZ)


def store_edges(place_ref, masked, ea_ref, eb_ref, oa_ref, ob_ref):
    up_slab = place_ref[0] % 2 == 0
    up_grp = place_ref[1] % 2 == 0
    for k in range(2):
        at = pl.ds(k * BZ, BZ)
        ea_ref[:, at] = jnp.where(up_slab, masked[1][k], masked[0][k])
        eb_ref[:, at] = jnp.where(up_slab, masked[0][k], masked[1][k])
        oa_ref[:, at] = jnp.where(up_grp, masked[k][1], masked[k][0])
        ob_ref[:, at] = jnp.where(up_grp, masked[k][0], masked[k][1])


def prepare_kernel(coupling_ref, occ_ref, w_ref, rowabs_ref, mask_ref):
    total = jnp.zeros((NODES, NODES), F32)
    for dx in range(3):
        for dz in range(3):
            parts = []
            for dy in range(3):
                k = (dx * 3 + dy) * 3 + dz
                coupled = 0.5 * (coupling_ref[k] + coupling_ref[26 - k].T)
                total = total + jnp.abs(coupled)
                parts.append(coupled)
            wide = jnp.concatenate(parts, axis=1)
            high = wide.astype(BF16)
            w_ref[dx, pl.ds(dz * NODES, NODES), :] = high
            w_ref[dx, pl.ds((3 + dz) * NODES, NODES), :] = (wide - high.astype(F32)).astype(BF16)
    rowabs_ref[...] = jnp.broadcast_to(jnp.sum(total, axis=1, keepdims=True), (NODES, 128))
    for x in range(2):
        for y in range(2):
            mask_ref[:, column(x, y)] = jnp.broadcast_to(occ_ref[x, y : y + 1, :].astype(F32), (8, BZ))


def prepare(coupling, occupied):
    return pl.pallas_call(
        prepare_kernel,
        name="prepare",
        in_specs=[pl.BlockSpec(memory_space=pltpu.VMEM)] * 2,
        out_specs=[pl.BlockSpec(memory_space=pltpu.VMEM)] * 3,
        out_shape=[
            pltpu.VMEM((3, 6 * NODES, 3 * NODES), BF16),
            pltpu.VMEM((NODES, 128), F32),
            pltpu.VMEM((8, N_COLS * BZ), F32),
        ],
        compiler_params=pltpu.CompilerParams(vmem_limit_bytes=8 << 20),
        cost_estimate=pl.CostEstimate(flops=10**7, transcendentals=0, bytes_accessed=4 * 10**6),
    )(coupling, occupied)


def assemble_kernel(place_ref, recv_ref, mask_ref, rowabs_ref, v_ref, diag_ref, maskc_ref, c_ref,
                    ea_ref, eb_ref, oa_ref, ob_ref, turned):
    seat = place_ref[1] % 16
    turned[...] = recv_ref[pl.ds(CAP, SENDERS, stride=ROWS), :].T
    where = turned[pl.ds(pl.multiple_of(seat * 8, 8), 8), :].astype(jnp.int32)
    other = lax.rem(seat + 1, 16)
    sums = turned[pl.ds(pl.multiple_of(other * 8, 8), 8), :]
    sum0 = jnp.sum(sums[0:1, :], keepdims=True)
    sum1 = jnp.sum(sums[1:2, :], keepdims=True)
    rowabs = rowabs_ref[...]
    mean = jnp.sum(rowabs[:, 0:1], keepdims=True) * (1.0 / NODES)
    centre = mean + 0.5 + 4.0 * (sum1 / sum0)
    inverse = 1.0 / centre
    c_ref[...] = jnp.broadcast_to(centre, (8, 128))
    tiles = []
    for c in range(CAP):
        block = recv_ref[pl.ds(c, SENDERS, stride=ROWS), :]
        high = block.astype(BF16)
        low = (block - high.astype(F32)).astype(BF16)
        tiles.append(jnp.concatenate([high, low], axis=1))
    table = jnp.concatenate(tiles, axis=0)
    masked = []
    for x in range(2):
        masked.append([])
        for y in range(2):
            picks = []
            for c in range(CAP):
                hit = row_iota((BZ, SENDERS)) + (x * 2 + y) * BZ == where[c : c + 1, :]
                picks.append(hit.astype(F32).astype(BF16))
            pick = jnp.concatenate(picks, axis=1)
            both = jnp.dot(pick, table, preferred_element_type=F32)
            ordered = (both[:, :128] + both[:, 128:]).T
            rhs = ordered[:NODES]
            dens = ordered[NODES:]
            mask = mask_ref[0:1, column(x, y)]
            v_ref[:, column(x, y)] = rhs
            diag = rowabs[:, 0:1] + 0.5 + 4.0 * dens
            diag_ref[:, column(x, y)] = (diag - centre) * inverse
            maskc_ref[:, column(x, y)] = jnp.broadcast_to(mask * inverse, (8, BZ))
            masked[x].append(rhs * mask)
    store_edges(place_ref, masked, ea_ref, eb_ref, oa_ref, ob_ref)


FIELD = pltpu.VMEM((NODES, N_COLS * BZ), F32)
EDGE = pltpu.VMEM((NODES, 2 * BZ), F32)


def in_specs(count):
    return [pl.BlockSpec(memory_space=pltpu.SMEM)] + [pl.BlockSpec(memory_space=pltpu.VMEM)] * count


def assemble(place, recv, mask, rowabs):
    return pl.pallas_call(
        assemble_kernel,
        name="assemble",
        in_specs=in_specs(3),
        out_specs=[pl.BlockSpec(memory_space=pltpu.VMEM)] * 8,
        out_shape=[FIELD, FIELD, pltpu.VMEM((8, N_COLS * BZ), F32), pltpu.VMEM((8, 128), F32), EDGE, EDGE, EDGE, EDGE],
        scratch_shapes=[pltpu.VMEM((128, 128), F32)],
        compiler_params=pltpu.CompilerParams(vmem_limit_bytes=16 << 20),
    )(place, vmem(recv), vmem(mask), vmem(rowabs))


def apply_kernel(order, place_ref, v_ref, diag_ref, mask_ref, maskc_ref, ra_ref, rb_ref, ga_ref, gb_ref, w_ref, *rest):
    rest = list(rest)
    mom_ref = rest.pop(0) if order else None
    o_ref, mom_out = rest[:2]
    edges = rest[2:-2]
    high, low = rest[-2:]
    (x_low, x_high), (y_low, y_high) = parity_weights(place_ref)
    last = len(edges) == 0

    def put(px, py, src):
        top = src.astype(BF16)
        rows = pl.ds((px * 4 + py) * NODES, NODES)
        high[rows, :] = top
        low[rows, :] = (src - top.astype(F32)).astype(BF16)

    for x in range(2):
        for y in range(2):
            put(x + 1, y + 1, v_ref[:, column(x, y)] * mask_ref[0:1, column(x, y)])
    for y in range(2):
        at = pl.ds(y * BZ, BZ)
        put(0, y + 1, blend(x_low, ra_ref[:, at], rb_ref[:, at]))
        put(3, y + 1, blend(x_high, ra_ref[:, at], rb_ref[:, at]))
    for py, pair in ((0, y_low), (3, y_high)):
        line = [blend(pair, ga_ref[:, pl.ds(k * BZ, BZ)], gb_ref[:, pl.ds(k * BZ, BZ)]) for k in range(4)]
        put(1, py, line[1])
        put(2, py, line[2])
        put(0, py, blend(x_low, line[0], line[3]))
        put(3, py, blend(x_high, line[0], line[3]))
    lanes = lane_iota((NODES, BZ))
    sq = jnp.zeros((NODES, BZ), F32)
    cross = jnp.zeros((NODES, BZ), F32)
    masked = []
    for x in range(2):
        masked.append([])
        for y in range(2):
            full = jnp.zeros((6 * NODES, BZ), F32)
            half = jnp.zeros((3 * NODES, BZ), F32)
            for dx in range(3):
                rows = pl.ds(((x + dx) * 4 + y) * NODES, 3 * NODES)
                full = full + jnp.dot(w_ref[dx], high[rows, :], preferred_element_type=F32)
                half = half + jnp.dot(w_ref[dx, 0 : 3 * NODES, :], low[rows, :], preferred_element_type=F32)
            part = full[: 3 * NODES] + full[3 * NODES :] + half
            before = jnp.where(lanes == 0, 0.0, pltpu.roll(part[:NODES], 1, 1))
            after = jnp.where(lanes == BZ - 1, 0.0, pltpu.roll(part[2 * NODES :], BZ - 1, 1))
            total = part[NODES : 2 * NODES] + before + after
            at = column(x, y)
            v = v_ref[:, at]
            new = diag_ref[:, at] * v - maskc_ref[0:1, at] * total
            o_ref[:, at] = new
            masked[x].append(new * mask_ref[0:1, at])
            sq = sq + v * v
            cross = cross + v * new
    if not last:
        store_edges(place_ref, masked, *edges)
    sq = jnp.sum(sq, keepdims=True)
    cross = jnp.sum(cross, keepdims=True)
    spot = lane_iota((1, 128))
    before = mom_ref[0:1, :] if order else jnp.zeros((1, 128), F32)
    mom = jnp.where(spot == 2 * order, sq, jnp.where(spot == 2 * order + 1, cross, before))
    mom_out[...] = jnp.broadcast_to(mom, mom_out.shape)


def apply_stiffness(order, place, v, diag, mask, maskc, halos, weights, moments):
    more = [] if moments is None else [moments]
    last = order == 2
    moment = jax.ShapeDtypeStruct((SENDERS, 128), F32) if last else pltpu.VMEM((8, 128), F32)
    shapes = [FIELD, moment] + ([] if last else [EDGE] * 4)
    operands = [v, diag, mask, maskc, *halos, weights] + more
    return pl.pallas_call(
        functools.partial(apply_kernel, order),
        name="stiffness",
        in_specs=in_specs(len(operands)),
        out_specs=[pl.BlockSpec(memory_space=pltpu.VMEM)] * len(shapes),
        out_shape=shapes,
        scratch_shapes=[pltpu.VMEM((16 * NODES, BZ), BF16), pltpu.VMEM((16 * NODES, BZ), BF16)],
        compiler_params=pltpu.CompilerParams(vmem_limit_bytes=16 << 20),
    )(place, *[vmem(x) for x in operands])


def finish_kernel(mom_ref, c_ref, v0_ref, v1_ref, v2_ref, v3_ref, x_ref, r_ref):
    row = jnp.sum(mom_ref[...], axis=0, keepdims=True)
    lanes = lane_iota((1, 128))
    m = [jnp.sum(jnp.where(lanes == k, row, 0.0), keepdims=True) for k in range(6)]
    zero = jnp.zeros((1, 1), F32)
    one = jnp.ones((1, 1), F32)

    def inner(f, g):
        total = zero
        for i, a in enumerate(f):
            for j, b in enumerate(g):
                if a is not None and b is not None:
                    total = total + a * b * m[i + j]
        return total

    r = [one, None, None, None]
    p = [one, None, None, None]
    x = [None, None, None]
    norm = m[0]

    def plus(a, b):
        if a is None:
            return b
        return a if b is None else a + b

    for step in range(3):
        image = [plus(p[k], p[k - 1] if k else None) for k in range(4)]
        alpha = norm / inner(p, image)
        for k in range(3):
            if p[k] is not None:
                x[k] = plus(x[k], alpha * p[k])
        for k in range(4):
            if image[k] is not None:
                r[k] = plus(r[k], -(alpha * image[k]))
        if step < 2:
            new = inner(r, r)
            beta = new / norm
            p = [plus(r[k], None if p[k] is None else beta * p[k]) for k in range(4)]
            norm = new
    inverse = 1.0 / c_ref[0:1, 0:1]
    x = [value * inverse for value in x]
    for chunk in range(8):
        bx, by, zt = chunk // 4, chunk // 2 % 2, chunk % 2
        spot = bx * 4 + zt * 2 + by
        at = pl.ds(chunk * 128, 128)
        v0, v1, v2, v3 = v0_ref[:, at], v1_ref[:, at], v2_ref[:, at], v3_ref[:, at]
        x_ref[:, spot, :] = x[0] * v0 + x[1] * v1 + x[2] * v2
        r_ref[:, spot, :] = r[0] * v0 + r[1] * v1 + r[2] * v2 + r[3] * v3


def finish(moments, centre, fields):
    out = jax.ShapeDtypeStruct((NODES, 8, 128), F32)
    return pl.pallas_call(
        finish_kernel,
        name="finish",
        in_specs=[pl.BlockSpec(memory_space=pltpu.VMEM)] * 6,
        out_specs=[pl.BlockSpec(memory_space=pltpu.VMEM)] * 2,
        out_shape=[out, out],
        compiler_params=pltpu.CompilerParams(vmem_limit_bytes=16 << 20),
    )(moments, *[vmem(x) for x in (centre, *fields)])


def swap(axis, first):
    count = lax.axis_size(axis)
    pairs = []
    for i in range(count):
        j = i + 1 if (i - first) % 2 == 0 else i - 1
        pairs.append((i, j if 0 <= j < count else i))
    return pairs


def exchange(grp, ea, eb, oa, ob):
    ra = lax.ppermute(ea, "slab", swap("slab", 0))
    rb = lax.ppermute(eb, "slab", swap("slab", 1))
    up = grp % 2 == 0

    def line(own, upper):
        take = [jnp.where(upper, r[:, BZ:], r[:, :BZ]) for r in (ra, rb)]
        return jnp.concatenate([take[0], own, take[1]], axis=1)

    gb = lax.ppermute(line(ob, jnp.logical_not(up)), "grp", swap("grp", 1))
    ga = lax.ppermute(line(oa, up), "grp", swap("grp", 0))
    return ra, rb, ga, gb


def on_device(samples, block_ids, tile_counts, occupied, coupling):
    slab, grp = lax.axis_index("slab"), lax.axis_index("grp")
    place = jnp.stack([slab, grp, lax.axis_size("slab"), lax.axis_size("grp")]).astype(jnp.int32)
    payload = splat(samples, tile_counts, block_ids)
    recv = lax.all_to_all(payload.reshape(SENDERS, 1, ROWS * 128), AXES, split_axis=0, concat_axis=0, tiled=True)
    weights, rowabs, mask = prepare(coupling, occupied)
    v, diag, maskc, centre, *edges = assemble(place, recv.reshape(SENDERS * ROWS, 128), mask, rowabs)
    fields = [v]
    moments = None
    for order in range(3):
        v, moments, *edges = apply_stiffness(
            order, place, v, diag, mask, maskc, exchange(grp, *edges), weights, moments
        )
        fields.append(v)
    shared = lax.all_to_all(moments.reshape(SENDERS, 1, 128), AXES, split_axis=0, concat_axis=0, tiled=True)
    outs = finish(shared.reshape(SENDERS, 128), centre, fields)

    def settle(out):
        out = out.reshape(NODES, 2, 2, 2, 128)
        return jnp.transpose(out, (0, 1, 3, 2, 4)).reshape(NODES, 2, 2, BZ)

    return settle(outs[0]), settle(outs[1])


def solution(mesh):
    placed = (P(AXES, None, None), P(AXES), P(AXES), P("slab", "grp", None), P())
    return jax.shard_map(
        on_device,
        mesh=mesh,
        in_specs=placed,
        out_specs=(P(None, "slab", "grp", None), P(None, "slab", "grp", None)),
        check_vma=False,
    )
```

```python
import functools

import jax
import jax.numpy as jnp
from jax import lax
from jax.experimental import pallas as pl
from jax.experimental.pallas import tpu as pltpu
from jax.sharding import PartitionSpec as P

AXES = ("slab", "grp")
F32 = jnp.float32
BF16 = jnp.bfloat16
N_COLS = 4
BZ = 256
NODES = 64
SENDERS = 128
CAP = 8
ROWS = CAP + 1


def lane_iota(shape):
    return lax.broadcasted_iota(jnp.int32, shape, len(shape) - 1)


def row_iota(shape):
    return lax.broadcasted_iota(jnp.int32, shape, 0)


def basis_of(pos):
    u = 4.0 * pos
    cell = jnp.floor(u)
    w = u - cell
    rest = 1.0 - w
    low = 0.5 * (rest * rest)
    high = 0.5 * (w * w)
    off = w - 0.5
    mid = 0.75 - off * off
    slow = -4.0 * rest
    shigh = 4.0 * w
    smid = -8.0 * off
    at = [cell == float(i) for i in range(4)]
    zero = jnp.zeros_like(u)
    values, slopes = [], []
    for i in range(4):
        val, slo = zero, zero
        if i + 1 < 4:
            val = jnp.where(at[i + 1], low, val)
            slo = jnp.where(at[i + 1], slow, slo)
        if i - 1 >= 0:
            val = jnp.where(at[i - 1], high, val)
            slo = jnp.where(at[i - 1], shigh, slo)
        values.append(jnp.where(at[i], mid, val))
        slopes.append(jnp.where(at[i], smid, slo))
    return values, slopes


def splat_kernel(samp_ref, cnt_ref, ids_ref, out_ref, flip, basis, acc, stats):
    step = pl.program_id(0)
    last = pl.num_programs(0) - 1

    @pl.when(step == 0)
    def _():
        stats[...] = jnp.zeros_like(stats)

    for k in range(6):
        flip[k] = samp_ref[k].T
    counts = cnt_ref[pl.ds(step, 1), :]

    def evaluate(group, carry):
        rows = pl.ds(pl.multiple_of(group * 8, 8), 8)
        valid = (row_iota((8, 128)) + group * 8 < counts).astype(F32)
        n0 = flip[3, rows, :] * valid
        n1 = flip[4, rows, :] * valid
        n2 = flip[5, rows, :] * valid
        val, slo = basis_of(flip[0, rows, :])
        for i in range(4):
            basis[i, rows, :] = slo[i] * n0
            basis[4 + i, rows, :] = val[i] * n1
            basis[8 + i, rows, :] = val[i] * n2
            basis[12 + i, rows, :] = val[i] * valid
        for d in (1, 2):
            val, slo = basis_of(flip[d, rows, :])
            for i in range(4):
                basis[8 + 8 * d + i, rows, :] = val[i]
                basis[12 + 8 * d + i, rows, :] = slo[i]
        return carry

    lax.fori_loop(0, 16, evaluate, 0, unroll=2)

    for i in range(4):
        def add_group(group, sums, i=i):
            rows = pl.ds(group * 8, 8)
            a = basis[i, rows, :]
            b = basis[4 + i, rows, :]
            c = basis[8 + i, rows, :]
            d = basis[12 + i, rows, :]
            v2 = [basis[24 + l, rows, :] for l in range(4)]
            s2 = [basis[28 + l, rows, :] for l in range(4)]
            out = list(sums)
            for j in range(4):
                v1 = basis[16 + j, rows, :]
                s1 = basis[20 + j, rows, :]
                first = a * v1 + b * s1
                second = c * v1
                dens = d * v1
                for l in range(4):
                    at = j * 4 + l
                    out[at] = out[at] + (first * v2[l] + second * s2[l])
                    out[16 + at] = out[16 + at] + dens * v2[l]
            return tuple(out)

        zero = jnp.zeros((8, 128), F32)
        sums = (zero,) * 32
        for group in range(16):
            sums = add_group(group, sums)
        for at in range(16):
            acc[pl.ds((i * 16 + at) * 8, 8), :] = sums[at]
            acc[pl.ds((64 + i * 16 + at) * 8, 8), :] = sums[16 + at]

    total = acc[pl.ds(0, 128, stride=8), :]
    for s in range(1, 8):
        total = total + acc[pl.ds(s, 128, stride=8), :]
    square = total[:64] * total[:64]
    weighted = total[64:] * square
    part, wpart = square[:8], weighted[:8]
    for k in range(1, 8):
        part = part + square[8 * k : 8 * k + 8]
        wpart = wpart + weighted[8 * k : 8 * k + 8]
    stats[0] = stats[0] + part
    stats[1] = stats[1] + wpart
    by_tile = total.T
    for d in range(16):
        out_ref[step, pl.ds(ROWS * d, 8), :] = by_tile[8 * d : 8 * d + 8]

    @pl.when(step == last)
    def _():
        ids = ids_ref[...]
        local = ((ids >> 14) & 1) * 512 + ((ids >> 8) & 1) * 256 + (ids & 255)
        local = local.astype(F32)
        sum0 = jnp.sum(stats[0], keepdims=True)
        sum1 = jnp.sum(stats[1], keepdims=True)
        lanes = lane_iota((1, 128))
        both = jnp.where(lanes % 2 == 0, sum0, sum1)
        for g in range(8):
            for d in range(16):
                row = jnp.where(lanes // 8 == d, local[g : g + 1], both)
                out_ref[g, pl.ds(ROWS * d + CAP, 1), :] = row


def splat(samples, counts, ids):
    tiles = samples.shape[0]
    groups = tiles // 128
    return pl.pallas_call(
        splat_kernel,
        name="splat",
        grid=(groups,),
        in_specs=[
            pl.BlockSpec((6, 128, 128), lambda g: (0, g, 0)),
            pl.BlockSpec((groups, 128), lambda g: (0, 0)),
            pl.BlockSpec((groups, 128), lambda g: (0, 0)),
        ],
        out_specs=pl.BlockSpec((groups, 16 * ROWS, 128), lambda g: (0, 0, 0)),
        out_shape=jax.ShapeDtypeStruct((groups, 16 * ROWS, 128), F32),
        scratch_shapes=[
            pltpu.VMEM((6, 128, 128), F32),
            pltpu.VMEM((32, 128, 128), F32),
            pltpu.VMEM((1024, 128), F32),
            pltpu.VMEM((2, 8, 128), F32),
        ],
    )(jnp.transpose(samples, (1, 0, 2)), counts.reshape(groups, 128), ids.reshape(groups, 128))


def vmem(x):
    return pltpu.with_memory_space_constraint(x, pltpu.VMEM)


def parity_weights(place_ref):
    slab, grp = place_ref[0], place_ref[1]
    slabs, grps = place_ref[2], place_ref[3]

    def pick(cond):
        return jnp.where(cond, 1.0, 0.0).astype(F32)

    def sides(at, count):
        odd = at % 2 == 1
        low = (pick(odd), pick(jnp.logical_and(jnp.logical_not(odd), at > 0)))
        high = (pick(jnp.logical_not(odd)), pick(jnp.logical_and(odd, at < count - 1)))
        return low, high

    return sides(slab, slabs), sides(grp, grps)


def blend(pair, a, b):
    return a * pair[0] + b * pair[1]


def column(x, y):
    return pl.ds((x * 2 + y) * BZ, BZ)


def store_edges(place_ref, masked, ea_ref, eb_ref, oa_ref, ob_ref):
    up_slab = place_ref[0] % 2 == 0
    up_grp = place_ref[1] % 2 == 0
    for k in range(2):
        at = pl.ds(k * BZ, BZ)
        ea_ref[:, at] = jnp.where(up_slab, masked[1][k], masked[0][k])
        eb_ref[:, at] = jnp.where(up_slab, masked[0][k], masked[1][k])
        oa_ref[:, at] = jnp.where(up_grp, masked[k][1], masked[k][0])
        ob_ref[:, at] = jnp.where(up_grp, masked[k][0], masked[k][1])


def prepare_kernel(coupling_ref, occ_ref, w_ref, rowabs_ref, mask_ref):
    total = jnp.zeros((NODES, NODES), F32)
    for dx in range(3):
        for dz in range(3):
            parts = []
            for dy in range(3):
                k = (dx * 3 + dy) * 3 + dz
                coupled = 0.5 * (coupling_ref[k] + coupling_ref[26 - k].T)
                total = total + jnp.abs(coupled)
                parts.append(coupled)
            wide = jnp.concatenate(parts, axis=1)
            high = wide.astype(BF16)
            w_ref[dx, pl.ds(dz * NODES, NODES), :] = high
            w_ref[dx, pl.ds((3 + dz) * NODES, NODES), :] = (wide - high.astype(F32)).astype(BF16)
    rowabs_ref[...] = jnp.broadcast_to(jnp.sum(total, axis=1, keepdims=True), (NODES, 128))
    for x in range(2):
        for y in range(2):
            mask_ref[:, column(x, y)] = jnp.broadcast_to(occ_ref[x, y : y + 1, :].astype(F32), (8, BZ))


def prepare(coupling, occupied):
    return pl.pallas_call(
        prepare_kernel,
        name="prepare",
        in_specs=[pl.BlockSpec(memory_space=pltpu.VMEM)] * 2,
        out_specs=[pl.BlockSpec(memory_space=pltpu.VMEM)] * 3,
        out_shape=[
            pltpu.VMEM((3, 6 * NODES, 3 * NODES), BF16),
            pltpu.VMEM((NODES, 128), F32),
            pltpu.VMEM((8, N_COLS * BZ), F32),
        ],
        compiler_params=pltpu.CompilerParams(vmem_limit_bytes=8 << 20),
        cost_estimate=pl.CostEstimate(flops=10**7, transcendentals=0, bytes_accessed=4 * 10**6),
    )(coupling, occupied)


def assemble_kernel(place_ref, recv_ref, mask_ref, rowabs_ref, v_ref, diag_ref, maskc_ref, c_ref,
                    ea_ref, eb_ref, oa_ref, ob_ref, turned):
    seat = place_ref[1] % 16
    turned[...] = recv_ref[pl.ds(CAP, SENDERS, stride=ROWS), :].T
    where = turned[pl.ds(pl.multiple_of(seat * 8, 8), 8), :].astype(jnp.int32)
    other = lax.rem(seat + 1, 16)
    sums = turned[pl.ds(pl.multiple_of(other * 8, 8), 8), :]
    sum0 = jnp.sum(sums[0:1, :], keepdims=True)
    sum1 = jnp.sum(sums[1:2, :], keepdims=True)
    rowabs = rowabs_ref[...]
    mean = jnp.sum(rowabs[:, 0:1], keepdims=True) * (1.0 / NODES)
    centre = mean + 0.5 + 4.0 * (sum1 / sum0)
    inverse = 1.0 / centre
    c_ref[...] = jnp.broadcast_to(centre, (8, 128))
    tiles = []
    for c in range(CAP):
        block = recv_ref[pl.ds(c, SENDERS, stride=ROWS), :]
        high = block.astype(BF16)
        low = (block - high.astype(F32)).astype(BF16)
        tiles.append(jnp.concatenate([high, low], axis=1))
    table = jnp.concatenate(tiles, axis=0)
    masked = []
    for x in range(2):
        masked.append([])
        for y in range(2):
            picks = []
            for c in range(CAP):
                hit = row_iota((BZ, SENDERS)) + (x * 2 + y) * BZ == where[c : c + 1, :]
                picks.append(hit.astype(F32).astype(BF16))
            pick = jnp.concatenate(picks, axis=1)
            both = jnp.dot(pick, table, preferred_element_type=F32)
            ordered = (both[:, :128] + both[:, 128:]).T
            rhs = ordered[:NODES]
            dens = ordered[NODES:]
            mask = mask_ref[0:1, column(x, y)]
            v_ref[:, column(x, y)] = rhs
            diag = rowabs[:, 0:1] + 0.5 + 4.0 * dens
            diag_ref[:, column(x, y)] = (diag - centre) * inverse
            maskc_ref[:, column(x, y)] = jnp.broadcast_to(mask * inverse, (8, BZ))
            masked[x].append(rhs * mask)
    store_edges(place_ref, masked, ea_ref, eb_ref, oa_ref, ob_ref)


FIELD = pltpu.VMEM((NODES, N_COLS * BZ), F32)
EDGE = pltpu.VMEM((NODES, 2 * BZ), F32)


def in_specs(count):
    return [pl.BlockSpec(memory_space=pltpu.SMEM)] + [pl.BlockSpec(memory_space=pltpu.VMEM)] * count


def assemble(place, recv, mask, rowabs):
    return pl.pallas_call(
        assemble_kernel,
        name="assemble",
        in_specs=in_specs(3),
        out_specs=[pl.BlockSpec(memory_space=pltpu.VMEM)] * 8,
        out_shape=[FIELD, FIELD, pltpu.VMEM((8, N_COLS * BZ), F32), pltpu.VMEM((8, 128), F32), EDGE, EDGE, EDGE, EDGE],
        scratch_shapes=[pltpu.VMEM((128, 128), F32)],
        compiler_params=pltpu.CompilerParams(vmem_limit_bytes=16 << 20),
    )(place, vmem(recv), vmem(mask), vmem(rowabs))


def spread(part):
    lanes = lane_iota((NODES, BZ))
    before = jnp.where(lanes == 0, 0.0, pltpu.roll(part[:NODES], 1, 1))
    after = jnp.where(lanes == BZ - 1, 0.0, pltpu.roll(part[2 * NODES :], BZ - 1, 1))
    return part[NODES : 2 * NODES] + before + after


def split(src):
    top = src.astype(BF16)
    return top, (src - top.astype(F32)).astype(BF16)


def sides_kernel(place_ref, v_ref, mask_ref, ra_ref, rb_ref, ya_ref, yb_ref, w_ref, o_ref, high, low):
    (x_low, x_high), (y_low, y_high) = parity_weights(place_ref)

    def put(px, py, src):
        rows = pl.ds((px * 4 + py) * NODES, NODES)
        high[rows, :], low[rows, :] = split(src)

    for x in range(2):
        for y in range(2):
            put(x + 1, y + 1, v_ref[:, column(x, y)] * mask_ref[0:1, column(x, y)])
    for k in range(2):
        at = pl.ds(k * BZ, BZ)
        put(0, k + 1, blend(x_low, ra_ref[:, at], rb_ref[:, at]))
        put(3, k + 1, blend(x_high, ra_ref[:, at], rb_ref[:, at]))
        put(k + 1, 0, blend(y_low, ya_ref[:, at], yb_ref[:, at]))
        put(k + 1, 3, blend(y_high, ya_ref[:, at], yb_ref[:, at]))
    nothing = jnp.zeros((NODES, BZ), BF16)
    for px in (0, 3):
        for py in (0, 3):
            rows = pl.ds((px * 4 + py) * NODES, NODES)
            high[rows, :] = nothing
            low[rows, :] = nothing
    for x in range(2):
        for y in range(2):
            full = jnp.zeros((6 * NODES, BZ), F32)
            half = jnp.zeros((3 * NODES, BZ), F32)
            for dx in range(3):
                rows = pl.ds(((x + dx) * 4 + y) * NODES, 3 * NODES)
                full = full + jnp.dot(w_ref[dx], high[rows, :], preferred_element_type=F32)
                half = half + jnp.dot(w_ref[dx, 0 : 3 * NODES, :], low[rows, :], preferred_element_type=F32)
            o_ref[:, column(x, y)] = spread(full[: 3 * NODES] + full[3 * NODES :] + half)


def sides(place, v, mask, ra, rb, ya, yb, weights):
    operands = (v, mask, ra, rb, ya, yb, weights)
    return pl.pallas_call(
        sides_kernel,
        name="sides",
        in_specs=in_specs(len(operands)),
        out_specs=pl.BlockSpec(memory_space=pltpu.VMEM),
        out_shape=FIELD,
        scratch_shapes=[pltpu.VMEM((16 * NODES, BZ), BF16), pltpu.VMEM((16 * NODES, BZ), BF16)],
        compiler_params=pltpu.CompilerParams(vmem_limit_bytes=16 << 20),
        cost_estimate=pl.CostEstimate(flops=15 * 10**8, transcendentals=0, bytes_accessed=2 * 10**6),
    )(place, *[vmem(x) for x in operands])


def corners_kernel(order, place_ref, sum_ref, v_ref, diag_ref, mask_ref, maskc_ref, ca_ref, cb_ref, w_ref, *rest):
    rest = list(rest)
    mom_ref = rest.pop(0) if order else None
    o_ref, mom_out = rest[:2]
    edges = rest[2:]
    x_pairs, y_pairs = parity_weights(place_ref)
    sq = jnp.zeros((NODES, BZ), F32)
    cross = jnp.zeros((NODES, BZ), F32)
    masked = [[], []]
    for y in range(2):
        line = [blend(y_pairs[y], ca_ref[:, pl.ds(k * BZ, BZ)], cb_ref[:, pl.ds(k * BZ, BZ)]) for k in range(2)]
        for x in range(2):
            high, low = split(blend(x_pairs[x], line[0], line[1]))
            cols = pl.ds(2 * y * NODES, NODES)
            full = jnp.dot(w_ref[2 * x, :, cols], high, preferred_element_type=F32)
            half = jnp.dot(w_ref[2 * x, 0 : 3 * NODES, cols], low, preferred_element_type=F32)
            at = column(x, y)
            total = sum_ref[:, at] + spread(full[: 3 * NODES] + full[3 * NODES :] + half)
            v = v_ref[:, at]
            new = diag_ref[:, at] * v - maskc_ref[0:1, at] * total
            o_ref[:, at] = new
            masked[x].append(new * mask_ref[0:1, at])
            sq = sq + v * v
            cross = cross + v * new
    if edges:
        store_edges(place_ref, masked, *edges)
    sq = jnp.sum(sq, keepdims=True)
    cross = jnp.sum(cross, keepdims=True)
    spot = lane_iota((1, 128))
    before = mom_ref[0:1, :] if order else jnp.zeros((1, 128), F32)
    mom = jnp.where(spot == 2 * order, sq, jnp.where(spot == 2 * order + 1, cross, before))
    mom_out[...] = jnp.broadcast_to(mom, mom_out.shape)


def apply_stiffness(order, place, v, diag, mask, maskc, edges, weights, moments):
    ra, rb, ya, yb, ca, cb = exchange(place[1], *edges)
    part = sides(place, v, mask, ra, rb, ya, yb, weights)
    more = [] if moments is None else [moments]
    last = order == 2
    moment = jax.ShapeDtypeStruct((SENDERS, 128), F32) if last else pltpu.VMEM((8, 128), F32)
    shapes = [FIELD, moment] + ([] if last else [EDGE] * 4)
    operands = [part, v, diag, mask, maskc, ca, cb, weights] + more
    return pl.pallas_call(
        functools.partial(corners_kernel, order),
        name="corners",
        in_specs=in_specs(len(operands)),
        out_specs=[pl.BlockSpec(memory_space=pltpu.VMEM)] * len(shapes),
        out_shape=shapes,
        compiler_params=pltpu.CompilerParams(vmem_limit_bytes=16 << 20),
    )(place, *[vmem(x) for x in operands])


def finish_kernel(mom_ref, c_ref, v0_ref, v1_ref, v2_ref, v3_ref, x_ref, r_ref):
    row = jnp.sum(mom_ref[...], axis=0, keepdims=True)
    lanes = lane_iota((1, 128))
    m = [jnp.sum(jnp.where(lanes == k, row, 0.0), keepdims=True) for k in range(6)]
    zero = jnp.zeros((1, 1), F32)
    one = jnp.ones((1, 1), F32)

    def inner(f, g):
        total = zero
        for i, a in enumerate(f):
            for j, b in enumerate(g):
                if a is not None and b is not None:
                    total = total + a * b * m[i + j]
        return total

    r = [one, None, None, None]
    p = [one, None, None, None]
    x = [None, None, None]
    norm = m[0]

    def plus(a, b):
        if a is None:
            return b
        return a if b is None else a + b

    for step in range(3):
        image = [plus(p[k], p[k - 1] if k else None) for k in range(4)]
        alpha = norm / inner(p, image)
        for k in range(3):
            if p[k] is not None:
                x[k] = plus(x[k], alpha * p[k])
        for k in range(4):
            if image[k] is not None:
                r[k] = plus(r[k], -(alpha * image[k]))
        if step < 2:
            new = inner(r, r)
            beta = new / norm
            p = [plus(r[k], None if p[k] is None else beta * p[k]) for k in range(4)]
            norm = new
    inverse = 1.0 / c_ref[0:1, 0:1]
    x = [value * inverse for value in x]
    for chunk in range(8):
        bx, by, zt = chunk // 4, chunk // 2 % 2, chunk % 2
        spot = bx * 4 + zt * 2 + by
        at = pl.ds(chunk * 128, 128)
        v0, v1, v2, v3 = v0_ref[:, at], v1_ref[:, at], v2_ref[:, at], v3_ref[:, at]
        x_ref[:, spot, :] = x[0] * v0 + x[1] * v1 + x[2] * v2
        r_ref[:, spot, :] = r[0] * v0 + r[1] * v1 + r[2] * v2 + r[3] * v3


def finish(moments, centre, fields):
    out = jax.ShapeDtypeStruct((NODES, 8, 128), F32)
    return pl.pallas_call(
        finish_kernel,
        name="finish",
        in_specs=[pl.BlockSpec(memory_space=pltpu.VMEM)] * 6,
        out_specs=[pl.BlockSpec(memory_space=pltpu.VMEM)] * 2,
        out_shape=[out, out],
        compiler_params=pltpu.CompilerParams(vmem_limit_bytes=16 << 20),
    )(moments, *[vmem(x) for x in (centre, *fields)])


def swap(axis, first):
    count = lax.axis_size(axis)
    pairs = []
    for i in range(count):
        j = i + 1 if (i - first) % 2 == 0 else i - 1
        pairs.append((i, j if 0 <= j < count else i))
    return pairs


def exchange(grp, ea, eb, oa, ob):
    yb = lax.ppermute(ob, "grp", swap("grp", 1))
    ra = lax.ppermute(ea, "slab", swap("slab", 0))
    rb = lax.ppermute(eb, "slab", swap("slab", 1))
    ya = lax.ppermute(oa, "grp", swap("grp", 0))
    up = grp % 2 == 0

    def line(upper):
        return jnp.concatenate([jnp.where(upper, r[:, BZ:], r[:, :BZ]) for r in (ra, rb)], axis=1)

    cb = lax.ppermute(line(jnp.logical_not(up)), "grp", swap("grp", 1))
    ca = lax.ppermute(line(up), "grp", swap("grp", 0))
    return ra, rb, ya, yb, ca, cb


def on_device(samples, block_ids, tile_counts, occupied, coupling):
    slab, grp = lax.axis_index("slab"), lax.axis_index("grp")
    place = jnp.stack([slab, grp, lax.axis_size("slab"), lax.axis_size("grp")]).astype(jnp.int32)
    payload = splat(samples, tile_counts, block_ids)
    recv = lax.all_to_all(payload.reshape(SENDERS, 1, ROWS * 128), AXES, split_axis=0, concat_axis=0, tiled=True)
    weights, rowabs, mask = prepare(coupling, occupied)
    v, diag, maskc, centre, *edges = assemble(place, recv.reshape(SENDERS * ROWS, 128), mask, rowabs)
    fields = [v]
    moments = None
    for order in range(3):
        v, moments, *edges = apply_stiffness(
            order, place, v, diag, mask, maskc, edges, weights, moments
        )
        fields.append(v)
    shared = lax.all_to_all(moments.reshape(SENDERS, 1, 128), AXES, split_axis=0, concat_axis=0, tiled=True)
    outs = finish(shared.reshape(SENDERS, 128), centre, fields)

    def settle(out):
        out = out.reshape(NODES, 2, 2, 2, 128)
        return jnp.transpose(out, (0, 1, 3, 2, 4)).reshape(NODES, 2, 2, BZ)

    return settle(outs[0]), settle(outs[1])


def solution(mesh):
    placed = (P(AXES, None, None), P(AXES), P(AXES), P("slab", "grp", None), P())
    return jax.shard_map(
        on_device,
        mesh=mesh,
        in_specs=placed,
        out_specs=(P(None, "slab", "grp", None), P(None, "slab", "grp", None)),
        check_vma=False,
    )
```

```python
import functools

import jax
import jax.numpy as jnp
from jax import lax
from jax.experimental import pallas as pl
from jax.experimental.pallas import tpu as pltpu
from jax.sharding import PartitionSpec as P

AXES = ("slab", "grp")
F32 = jnp.float32
BF16 = jnp.bfloat16
N_COLS = 4
BZ = 256
NODES = 64
SENDERS = 128
CAP = 8
ROWS = CAP + 1


def lane_iota(shape):
    return lax.broadcasted_iota(jnp.int32, shape, len(shape) - 1)


def row_iota(shape):
    return lax.broadcasted_iota(jnp.int32, shape, 0)


def basis_of(pos):
    u = 4.0 * pos
    w = u - jnp.floor(u)
    back = w - 1.0
    low = back * back
    high = w * w
    turn = w * back
    mid = 1.0 - (turn + turn)
    smid = -(w + back)
    in0, in1, in2 = u < 1.0, u < 2.0, u < 3.0
    zero = jnp.zeros_like(u)

    def nodes(below, at, above):
        return [
            jnp.where(in0, at, jnp.where(in1, below, zero)),
            jnp.where(in0, above, jnp.where(in1, at, jnp.where(in2, below, zero))),
            jnp.where(in0, zero, jnp.where(in1, above, jnp.where(in2, at, below))),
            jnp.where(in1, zero, jnp.where(in2, above, at)),
        ]

    return nodes(low, mid, high), nodes(back, smid, w)


def splat_kernel(samp_ref, cnt_ref, ids_ref, out_ref, held, sems, flip, basis, acc, stats):
    groups = out_ref.shape[0]

    def fetch(g):
        return pltpu.make_async_copy(samp_ref.at[:, pl.ds(g * 128, 128), :], held.at[g], sems.at[g])

    def turn(g):
        for k in range(6):
            flip[k] = held[g, k].T

    def evaluate(g):
        counts = cnt_ref[pl.ds(g, 1), :]
        for group in range(16):
            rows = pl.ds(group * 8, 8)
            live = row_iota((8, 128)) + group * 8 < counts
            n0 = jnp.where(live, flip[3, rows, :], 0.0)
            n1 = jnp.where(live, flip[4, rows, :], 0.0)
            n2 = jnp.where(live, flip[5, rows, :], 0.0)
            eighth = jnp.where(live, 0.125, 0.0)
            val, slo = basis_of(flip[0, rows, :])
            for i in range(4):
                basis[i, rows, :] = slo[i] * n0
                basis[4 + i, rows, :] = val[i] * n1
                basis[8 + i, rows, :] = val[i] * n2
                basis[12 + i, rows, :] = val[i] * eighth
            for d in (1, 2):
                val, slo = basis_of(flip[d, rows, :])
                for i in range(4):
                    basis[8 + 8 * d + i, rows, :] = val[i]
                    basis[12 + 8 * d + i, rows, :] = slo[i]

    def accumulate(i, js):
        rhs_sums, dens_sums = {}, {}
        for group in range(16):
            rows = pl.ds(group * 8, 8)
            a = basis[i, rows, :]
            b = basis[4 + i, rows, :]
            c = basis[8 + i, rows, :]
            d = basis[12 + i, rows, :]
            v2 = [basis[24 + l, rows, :] for l in range(4)]
            s2 = [basis[28 + l, rows, :] for l in range(4)]
            for j in js:
                v1 = basis[16 + j, rows, :]
                s1 = basis[20 + j, rows, :]
                first = a * v1 + b * s1
                second = c * v1
                dens = d * v1
                for l in range(4):
                    at = j * 4 + l
                    rhs = first * v2[l] + second * s2[l]
                    den = dens * v2[l]
                    rhs_sums[at] = rhs if group == 0 else rhs_sums[at] + rhs
                    dens_sums[at] = den if group == 0 else dens_sums[at] + den
        for at in rhs_sums:
            acc[pl.ds((i * 16 + at) * 8, 8), :] = rhs_sums[at]
            acc[pl.ds((64 + i * 16 + at) * 8, 8), :] = dens_sums[at]

    def settle(g, real):
        total = acc[pl.ds(0, 128, stride=8), :]
        for s in range(1, 8):
            total = total + acc[pl.ds(s, 128, stride=8), :]
        square = total[:64] * total[:64]
        weighted = total[64:] * square
        part, wpart = square[:8], weighted[:8]
        for k in range(1, 8):
            part = part + square[8 * k : 8 * k + 8]
            wpart = wpart + weighted[8 * k : 8 * k + 8]
        stats[0] = stats[0] + jnp.where(real, part, 0.0)
        stats[1] = stats[1] + jnp.where(real, wpart, 0.0)
        by_tile = total.T
        for d in range(16):
            out_ref[g, pl.ds(ROWS * d, 8), :] = by_tile[8 * d : 8 * d + 8]

    for g in range(groups):
        fetch(g).start()
    stats[...] = jnp.zeros_like(stats)
    acc[...] = jnp.zeros_like(acc)
    fetch(0).wait()
    turn(0)

    def advance(g, carry):
        following = jnp.minimum(g + 1, groups - 1)

        @pl.when(g + 1 < groups)
        def _():
            fetch(following).wait()

        settle(jnp.maximum(g - 1, 0), g > 0)
        evaluate(g)
        turn(following)
        for i in range(4):
            for js in ((0, 1), (2, 3)):
                accumulate(i, js)
        return carry

    lax.fori_loop(0, groups, advance, 0)
    settle(groups - 1, True)
    ids = ids_ref[...]
    local = ((ids >> 14) & 1) * 512 + ((ids >> 8) & 1) * 256 + (ids & 255)
    local = local.astype(F32)
    sum0 = jnp.sum(stats[0], keepdims=True)
    sum1 = jnp.sum(stats[1], keepdims=True)
    lanes = lane_iota((1, 128))
    both = jnp.where(lanes % 2 == 0, sum0, sum1)
    for g in range(groups):
        for d in range(16):
            row = jnp.where(lanes // 8 == d, local[g : g + 1], both)
            out_ref[g, pl.ds(ROWS * d + CAP, 1), :] = row


def splat(samples, counts, ids):
    tiles = samples.shape[0]
    groups = tiles // 128
    return pl.pallas_call(
        splat_kernel,
        name="splat",
        in_specs=[pl.BlockSpec(memory_space=pltpu.HBM)] + [pl.BlockSpec(memory_space=pltpu.VMEM)] * 2,
        out_specs=pl.BlockSpec(memory_space=pltpu.VMEM),
        out_shape=pltpu.VMEM((groups, 16 * ROWS, 128), F32),
        scratch_shapes=[
            pltpu.VMEM((groups, 6, 128, 128), F32),
            pltpu.SemaphoreType.DMA((groups,)),
            pltpu.VMEM((6, 128, 128), F32),
            pltpu.VMEM((32, 128, 128), F32),
            pltpu.VMEM((1024, 128), F32),
            pltpu.VMEM((2, 8, 128), F32),
        ],
        compiler_params=pltpu.CompilerParams(vmem_limit_bytes=24 << 20),
    )(pltpu.with_memory_space_constraint(jnp.transpose(samples, (1, 0, 2)), pltpu.HBM), counts.reshape(groups, 128), ids.reshape(groups, 128))


def vmem(x):
    return pltpu.with_memory_space_constraint(x, pltpu.VMEM)


def parity_weights(place_ref):
    slab, grp = place_ref[0], place_ref[1]
    slabs, grps = place_ref[2], place_ref[3]

    def pick(cond):
        return jnp.where(cond, 1.0, 0.0).astype(F32)

    def sides(at, count):
        odd = at % 2 == 1
        low = (pick(odd), pick(jnp.logical_and(jnp.logical_not(odd), at > 0)))
        high = (pick(jnp.logical_not(odd)), pick(jnp.logical_and(odd, at < count - 1)))
        return low, high

    return sides(slab, slabs), sides(grp, grps)


def blend(pair, a, b):
    return a * pair[0] + b * pair[1]


def column(x, y):
    return pl.ds((x * 2 + y) * BZ, BZ)


def store_edges(place_ref, masked, ea_ref, eb_ref, oa_ref, ob_ref):
    up_slab = place_ref[0] % 2 == 0
    up_grp = place_ref[1] % 2 == 0
    for k in range(2):
        at = pl.ds(k * BZ, BZ)
        ea_ref[:, at] = jnp.where(up_slab, masked[1][k], masked[0][k])
        eb_ref[:, at] = jnp.where(up_slab, masked[0][k], masked[1][k])
        oa_ref[:, at] = jnp.where(up_grp, masked[k][1], masked[k][0])
        ob_ref[:, at] = jnp.where(up_grp, masked[k][0], masked[k][1])


def prepare_kernel(coupling_ref, occ_ref, w_ref, rowabs_ref, mask_ref):
    total = jnp.zeros((NODES, NODES), F32)
    for dx in range(3):
        for dz in range(3):
            parts = []
            for dy in range(3):
                k = (dx * 3 + dy) * 3 + dz
                coupled = 0.5 * (coupling_ref[k] + coupling_ref[26 - k].T)
                total = total + jnp.abs(coupled)
                parts.append(coupled)
            wide = jnp.concatenate(parts, axis=1)
            high = wide.astype(BF16)
            w_ref[dx, pl.ds(dz * NODES, NODES), :] = high
            w_ref[dx, pl.ds((3 + dz) * NODES, NODES), :] = (wide - high.astype(F32)).astype(BF16)
    rowabs_ref[...] = jnp.broadcast_to(jnp.sum(total, axis=1, keepdims=True), (NODES, 128))
    for x in range(2):
        for y in range(2):
            mask_ref[:, column(x, y)] = jnp.broadcast_to(occ_ref[x, y : y + 1, :].astype(F32), (8, BZ))


def prepare(coupling, occupied):
    return pl.pallas_call(
        prepare_kernel,
        name="prepare",
        in_specs=[pl.BlockSpec(memory_space=pltpu.VMEM)] * 2,
        out_specs=[pl.BlockSpec(memory_space=pltpu.VMEM)] * 3,
        out_shape=[
            pltpu.VMEM((3, 6 * NODES, 3 * NODES), BF16),
            pltpu.VMEM((NODES, 128), F32),
            pltpu.VMEM((8, N_COLS * BZ), F32),
        ],
        compiler_params=pltpu.CompilerParams(vmem_limit_bytes=8 << 20),
        cost_estimate=pl.CostEstimate(flops=10**7, transcendentals=0, bytes_accessed=4 * 10**6),
    )(coupling, occupied)


def assemble_kernel(place_ref, recv_ref, mask_ref, rowabs_ref, v_ref, diag_ref, maskc_ref, c_ref,
                    ea_ref, eb_ref, oa_ref, ob_ref, turned):
    seat = place_ref[1] % 16
    turned[...] = recv_ref[pl.ds(CAP, SENDERS, stride=ROWS), :].T
    where = turned[pl.ds(pl.multiple_of(seat * 8, 8), 8), :].astype(jnp.int32)
    other = lax.rem(seat + 1, 16)
    sums = turned[pl.ds(pl.multiple_of(other * 8, 8), 8), :]
    sum0 = jnp.sum(sums[0:1, :], keepdims=True)
    sum1 = jnp.sum(sums[1:2, :], keepdims=True)
    rowabs = rowabs_ref[...]
    mean = jnp.sum(rowabs[:, 0:1], keepdims=True) * (1.0 / NODES)
    centre = mean + 0.5 + 4.0 * (sum1 / sum0)
    inverse = 1.0 / centre
    c_ref[...] = jnp.broadcast_to(centre, (8, 128))
    tiles = []
    for c in range(CAP):
        block = recv_ref[pl.ds(c, SENDERS, stride=ROWS), :]
        high = block.astype(BF16)
        low = (block - high.astype(F32)).astype(BF16)
        tiles.append(jnp.concatenate([high, low], axis=1))
    table = jnp.concatenate(tiles, axis=0)
    masked = []
    for x in range(2):
        masked.append([])
        for y in range(2):
            picks = []
            for c in range(CAP):
                hit = row_iota((BZ, SENDERS)) + (x * 2 + y) * BZ == where[c : c + 1, :]
                picks.append(hit.astype(F32).astype(BF16))
            pick = jnp.concatenate(picks, axis=1)
            both = jnp.dot(pick, table, preferred_element_type=F32)
            ordered = (both[:, :128] + both[:, 128:]).T
            rhs = ordered[:NODES]
            dens = ordered[NODES:]
            mask = mask_ref[0:1, column(x, y)]
            v_ref[:, column(x, y)] = rhs
            diag = rowabs[:, 0:1] + 0.5 + 4.0 * dens
            diag_ref[:, column(x, y)] = (diag - centre) * inverse
            maskc_ref[:, column(x, y)] = jnp.broadcast_to(mask * inverse, (8, BZ))
            masked[x].append(rhs * mask)
    store_edges(place_ref, masked, ea_ref, eb_ref, oa_ref, ob_ref)


FIELD = pltpu.VMEM((NODES, N_COLS * BZ), F32)
EDGE = pltpu.VMEM((NODES, 2 * BZ), F32)


def in_specs(count):
    return [pl.BlockSpec(memory_space=pltpu.SMEM)] + [pl.BlockSpec(memory_space=pltpu.VMEM)] * count


def assemble(place, recv, mask, rowabs):
    return pl.pallas_call(
        assemble_kernel,
        name="assemble",
        in_specs=in_specs(3),
        out_specs=[pl.BlockSpec(memory_space=pltpu.VMEM)] * 8,
        out_shape=[FIELD, FIELD, pltpu.VMEM((8, N_COLS * BZ), F32), pltpu.VMEM((8, 128), F32), EDGE, EDGE, EDGE, EDGE],
        scratch_shapes=[pltpu.VMEM((128, 128), F32)],
        compiler_params=pltpu.CompilerParams(vmem_limit_bytes=16 << 20),
    )(place, vmem(recv), vmem(mask), vmem(rowabs))


def spread(part):
    lanes = lane_iota((NODES, BZ))
    before = jnp.where(lanes == 0, 0.0, pltpu.roll(part[:NODES], 1, 1))
    after = jnp.where(lanes == BZ - 1, 0.0, pltpu.roll(part[2 * NODES :], BZ - 1, 1))
    return part[NODES : 2 * NODES] + before + after


def split(src):
    top = src.astype(BF16)
    return top, (src - top.astype(F32)).astype(BF16)


def sides_kernel(place_ref, v_ref, mask_ref, ra_ref, rb_ref, ya_ref, yb_ref, w_ref, o_ref, high, low):
    (x_low, x_high), (y_low, y_high) = parity_weights(place_ref)

    def put(px, py, src):
        rows = pl.ds((px * 4 + py) * NODES, NODES)
        high[rows, :], low[rows, :] = split(src)

    for x in range(2):
        for y in range(2):
            put(x + 1, y + 1, v_ref[:, column(x, y)] * mask_ref[0:1, column(x, y)])
    for k in range(2):
        at = pl.ds(k * BZ, BZ)
        put(0, k + 1, blend(x_low, ra_ref[:, at], rb_ref[:, at]))
        put(3, k + 1, blend(x_high, ra_ref[:, at], rb_ref[:, at]))
        put(k + 1, 0, blend(y_low, ya_ref[:, at], yb_ref[:, at]))
        put(k + 1, 3, blend(y_high, ya_ref[:, at], yb_ref[:, at]))
    nothing = jnp.zeros((NODES, BZ), BF16)
    for px in (0, 3):
        for py in (0, 3):
            rows = pl.ds((px * 4 + py) * NODES, NODES)
            high[rows, :] = nothing
            low[rows, :] = nothing
    for x in range(2):
        for y in range(2):
            full = jnp.zeros((6 * NODES, BZ), F32)
            half = jnp.zeros((3 * NODES, BZ), F32)
            for dx in range(3):
                rows = pl.ds(((x + dx) * 4 + y) * NODES, 3 * NODES)
                full = full + jnp.dot(w_ref[dx], high[rows, :], preferred_element_type=F32)
                half = half + jnp.dot(w_ref[dx, 0 : 3 * NODES, :], low[rows, :], preferred_element_type=F32)
            o_ref[:, column(x, y)] = spread(full[: 3 * NODES] + full[3 * NODES :] + half)


def sides(place, v, mask, ra, rb, ya, yb, weights):
    operands = (v, mask, ra, rb, ya, yb, weights)
    return pl.pallas_call(
        sides_kernel,
        name="sides",
        in_specs=in_specs(len(operands)),
        out_specs=pl.BlockSpec(memory_space=pltpu.VMEM),
        out_shape=FIELD,
        scratch_shapes=[pltpu.VMEM((16 * NODES, BZ), BF16), pltpu.VMEM((16 * NODES, BZ), BF16)],
        compiler_params=pltpu.CompilerParams(vmem_limit_bytes=16 << 20),
        cost_estimate=pl.CostEstimate(flops=15 * 10**8, transcendentals=0, bytes_accessed=2 * 10**6),
    )(place, *[vmem(x) for x in operands])


def corners_kernel(order, place_ref, sum_ref, v_ref, diag_ref, mask_ref, maskc_ref, ca_ref, cb_ref, w_ref, *rest):
    rest = list(rest)
    mom_ref = rest.pop(0) if order else None
    o_ref, mom_out = rest[:2]
    edges = rest[2:]
    x_pairs, y_pairs = parity_weights(place_ref)
    sq = jnp.zeros((NODES, BZ), F32)
    cross = jnp.zeros((NODES, BZ), F32)
    masked = [[], []]
    for y in range(2):
        line = [blend(y_pairs[y], ca_ref[:, pl.ds(k * BZ, BZ)], cb_ref[:, pl.ds(k * BZ, BZ)]) for k in range(2)]
        for x in range(2):
            high, low = split(blend(x_pairs[x], line[0], line[1]))
            cols = pl.ds(2 * y * NODES, NODES)
            full = jnp.dot(w_ref[2 * x, :, cols], high, preferred_element_type=F32)
            half = jnp.dot(w_ref[2 * x, 0 : 3 * NODES, cols], low, preferred_element_type=F32)
            at = column(x, y)
            total = sum_ref[:, at] + spread(full[: 3 * NODES] + full[3 * NODES :] + half)
            v = v_ref[:, at]
            new = diag_ref[:, at] * v - maskc_ref[0:1, at] * total
            o_ref[:, at] = new
            masked[x].append(new * mask_ref[0:1, at])
            sq = sq + v * v
            cross = cross + v * new
    if edges:
        store_edges(place_ref, masked, *edges)
    sq = jnp.sum(sq, keepdims=True)
    cross = jnp.sum(cross, keepdims=True)
    spot = lane_iota((1, 128))
    before = mom_ref[0:1, :] if order else jnp.zeros((1, 128), F32)
    mom = jnp.where(spot == 2 * order, sq, jnp.where(spot == 2 * order + 1, cross, before))
    mom_out[...] = jnp.broadcast_to(mom, mom_out.shape)


def apply_stiffness(order, place, v, diag, mask, maskc, edges, weights, moments):
    ra, rb, ya, yb, ca, cb = exchange(place[1], *edges)
    part = sides(place, v, mask, ra, rb, ya, yb, weights)
    more = [] if moments is None else [moments]
    last = order == 2
    moment = jax.ShapeDtypeStruct((SENDERS, 128), F32) if last else pltpu.VMEM((8, 128), F32)
    shapes = [FIELD, moment] + ([] if last else [EDGE] * 4)
    operands = [part, v, diag, mask, maskc, ca, cb, weights] + more
    return pl.pallas_call(
        functools.partial(corners_kernel, order),
        name="corners",
        in_specs=in_specs(len(operands)),
        out_specs=[pl.BlockSpec(memory_space=pltpu.VMEM)] * len(shapes),
        out_shape=shapes,
        compiler_params=pltpu.CompilerParams(vmem_limit_bytes=16 << 20),
    )(place, *[vmem(x) for x in operands])


def finish_kernel(mom_ref, c_ref, v0_ref, v1_ref, v2_ref, v3_ref, x_ref, r_ref):
    row = jnp.sum(mom_ref[...], axis=0, keepdims=True)
    lanes = lane_iota((1, 128))
    m = [jnp.sum(jnp.where(lanes == k, row, 0.0), keepdims=True) for k in range(6)]
    zero = jnp.zeros((1, 1), F32)
    one = jnp.ones((1, 1), F32)

    def inner(f, g):
        total = zero
        for i, a in enumerate(f):
            for j, b in enumerate(g):
                if a is not None and b is not None:
                    total = total + a * b * m[i + j]
        return total

    r = [one, None, None, None]
    p = [one, None, None, None]
    x = [None, None, None]
    norm = m[0]

    def plus(a, b):
        if a is None:
            return b
        return a if b is None else a + b

    for step in range(3):
        image = [plus(p[k], p[k - 1] if k else None) for k in range(4)]
        alpha = norm / inner(p, image)
        for k in range(3):
            if p[k] is not None:
                x[k] = plus(x[k], alpha * p[k])
        for k in range(4):
            if image[k] is not None:
                r[k] = plus(r[k], -(alpha * image[k]))
        if step < 2:
            new = inner(r, r)
            beta = new / norm
            p = [plus(r[k], None if p[k] is None else beta * p[k]) for k in range(4)]
            norm = new
    inverse = 1.0 / c_ref[0:1, 0:1]
    x = [value * inverse for value in x]
    for chunk in range(8):
        bx, by, zt = chunk // 4, chunk // 2 % 2, chunk % 2
        spot = bx * 4 + zt * 2 + by
        at = pl.ds(chunk * 128, 128)
        v0, v1, v2, v3 = v0_ref[:, at], v1_ref[:, at], v2_ref[:, at], v3_ref[:, at]
        x_ref[:, spot, :] = x[0] * v0 + x[1] * v1 + x[2] * v2
        r_ref[:, spot, :] = r[0] * v0 + r[1] * v1 + r[2] * v2 + r[3] * v3


def finish(moments, centre, fields):
    out = jax.ShapeDtypeStruct((NODES, 8, 128), F32)
    return pl.pallas_call(
        finish_kernel,
        name="finish",
        in_specs=[pl.BlockSpec(memory_space=pltpu.VMEM)] * 6,
        out_specs=[pl.BlockSpec(memory_space=pltpu.VMEM)] * 2,
        out_shape=[out, out],
        compiler_params=pltpu.CompilerParams(vmem_limit_bytes=16 << 20),
    )(moments, *[vmem(x) for x in (centre, *fields)])


def swap(axis, first):
    count = lax.axis_size(axis)
    pairs = []
    for i in range(count):
        j = i + 1 if (i - first) % 2 == 0 else i - 1
        pairs.append((i, j if 0 <= j < count else i))
    return pairs


def exchange(grp, ea, eb, oa, ob):
    yb = lax.ppermute(ob, "grp", swap("grp", 1))
    ra = lax.ppermute(ea, "slab", swap("slab", 0))
    rb = lax.ppermute(eb, "slab", swap("slab", 1))
    ya = lax.ppermute(oa, "grp", swap("grp", 0))
    up = grp % 2 == 0

    def line(upper):
        return jnp.concatenate([jnp.where(upper, r[:, BZ:], r[:, :BZ]) for r in (ra, rb)], axis=1)

    cb = lax.ppermute(line(jnp.logical_not(up)), "grp", swap("grp", 1))
    ca = lax.ppermute(line(up), "grp", swap("grp", 0))
    return ra, rb, ya, yb, ca, cb


def on_device(samples, block_ids, tile_counts, occupied, coupling):
    slab, grp = lax.axis_index("slab"), lax.axis_index("grp")
    place = jnp.stack([slab, grp, lax.axis_size("slab"), lax.axis_size("grp")]).astype(jnp.int32)
    payload = splat(samples, tile_counts, block_ids)
    recv = lax.all_to_all(payload.reshape(SENDERS, 1, ROWS * 128), AXES, split_axis=0, concat_axis=0, tiled=True)
    weights, rowabs, mask = prepare(coupling, occupied)
    v, diag, maskc, centre, *edges = assemble(place, recv.reshape(SENDERS * ROWS, 128), mask, rowabs)
    fields = [v]
    moments = None
    for order in range(3):
        v, moments, *edges = apply_stiffness(
            order, place, v, diag, mask, maskc, edges, weights, moments
        )
        fields.append(v)
    shared = lax.all_to_all(moments.reshape(SENDERS, 1, 128), AXES, split_axis=0, concat_axis=0, tiled=True)
    outs = finish(shared.reshape(SENDERS, 128), centre, fields)

    def settle(out):
        out = out.reshape(NODES, 2, 2, 2, 128)
        return jnp.transpose(out, (0, 1, 3, 2, 4)).reshape(NODES, 2, 2, BZ)

    return settle(outs[0]), settle(outs[1])


def solution(mesh):
    placed = (P(AXES, None, None), P(AXES), P(AXES), P("slab", "grp", None), P())
    return jax.shard_map(
        on_device,
        mesh=mesh,
        in_specs=placed,
        out_specs=(P(None, "slab", "grp", None), P(None, "slab", "grp", None)),
        check_vma=False,
    )
```

```python
import functools

import jax
import jax.numpy as jnp
from jax import lax
from jax.experimental import pallas as pl
from jax.experimental.pallas import tpu as pltpu
from jax.sharding import PartitionSpec as P

AXES = ("slab", "grp")
F32 = jnp.float32
BF16 = jnp.bfloat16
N_COLS = 4
BZ = 256
NODES = 64
SENDERS = 128
CAP = 8
ROWS = CAP + 1


def lane_iota(shape):
    return lax.broadcasted_iota(jnp.int32, shape, len(shape) - 1)


def row_iota(shape):
    return lax.broadcasted_iota(jnp.int32, shape, 0)


def basis_of(pos):
    u = 4.0 * pos
    w = u - jnp.floor(u)
    back = w - 1.0
    low = back * back
    high = w * w
    turn = w * back
    mid = 1.0 - (turn + turn)
    smid = -(w + back)
    in0, in1, in2 = u < 1.0, u < 2.0, u < 3.0
    zero = jnp.zeros_like(u)

    def nodes(below, at, above):
        return [
            jnp.where(in0, at, jnp.where(in1, below, zero)),
            jnp.where(in0, above, jnp.where(in1, at, jnp.where(in2, below, zero))),
            jnp.where(in0, zero, jnp.where(in1, above, jnp.where(in2, at, below))),
            jnp.where(in1, zero, jnp.where(in2, above, at)),
        ]

    return nodes(low, mid, high), nodes(back, smid, w)


def splat_kernel(samp_ref, cnt_ref, ids_ref, out_ref, held, sems, flip, basis, acc, stats):
    groups = out_ref.shape[0]

    def fetch(g):
        return pltpu.make_async_copy(samp_ref.at[:, pl.ds(g * 128, 128), :], held.at[g], sems.at[g])

    def turn(g):
        for k in range(6):
            flip[k] = held[g, k].T

    def evaluate(g):
        counts = cnt_ref[pl.ds(g, 1), :]
        for group in range(16):
            rows = pl.ds(group * 8, 8)
            live = row_iota((8, 128)) + group * 8 < counts
            n0 = jnp.where(live, flip[3, rows, :], 0.0)
            n1 = jnp.where(live, flip[4, rows, :], 0.0)
            n2 = jnp.where(live, flip[5, rows, :], 0.0)
            eighth = jnp.where(live, 0.125, 0.0)
            val, slo = basis_of(flip[0, rows, :])
            for i in range(4):
                basis[i, rows, :] = slo[i] * n0
                basis[4 + i, rows, :] = val[i] * n1
                basis[8 + i, rows, :] = val[i] * n2
                basis[12 + i, rows, :] = val[i] * eighth
            for d in (1, 2):
                val, slo = basis_of(flip[d, rows, :])
                for i in range(4):
                    basis[8 + 8 * d + i, rows, :] = val[i]
                    basis[12 + 8 * d + i, rows, :] = slo[i]

    def accumulate(i, js):
        rhs_sums, dens_sums = {}, {}
        for group in range(16):
            rows = pl.ds(group * 8, 8)
            a = basis[i, rows, :]
            b = basis[4 + i, rows, :]
            c = basis[8 + i, rows, :]
            d = basis[12 + i, rows, :]
            v2 = [basis[24 + l, rows, :] for l in range(4)]
            s2 = [basis[28 + l, rows, :] for l in range(4)]
            for j in js:
                v1 = basis[16 + j, rows, :]
                s1 = basis[20 + j, rows, :]
                first = a * v1 + b * s1
                second = c * v1
                dens = d * v1
                for l in range(4):
                    at = j * 4 + l
                    rhs = first * v2[l] + second * s2[l]
                    den = dens * v2[l]
                    rhs_sums[at] = rhs if group == 0 else rhs_sums[at] + rhs
                    dens_sums[at] = den if group == 0 else dens_sums[at] + den
        for at in rhs_sums:
            acc[pl.ds((i * 16 + at) * 8, 8), :] = rhs_sums[at]
            acc[pl.ds((64 + i * 16 + at) * 8, 8), :] = dens_sums[at]

    def settle(g, real):
        total = acc[pl.ds(0, 128, stride=8), :]
        for s in range(1, 8):
            total = total + acc[pl.ds(s, 128, stride=8), :]
        square = total[:64] * total[:64]
        weighted = total[64:] * square
        part, wpart = square[:8], weighted[:8]
        for k in range(1, 8):
            part = part + square[8 * k : 8 * k + 8]
            wpart = wpart + weighted[8 * k : 8 * k + 8]
        stats[0] = stats[0] + jnp.where(real, part, 0.0)
        stats[1] = stats[1] + jnp.where(real, wpart, 0.0)
        by_tile = total.T
        for d in range(16):
            out_ref[g, pl.ds(ROWS * d, 8), :] = by_tile[8 * d : 8 * d + 8]

    for g in range(groups):
        fetch(g).start()
    stats[...] = jnp.zeros_like(stats)
    acc[...] = jnp.zeros_like(acc)
    fetch(0).wait()
    turn(0)

    def advance(g, carry):
        following = jnp.minimum(g + 1, groups - 1)

        @pl.when(g + 1 < groups)
        def _():
            fetch(following).wait()

        settle(jnp.maximum(g - 1, 0), g > 0)
        evaluate(g)
        turn(following)
        for i in range(4):
            for js in ((0, 1), (2, 3)):
                accumulate(i, js)
        return carry

    lax.fori_loop(0, groups, advance, 0)
    settle(groups - 1, True)
    ids = ids_ref[...]
    local = ((ids >> 14) & 1) * 512 + ((ids >> 8) & 1) * 256 + (ids & 255)
    local = local.astype(F32)
    sum0 = jnp.sum(stats[0], keepdims=True)
    sum1 = jnp.sum(stats[1], keepdims=True)
    lanes = lane_iota((1, 128))
    both = jnp.where(lanes % 2 == 0, sum0, sum1)
    for g in range(groups):
        for d in range(16):
            row = jnp.where(lanes // 8 == d, local[g : g + 1], both)
            out_ref[g, pl.ds(ROWS * d + CAP, 1), :] = row


def splat(samples, counts, ids):
    tiles = samples.shape[0]
    groups = tiles // 128
    return pl.pallas_call(
        splat_kernel,
        name="splat",
        in_specs=[pl.BlockSpec(memory_space=pltpu.HBM)] + [pl.BlockSpec(memory_space=pltpu.VMEM)] * 2,
        out_specs=pl.BlockSpec(memory_space=pltpu.VMEM),
        out_shape=pltpu.VMEM((groups, 16 * ROWS, 128), F32),
        scratch_shapes=[
            pltpu.VMEM((groups, 6, 128, 128), F32),
            pltpu.SemaphoreType.DMA((groups,)),
            pltpu.VMEM((6, 128, 128), F32),
            pltpu.VMEM((32, 128, 128), F32),
            pltpu.VMEM((1024, 128), F32),
            pltpu.VMEM((2, 8, 128), F32),
        ],
        compiler_params=pltpu.CompilerParams(vmem_limit_bytes=24 << 20),
    )(pltpu.with_memory_space_constraint(jnp.transpose(samples, (1, 0, 2)), pltpu.HBM), counts.reshape(groups, 128), ids.reshape(groups, 128))


def vmem(x):
    return pltpu.with_memory_space_constraint(x, pltpu.VMEM)


def parity_weights(place_ref):
    slab, grp = place_ref[0], place_ref[1]
    slabs, grps = place_ref[2], place_ref[3]

    def pick(cond):
        return jnp.where(cond, 1.0, 0.0).astype(F32)

    def sides(at, count):
        odd = at % 2 == 1
        low = (pick(odd), pick(jnp.logical_and(jnp.logical_not(odd), at > 0)))
        high = (pick(jnp.logical_not(odd)), pick(jnp.logical_and(odd, at < count - 1)))
        return low, high

    return sides(slab, slabs), sides(grp, grps)


def blend(pair, a, b):
    return a * pair[0] + b * pair[1]


def column(x, y):
    return pl.ds((x * 2 + y) * BZ, BZ)


def store_edges(place_ref, masked, ea_ref, eb_ref, oa_ref, ob_ref):
    up_slab = place_ref[0] % 2 == 0
    up_grp = place_ref[1] % 2 == 0
    for k in range(2):
        at = pl.ds(k * BZ, BZ)
        ea_ref[:, at] = jnp.where(up_slab, masked[1][k], masked[0][k])
        eb_ref[:, at] = jnp.where(up_slab, masked[0][k], masked[1][k])
        oa_ref[:, at] = jnp.where(up_grp, masked[k][1], masked[k][0])
        ob_ref[:, at] = jnp.where(up_grp, masked[k][0], masked[k][1])


def prepare_kernel(coupling_ref, occ_ref, w_ref, rowabs_ref, mask_ref):
    total = jnp.zeros((NODES, NODES), F32)
    for dx in range(3):
        for dz in range(3):
            parts = []
            for dy in range(3):
                k = (dx * 3 + dy) * 3 + dz
                coupled = 0.5 * (coupling_ref[k] + coupling_ref[26 - k].T)
                total = total + jnp.abs(coupled)
                parts.append(coupled)
            wide = jnp.concatenate(parts, axis=1)
            high = wide.astype(BF16)
            w_ref[dx, pl.ds(dz * NODES, NODES), :] = high
            w_ref[dx, pl.ds((3 + dz) * NODES, NODES), :] = (wide - high.astype(F32)).astype(BF16)
    rowabs_ref[...] = jnp.broadcast_to(jnp.sum(total, axis=1, keepdims=True), (NODES, 128))
    for x in range(2):
        for y in range(2):
            mask_ref[:, column(x, y)] = jnp.broadcast_to(occ_ref[x, y : y + 1, :].astype(F32), (8, BZ))


def prepare(coupling, occupied):
    return pl.pallas_call(
        prepare_kernel,
        name="prepare",
        in_specs=[pl.BlockSpec(memory_space=pltpu.VMEM)] * 2,
        out_specs=[pl.BlockSpec(memory_space=pltpu.VMEM)] * 3,
        out_shape=[
            pltpu.VMEM((3, 6 * NODES, 3 * NODES), BF16),
            pltpu.VMEM((NODES, 128), F32),
            pltpu.VMEM((8, N_COLS * BZ), F32),
        ],
        compiler_params=pltpu.CompilerParams(vmem_limit_bytes=8 << 20),
        cost_estimate=pl.CostEstimate(flops=10**7, transcendentals=0, bytes_accessed=4 * 10**6),
    )(coupling, occupied)


def assemble_kernel(place_ref, recv_ref, mask_ref, rowabs_ref, v_ref, diag_ref, maskc_ref, c_ref,
                    ea_ref, eb_ref, oa_ref, ob_ref, turned):
    seat = place_ref[1] % 16
    turned[...] = recv_ref[pl.ds(CAP, SENDERS, stride=ROWS), :].T
    where = turned[pl.ds(pl.multiple_of(seat * 8, 8), 8), :].astype(jnp.int32)
    other = lax.rem(seat + 1, 16)
    sums = turned[pl.ds(pl.multiple_of(other * 8, 8), 8), :]
    sum0 = jnp.sum(sums[0:1, :], keepdims=True)
    sum1 = jnp.sum(sums[1:2, :], keepdims=True)
    rowabs = rowabs_ref[...]
    mean = jnp.sum(rowabs[:, 0:1], keepdims=True) * (1.0 / NODES)
    centre = mean + 0.5 + 4.0 * (sum1 / sum0)
    inverse = 1.0 / centre
    c_ref[...] = jnp.broadcast_to(centre, (8, 128))
    tiles = []
    for c in range(CAP):
        block = recv_ref[pl.ds(c, SENDERS, stride=ROWS), :]
        high = block.astype(BF16)
        low = (block - high.astype(F32)).astype(BF16)
        tiles.append(jnp.concatenate([high, low], axis=1))
    table = jnp.concatenate(tiles, axis=0)
    masked = []
    for x in range(2):
        masked.append([])
        for y in range(2):
            picks = []
            for c in range(CAP):
                hit = row_iota((BZ, SENDERS)) + (x * 2 + y) * BZ == where[c : c + 1, :]
                picks.append(hit.astype(F32).astype(BF16))
            pick = jnp.concatenate(picks, axis=1)
            both = jnp.dot(pick, table, preferred_element_type=F32)
            ordered = (both[:, :128] + both[:, 128:]).T
            rhs = ordered[:NODES]
            dens = ordered[NODES:]
            mask = mask_ref[0:1, column(x, y)]
            v_ref[:, column(x, y)] = rhs
            diag = rowabs[:, 0:1] + 0.5 + 4.0 * dens
            diag_ref[:, column(x, y)] = (diag - centre) * inverse
            maskc_ref[:, column(x, y)] = jnp.broadcast_to(mask * inverse, (8, BZ))
            masked[x].append(rhs * mask)
    store_edges(place_ref, masked, ea_ref, eb_ref, oa_ref, ob_ref)


FIELD = pltpu.VMEM((NODES, N_COLS * BZ), F32)
EDGE = pltpu.VMEM((NODES, 2 * BZ), F32)


def in_specs(count):
    return [pl.BlockSpec(memory_space=pltpu.SMEM)] + [pl.BlockSpec(memory_space=pltpu.VMEM)] * count


def assemble(place, recv, mask, rowabs):
    return pl.pallas_call(
        assemble_kernel,
        name="assemble",
        in_specs=in_specs(3),
        out_specs=[pl.BlockSpec(memory_space=pltpu.VMEM)] * 8,
        out_shape=[FIELD, FIELD, pltpu.VMEM((8, N_COLS * BZ), F32), pltpu.VMEM((8, 128), F32), EDGE, EDGE, EDGE, EDGE],
        scratch_shapes=[pltpu.VMEM((128, 128), F32)],
        compiler_params=pltpu.CompilerParams(vmem_limit_bytes=16 << 20),
    )(place, vmem(recv), vmem(mask), vmem(rowabs))


def spread(part):
    lanes = lane_iota((NODES, BZ))
    before = jnp.where(lanes == 0, 0.0, pltpu.roll(part[:NODES], 1, 1))
    after = jnp.where(lanes == BZ - 1, 0.0, pltpu.roll(part[2 * NODES :], BZ - 1, 1))
    return part[NODES : 2 * NODES] + before + after


def split(src):
    top = src.astype(BF16)
    return top, (src - top.astype(F32)).astype(BF16)


def product(w_ref, dx, cols, high, low):
    full = jnp.dot(w_ref[dx, :, cols], high, preferred_element_type=F32)
    half = jnp.dot(w_ref[dx, 0 : 3 * NODES, cols], low, preferred_element_type=F32)
    return spread(full[: 3 * NODES] + full[3 * NODES :] + half)


def put_moments(order, mom_ref, mom_out, sq, cross):
    sq = jnp.sum(sq, keepdims=True)
    cross = jnp.sum(cross, keepdims=True)
    spot = lane_iota((1, 128))
    before = jnp.zeros((1, 128), F32) if mom_ref is None else mom_ref[0:1, :]
    mom = jnp.where(spot == 2 * order, sq, jnp.where(spot == 2 * order + 1, cross, before))
    mom_out[...] = jnp.broadcast_to(mom, mom_out.shape)


def sides_kernel(last, place_ref, v_ref, mask_ref, ra_ref, rb_ref, ya_ref, yb_ref, w_ref, *rest):
    if last:
        diag_ref, maskc_ref, c_ref, mom_ref, o_ref, mom_out, high, low = rest
    else:
        o_ref, high, low = rest
    (x_low, x_high), (y_low, y_high) = parity_weights(place_ref)
    halo = {}

    def at_rows(px, py):
        return pl.ds((px * 4 + py) * NODES, NODES)

    def put(px, py, src):
        high[at_rows(px, py), :], low[at_rows(px, py), :] = split(src)

    for x in range(2):
        for y in range(2):
            put(x + 1, y + 1, v_ref[:, column(x, y)] * mask_ref[0:1, column(x, y)])
    for k in range(2):
        at = pl.ds(k * BZ, BZ)
        halo[k] = (blend(x_low, ra_ref[:, at], rb_ref[:, at]), blend(x_high, ra_ref[:, at], rb_ref[:, at]))
        put(0, k + 1, halo[k][0])
        put(3, k + 1, halo[k][1])
        put(k + 1, 0, blend(y_low, ya_ref[:, at], yb_ref[:, at]))
        put(k + 1, 3, blend(y_high, ya_ref[:, at], yb_ref[:, at]))
    nothing = jnp.zeros((NODES, BZ), BF16)
    for px in (0, 3):
        for py in (0, 3):
            high[at_rows(px, py), :] = nothing
            low[at_rows(px, py), :] = nothing
    sq = jnp.zeros((NODES, BZ), F32)
    cross = jnp.zeros((NODES, BZ), F32)
    for x in range(2):
        for y in range(2):
            full = jnp.zeros((6 * NODES, BZ), F32)
            half = jnp.zeros((3 * NODES, BZ), F32)
            for dx in range(3):
                rows = pl.ds(((x + dx) * 4 + y) * NODES, 3 * NODES)
                full = full + jnp.dot(w_ref[dx], high[rows, :], preferred_element_type=F32)
                half = half + jnp.dot(w_ref[dx, 0 : 3 * NODES, :], low[rows, :], preferred_element_type=F32)
            at = column(x, y)
            total = spread(full[: 3 * NODES] + full[3 * NODES :] + half)
            o_ref[:, at] = total
            if last:
                v = v_ref[:, at]
                sq = sq + v * v
                cross = cross + v * (diag_ref[:, at] * v - maskc_ref[0:1, at] * total)
    if not last:
        return
    energy = jnp.zeros((NODES, BZ), F32)
    for x in range(2):
        for y in range(2):
            near = at_rows(x + 1, 3 * y)
            cols = pl.ds(2 * y * NODES, NODES)
            energy = energy + halo[y][x] * product(w_ref, 2 - 2 * x, cols, high[near, :], low[near, :])
    cross = cross - energy * (1.0 / c_ref[0:1, 0:1])
    put_moments(2, mom_ref, mom_out, sq, cross)


def sides(place, operands, last):
    shapes = [FIELD] + ([pltpu.VMEM((SENDERS, 128), F32)] if last else [])
    return pl.pallas_call(
        functools.partial(sides_kernel, last),
        name="sides",
        in_specs=in_specs(len(operands)),
        out_specs=[pl.BlockSpec(memory_space=pltpu.VMEM)] * len(shapes),
        out_shape=shapes,
        scratch_shapes=[pltpu.VMEM((16 * NODES, BZ), BF16), pltpu.VMEM((16 * NODES, BZ), BF16)],
        compiler_params=pltpu.CompilerParams(vmem_limit_bytes=16 << 20),
        cost_estimate=pl.CostEstimate(flops=15 * 10**8, transcendentals=0, bytes_accessed=2 * 10**6),
    )(place, *[vmem(x) for x in operands])


def corners_kernel(order, last, place_ref, sum_ref, v_ref, diag_ref, mask_ref, maskc_ref, ca_ref, cb_ref, w_ref, *rest):
    rest = list(rest)
    mom_ref = rest.pop(0) if order and not last else None
    o_ref = rest.pop(0)
    x_pairs, y_pairs = parity_weights(place_ref)
    sq = jnp.zeros((NODES, BZ), F32)
    cross = jnp.zeros((NODES, BZ), F32)
    masked = [[], []]
    for y in range(2):
        line = [blend(y_pairs[y], ca_ref[:, pl.ds(k * BZ, BZ)], cb_ref[:, pl.ds(k * BZ, BZ)]) for k in range(2)]
        for x in range(2):
            high, low = split(blend(x_pairs[x], line[0], line[1]))
            at = column(x, y)
            total = sum_ref[:, at] + product(w_ref, 2 * x, pl.ds(2 * y * NODES, NODES), high, low)
            v = v_ref[:, at]
            new = diag_ref[:, at] * v - maskc_ref[0:1, at] * total
            o_ref[:, at] = new
            if not last:
                masked[x].append(new * mask_ref[0:1, at])
                sq = sq + v * v
                cross = cross + v * new
    if not last:
        store_edges(place_ref, masked, *rest[1:])
        put_moments(order, mom_ref, rest[0], sq, cross)


def corners(order, place, operands, last):
    shapes = [FIELD] + ([] if last else [pltpu.VMEM((8, 128), F32)] + [EDGE] * 4)
    return pl.pallas_call(
        functools.partial(corners_kernel, order, last),
        name="corners",
        in_specs=in_specs(len(operands)),
        out_specs=[pl.BlockSpec(memory_space=pltpu.VMEM)] * len(shapes),
        out_shape=shapes,
        compiler_params=pltpu.CompilerParams(vmem_limit_bytes=16 << 20),
        cost_estimate=pl.CostEstimate(flops=5 * 10**8, transcendentals=0, bytes_accessed=2 * 10**6),
    )(place, *[vmem(x) for x in operands])


def apply_stiffness(order, place, v, diag, mask, maskc, centre, edges, weights, moments):
    last = order == 2
    ra, rb, ya, yb, ca, cb = exchange(place[1], *edges)
    operands = [v, mask, ra, rb, ya, yb, weights] + ([diag, maskc, centre, moments] if last else [])
    part, *shared = sides(place, operands, last)
    operands = [part, v, diag, mask, maskc, ca, cb, weights]
    if last:
        return corners(order, place, operands, last)[0], shared[0], []
    new, moments, *edges = corners(order, place, operands + ([] if moments is None else [moments]), last)
    return new, moments, edges


def finish_kernel(mom_ref, c_ref, v0_ref, v1_ref, v2_ref, v3_ref, x_ref, r_ref):
    row = jnp.sum(mom_ref[...], axis=0, keepdims=True)
    lanes = lane_iota((1, 128))
    m = [jnp.sum(jnp.where(lanes == k, row, 0.0), keepdims=True) for k in range(6)]
    zero = jnp.zeros((1, 1), F32)
    one = jnp.ones((1, 1), F32)

    def inner(f, g):
        total = zero
        for i, a in enumerate(f):
            for j, b in enumerate(g):
                if a is not None and b is not None:
                    total = total + a * b * m[i + j]
        return total

    r = [one, None, None, None]
    p = [one, None, None, None]
    x = [None, None, None]
    norm = m[0]

    def plus(a, b):
        if a is None:
            return b
        return a if b is None else a + b

    for step in range(3):
        image = [plus(p[k], p[k - 1] if k else None) for k in range(4)]
        alpha = norm / inner(p, image)
        for k in range(3):
            if p[k] is not None:
                x[k] = plus(x[k], alpha * p[k])
        for k in range(4):
            if image[k] is not None:
                r[k] = plus(r[k], -(alpha * image[k]))
        if step < 2:
            new = inner(r, r)
            beta = new / norm
            p = [plus(r[k], None if p[k] is None else beta * p[k]) for k in range(4)]
            norm = new
    inverse = 1.0 / c_ref[0:1, 0:1]
    x = [value * inverse for value in x]
    for chunk in range(8):
        bx, by, zt = chunk // 4, chunk // 2 % 2, chunk % 2
        spot = bx * 4 + zt * 2 + by
        at = pl.ds(chunk * 128, 128)
        v0, v1, v2, v3 = v0_ref[:, at], v1_ref[:, at], v2_ref[:, at], v3_ref[:, at]
        x_ref[:, spot, :] = x[0] * v0 + x[1] * v1 + x[2] * v2
        r_ref[:, spot, :] = r[0] * v0 + r[1] * v1 + r[2] * v2 + r[3] * v3


def finish(moments, centre, fields):
    out = jax.ShapeDtypeStruct((NODES, 8, 128), F32)
    return pl.pallas_call(
        finish_kernel,
        name="finish",
        in_specs=[pl.BlockSpec(memory_space=pltpu.VMEM)] * 6,
        out_specs=[pl.BlockSpec(memory_space=pltpu.VMEM)] * 2,
        out_shape=[out, out],
        compiler_params=pltpu.CompilerParams(vmem_limit_bytes=16 << 20),
    )(moments, *[vmem(x) for x in (centre, *fields)])


def swap(axis, first):
    count = lax.axis_size(axis)
    pairs = []
    for i in range(count):
        j = i + 1 if (i - first) % 2 == 0 else i - 1
        pairs.append((i, j if 0 <= j < count else i))
    return pairs


def exchange(grp, ea, eb, oa, ob):
    yb = lax.ppermute(ob, "grp", swap("grp", 1))
    ra = lax.ppermute(ea, "slab", swap("slab", 0))
    rb = lax.ppermute(eb, "slab", swap("slab", 1))
    ya = lax.ppermute(oa, "grp", swap("grp", 0))
    up = grp % 2 == 0

    def line(upper):
        return jnp.concatenate([jnp.where(upper, r[:, BZ:], r[:, :BZ]) for r in (ra, rb)], axis=1)

    cb = lax.ppermute(line(jnp.logical_not(up)), "grp", swap("grp", 1))
    ca = lax.ppermute(line(up), "grp", swap("grp", 0))
    return ra, rb, ya, yb, ca, cb


def on_device(samples, block_ids, tile_counts, occupied, coupling):
    slab, grp = lax.axis_index("slab"), lax.axis_index("grp")
    place = jnp.stack([slab, grp, lax.axis_size("slab"), lax.axis_size("grp")]).astype(jnp.int32)
    payload = splat(samples, tile_counts, block_ids)
    recv = lax.all_to_all(payload.reshape(SENDERS, 1, ROWS * 128), AXES, split_axis=0, concat_axis=0, tiled=True)
    weights, rowabs, mask = prepare(coupling, occupied)
    v, diag, maskc, centre, *edges = assemble(place, recv.reshape(SENDERS * ROWS, 128), mask, rowabs)
    fields = [v]
    moments = None
    for order in range(3):
        v, moments, edges = apply_stiffness(
            order, place, v, diag, mask, maskc, centre, edges, weights, moments
        )
        fields.append(v)
    shared = lax.all_to_all(moments.reshape(SENDERS, 1, 128), AXES, split_axis=0, concat_axis=0, tiled=True)
    outs = finish(shared.reshape(SENDERS, 128), centre, fields)

    def settle(out):
        out = out.reshape(NODES, 2, 2, 2, 128)
        return jnp.transpose(out, (0, 1, 3, 2, 4)).reshape(NODES, 2, 2, BZ)

    return settle(outs[0]), settle(outs[1])


def solution(mesh):
    placed = (P(AXES, None, None), P(AXES), P(AXES), P("slab", "grp", None), P())
    return jax.shard_map(
        on_device,
        mesh=mesh,
        in_specs=placed,
        out_specs=(P(None, "slab", "grp", None), P(None, "slab", "grp", None)),
        check_vma=False,
    )
```

```python
import functools

import jax
import jax.numpy as jnp
from jax import lax
from jax.experimental import pallas as pl
from jax.experimental.pallas import tpu as pltpu
from jax.sharding import PartitionSpec as P

AXES = ("slab", "grp")
F32 = jnp.float32
BF16 = jnp.bfloat16
N_COLS = 4
BZ = 256
NODES = 64
SENDERS = 128
CAP = 8
ROWS = CAP + 1


def lane_iota(shape):
    return lax.broadcasted_iota(jnp.int32, shape, len(shape) - 1)


def row_iota(shape):
    return lax.broadcasted_iota(jnp.int32, shape, 0)


def basis_of(pos):
    u = 4.0 * pos
    w = u - jnp.floor(u)
    back = w - 1.0
    low = back * back
    high = w * w
    turn = w * back
    mid = 1.0 - (turn + turn)
    smid = -(w + back)
    in0, in1, in2 = u < 1.0, u < 2.0, u < 3.0
    zero = jnp.zeros_like(u)

    def nodes(below, at, above):
        return [
            jnp.where(in0, at, jnp.where(in1, below, zero)),
            jnp.where(in0, above, jnp.where(in1, at, jnp.where(in2, below, zero))),
            jnp.where(in0, zero, jnp.where(in1, above, jnp.where(in2, at, below))),
            jnp.where(in1, zero, jnp.where(in2, above, at)),
        ]

    return nodes(low, mid, high), nodes(back, smid, w)


def splat_kernel(samp_ref, cnt_ref, ids_ref, out_ref, held, sems, flip, basis, acc, stats):
    groups = out_ref.shape[0]

    def fetch(g):
        return pltpu.make_async_copy(samp_ref.at[:, pl.ds(g * 128, 128), :], held.at[g], sems.at[g])

    def turn(g):
        for k in range(6):
            flip[k] = held[g, k].T

    def evaluate(g):
        counts = cnt_ref[pl.ds(g, 1), :]
        for group in range(16):
            rows = pl.ds(group * 8, 8)
            live = row_iota((8, 128)) + group * 8 < counts
            n0 = jnp.where(live, flip[3, rows, :], 0.0)
            n1 = jnp.where(live, flip[4, rows, :], 0.0)
            n2 = jnp.where(live, flip[5, rows, :], 0.0)
            eighth = jnp.where(live, 0.125, 0.0)
            val, slo = basis_of(flip[0, rows, :])
            for i in range(4):
                basis[i, rows, :] = slo[i] * n0
                basis[4 + i, rows, :] = val[i] * n1
                basis[8 + i, rows, :] = val[i] * n2
                basis[12 + i, rows, :] = val[i] * eighth
            for d in (1, 2):
                val, slo = basis_of(flip[d, rows, :])
                for i in range(4):
                    basis[8 + 8 * d + i, rows, :] = val[i]
                    basis[12 + 8 * d + i, rows, :] = slo[i]

    def accumulate(i, js):
        rhs_sums, dens_sums = {}, {}
        for group in range(16):
            rows = pl.ds(group * 8, 8)
            a = basis[i, rows, :]
            b = basis[4 + i, rows, :]
            c = basis[8 + i, rows, :]
            d = basis[12 + i, rows, :]
            v2 = [basis[24 + l, rows, :] for l in range(4)]
            s2 = [basis[28 + l, rows, :] for l in range(4)]
            for j in js:
                v1 = basis[16 + j, rows, :]
                s1 = basis[20 + j, rows, :]
                first = a * v1 + b * s1
                second = c * v1
                dens = d * v1
                for l in range(4):
                    at = j * 4 + l
                    rhs = first * v2[l] + second * s2[l]
                    den = dens * v2[l]
                    rhs_sums[at] = rhs if group == 0 else rhs_sums[at] + rhs
                    dens_sums[at] = den if group == 0 else dens_sums[at] + den
        for at in rhs_sums:
            acc[pl.ds((i * 16 + at) * 8, 8), :] = rhs_sums[at]
            acc[pl.ds((64 + i * 16 + at) * 8, 8), :] = dens_sums[at]

    def settle(g, real):
        total = acc[pl.ds(0, 128, stride=8), :]
        for s in range(1, 8):
            total = total + acc[pl.ds(s, 128, stride=8), :]
        square = total[:64] * total[:64]
        weighted = total[64:] * square
        part, wpart = square[:8], weighted[:8]
        for k in range(1, 8):
            part = part + square[8 * k : 8 * k + 8]
            wpart = wpart + weighted[8 * k : 8 * k + 8]
        stats[0] = stats[0] + jnp.where(real, part, 0.0)
        stats[1] = stats[1] + jnp.where(real, wpart, 0.0)
        by_tile = total.T
        for d in range(16):
            out_ref[g, pl.ds(ROWS * d, 8), :] = by_tile[8 * d : 8 * d + 8]

    for g in range(groups):
        fetch(g).start()
    stats[...] = jnp.zeros_like(stats)
    acc[...] = jnp.zeros_like(acc)
    fetch(0).wait()
    turn(0)

    def advance(g, carry):
        following = jnp.minimum(g + 1, groups - 1)

        @pl.when(g + 1 < groups)
        def _():
            fetch(following).wait()

        settle(jnp.maximum(g - 1, 0), g > 0)
        evaluate(g)
        turn(following)
        for i in range(4):
            for js in ((0, 1), (2, 3)):
                accumulate(i, js)
        return carry

    lax.fori_loop(0, groups, advance, 0)
    settle(groups - 1, True)
    ids = ids_ref[...]
    local = ((ids >> 14) & 1) * 512 + ((ids >> 8) & 1) * 256 + (ids & 255)
    local = local.astype(F32)
    sum0 = jnp.sum(stats[0], keepdims=True)
    sum1 = jnp.sum(stats[1], keepdims=True)
    lanes = lane_iota((1, 128))
    both = jnp.where(lanes % 2 == 0, sum0, sum1)
    for g in range(groups):
        for d in range(16):
            row = jnp.where(lanes // 8 == d, local[g : g + 1], both)
            out_ref[g, pl.ds(ROWS * d + CAP, 1), :] = row


def splat(samples, counts, ids):
    tiles = samples.shape[0]
    groups = tiles // 128
    return pl.pallas_call(
        splat_kernel,
        name="splat",
        in_specs=[pl.BlockSpec(memory_space=pltpu.HBM)] + [pl.BlockSpec(memory_space=pltpu.VMEM)] * 2,
        out_specs=pl.BlockSpec(memory_space=pltpu.VMEM),
        out_shape=pltpu.VMEM((groups, 16 * ROWS, 128), F32),
        scratch_shapes=[
            pltpu.VMEM((groups, 6, 128, 128), F32),
            pltpu.SemaphoreType.DMA((groups,)),
            pltpu.VMEM((6, 128, 128), F32),
            pltpu.VMEM((32, 128, 128), F32),
            pltpu.VMEM((1024, 128), F32),
            pltpu.VMEM((2, 8, 128), F32),
        ],
        compiler_params=pltpu.CompilerParams(vmem_limit_bytes=24 << 20),
    )(pltpu.with_memory_space_constraint(jnp.transpose(samples, (1, 0, 2)), pltpu.HBM), counts.reshape(groups, 128), ids.reshape(groups, 128))


def vmem(x):
    return pltpu.with_memory_space_constraint(x, pltpu.VMEM)


def parity_weights(place_ref):
    slab, grp = place_ref[0], place_ref[1]
    slabs, grps = place_ref[2], place_ref[3]

    def pick(cond):
        return jnp.where(cond, 1.0, 0.0).astype(F32)

    def sides(at, count):
        odd = at % 2 == 1
        low = (pick(odd), pick(jnp.logical_and(jnp.logical_not(odd), at > 0)))
        high = (pick(jnp.logical_not(odd)), pick(jnp.logical_and(odd, at < count - 1)))
        return low, high

    return sides(slab, slabs), sides(grp, grps)


def blend(pair, a, b):
    return a * pair[0] + b * pair[1]


def column(x, y):
    return pl.ds((x * 2 + y) * BZ, BZ)


def store_edges(place_ref, masked, ea_ref, eb_ref, oa_ref, ob_ref):
    up_slab = place_ref[0] % 2 == 0
    up_grp = place_ref[1] % 2 == 0
    for k in range(2):
        at = pl.ds(k * BZ, BZ)
        ea_ref[:, at] = jnp.where(up_slab, masked[1][k], masked[0][k])
        eb_ref[:, at] = jnp.where(up_slab, masked[0][k], masked[1][k])
        oa_ref[:, at] = jnp.where(up_grp, masked[k][1], masked[k][0])
        ob_ref[:, at] = jnp.where(up_grp, masked[k][0], masked[k][1])


def prepare_kernel(coupling_ref, occ_ref, w_ref, rowabs_ref, mask_ref):
    total = jnp.zeros((NODES, NODES), F32)
    for dx in range(3):
        for dz in range(3):
            parts = []
            for dy in range(3):
                k = (dx * 3 + dy) * 3 + dz
                coupled = 0.5 * (coupling_ref[k] + coupling_ref[26 - k].T)
                total = total + jnp.abs(coupled)
                parts.append(coupled)
            wide = jnp.concatenate(parts, axis=1)
            high = wide.astype(BF16)
            w_ref[dx, pl.ds(dz * NODES, NODES), :] = high
            w_ref[dx, pl.ds((3 + dz) * NODES, NODES), :] = (wide - high.astype(F32)).astype(BF16)
    rowabs_ref[...] = jnp.broadcast_to(jnp.sum(total, axis=1, keepdims=True), (NODES, 128))
    for x in range(2):
        for y in range(2):
            mask_ref[:, column(x, y)] = jnp.broadcast_to(occ_ref[x, y : y + 1, :].astype(F32), (8, BZ))


def prepare(coupling, occupied):
    return pl.pallas_call(
        prepare_kernel,
        name="prepare",
        in_specs=[pl.BlockSpec(memory_space=pltpu.VMEM)] * 2,
        out_specs=[pl.BlockSpec(memory_space=pltpu.VMEM)] * 3,
        out_shape=[
            pltpu.VMEM((3, 6 * NODES, 3 * NODES), BF16),
            pltpu.VMEM((NODES, 128), F32),
            pltpu.VMEM((8, N_COLS * BZ), F32),
        ],
        compiler_params=pltpu.CompilerParams(vmem_limit_bytes=8 << 20),
        cost_estimate=pl.CostEstimate(flops=10**7, transcendentals=0, bytes_accessed=4 * 10**6),
    )(coupling, occupied)


def assemble_kernel(place_ref, recv_ref, mask_ref, rowabs_ref, v_ref, diag_ref, maskc_ref, c_ref,
                    ea_ref, eb_ref, oa_ref, ob_ref, turned):
    seat = place_ref[1] % 16
    turned[...] = recv_ref[pl.ds(CAP, SENDERS, stride=ROWS), :].T
    where = turned[pl.ds(pl.multiple_of(seat * 8, 8), 8), :].astype(jnp.int32)
    other = lax.rem(seat + 1, 16)
    sums = turned[pl.ds(pl.multiple_of(other * 8, 8), 8), :]
    sum0 = jnp.sum(sums[0:1, :], keepdims=True)
    sum1 = jnp.sum(sums[1:2, :], keepdims=True)
    rowabs = rowabs_ref[...]
    mean = jnp.sum(rowabs[:, 0:1], keepdims=True) * (1.0 / NODES)
    centre = mean + 0.5 + 4.0 * (sum1 / sum0)
    inverse = 1.0 / centre
    c_ref[...] = jnp.broadcast_to(centre, (8, 128))
    tiles = []
    for c in range(CAP):
        block = recv_ref[pl.ds(c, SENDERS, stride=ROWS), :]
        high = block.astype(BF16)
        low = (block - high.astype(F32)).astype(BF16)
        tiles.append(jnp.concatenate([high, low], axis=1))
    table = jnp.concatenate(tiles, axis=0)
    masked = []
    for x in range(2):
        masked.append([])
        for y in range(2):
            picks = []
            for c in range(CAP):
                hit = row_iota((BZ, SENDERS)) + (x * 2 + y) * BZ == where[c : c + 1, :]
                picks.append(hit.astype(F32).astype(BF16))
            pick = jnp.concatenate(picks, axis=1)
            both = jnp.dot(pick, table, preferred_element_type=F32)
            ordered = (both[:, :128] + both[:, 128:]).T
            rhs = ordered[:NODES]
            dens = ordered[NODES:]
            mask = mask_ref[0:1, column(x, y)]
            v_ref[:, column(x, y)] = rhs
            diag = rowabs[:, 0:1] + 0.5 + 4.0 * dens
            diag_ref[:, column(x, y)] = (diag - centre) * inverse
            maskc_ref[:, column(x, y)] = jnp.broadcast_to(mask * inverse, (8, BZ))
            masked[x].append(rhs * mask)
    store_edges(place_ref, masked, ea_ref, eb_ref, oa_ref, ob_ref)


FIELD = pltpu.VMEM((NODES, N_COLS * BZ), F32)
EDGE = pltpu.VMEM((NODES, 2 * BZ), F32)


def in_specs(count):
    return [pl.BlockSpec(memory_space=pltpu.SMEM)] + [pl.BlockSpec(memory_space=pltpu.VMEM)] * count


def assemble(place, recv, mask, rowabs):
    return pl.pallas_call(
        assemble_kernel,
        name="assemble",
        in_specs=in_specs(3),
        out_specs=[pl.BlockSpec(memory_space=pltpu.VMEM)] * 8,
        out_shape=[FIELD, FIELD, pltpu.VMEM((8, N_COLS * BZ), F32), pltpu.VMEM((8, 128), F32), EDGE, EDGE, EDGE, EDGE],
        scratch_shapes=[pltpu.VMEM((128, 128), F32)],
        compiler_params=pltpu.CompilerParams(vmem_limit_bytes=16 << 20),
    )(place, vmem(recv), vmem(mask), vmem(rowabs))


def spread(part):
    lanes = lane_iota((NODES, BZ))
    before = jnp.where(lanes == 0, 0.0, pltpu.roll(part[:NODES], 1, 1))
    after = jnp.where(lanes == BZ - 1, 0.0, pltpu.roll(part[2 * NODES :], BZ - 1, 1))
    return part[NODES : 2 * NODES] + before + after


def split(src):
    top = src.astype(BF16)
    return top, (src - top.astype(F32)).astype(BF16)


def product(w_ref, dx, cols, high, low):
    full = jnp.dot(w_ref[dx, :, cols], high, preferred_element_type=F32)
    half = jnp.dot(w_ref[dx, 0 : 3 * NODES, cols], low, preferred_element_type=F32)
    return spread(full[: 3 * NODES] + full[3 * NODES :] + half)


def put_moments(order, mom_ref, mom_out, sq, cross):
    sq = jnp.sum(sq, keepdims=True)
    cross = jnp.sum(cross, keepdims=True)
    spot = lane_iota((1, 128))
    before = jnp.zeros((1, 128), F32) if mom_ref is None else mom_ref[0:1, :]
    mom = jnp.where(spot == 2 * order, sq, jnp.where(spot == 2 * order + 1, cross, before))
    mom_out[...] = jnp.broadcast_to(mom, mom_out.shape)


def sides_kernel(last, place_ref, v_ref, mask_ref, ra_ref, rb_ref, ya_ref, yb_ref, w_ref, *rest):
    if last:
        diag_ref, maskc_ref, c_ref, mom_ref, o_ref, mom_out, high, low = rest
    else:
        o_ref, high, low = rest
    (x_low, x_high), (y_low, y_high) = parity_weights(place_ref)
    halo = {}

    def at_rows(px, py):
        return pl.ds((px * 4 + py) * NODES, NODES)

    def put(px, py, src):
        high[at_rows(px, py), :], low[at_rows(px, py), :] = split(src)

    for x in range(2):
        for y in range(2):
            put(x + 1, y + 1, v_ref[:, column(x, y)] * mask_ref[0:1, column(x, y)])
    for k in range(2):
        at = pl.ds(k * BZ, BZ)
        halo[k] = (blend(x_low, ra_ref[:, at], rb_ref[:, at]), blend(x_high, ra_ref[:, at], rb_ref[:, at]))
        put(0, k + 1, halo[k][0])
        put(3, k + 1, halo[k][1])
        put(k + 1, 0, blend(y_low, ya_ref[:, at], yb_ref[:, at]))
        put(k + 1, 3, blend(y_high, ya_ref[:, at], yb_ref[:, at]))
    nothing = jnp.zeros((NODES, BZ), BF16)
    for px in (0, 3):
        for py in (0, 3):
            high[at_rows(px, py), :] = nothing
            low[at_rows(px, py), :] = nothing
    sq = jnp.zeros((NODES, BZ), F32)
    cross = jnp.zeros((NODES, BZ), F32)
    for x in range(2):
        for y in range(2):
            full = jnp.zeros((6 * NODES, BZ), F32)
            half = jnp.zeros((3 * NODES, BZ), F32)
            for dx in range(3):
                rows = pl.ds(((x + dx) * 4 + y) * NODES, 3 * NODES)
                full = full + jnp.dot(w_ref[dx], high[rows, :], preferred_element_type=F32)
                half = half + jnp.dot(w_ref[dx, 0 : 3 * NODES, :], low[rows, :], preferred_element_type=F32)
            at = column(x, y)
            total = spread(full[: 3 * NODES] + full[3 * NODES :] + half)
            o_ref[:, at] = total
            if last:
                v = v_ref[:, at]
                sq = sq + v * v
                cross = cross + v * (diag_ref[:, at] * v - maskc_ref[0:1, at] * total)
    if not last:
        return
    energy = jnp.zeros((NODES, BZ), F32)
    for x in range(2):
        for y in range(2):
            near = at_rows(x + 1, 3 * y)
            cols = pl.ds(2 * y * NODES, NODES)
            energy = energy + halo[y][x] * product(w_ref, 2 - 2 * x, cols, high[near, :], low[near, :])
    cross = cross - energy * (1.0 / c_ref[0:1, 0:1])
    put_moments(2, mom_ref, mom_out, sq, cross)


def sides(place, operands, last):
    shapes = [FIELD] + ([pltpu.VMEM((SENDERS, 128), F32)] if last else [])
    return pl.pallas_call(
        functools.partial(sides_kernel, last),
        name="sides",
        in_specs=in_specs(len(operands)),
        out_specs=[pl.BlockSpec(memory_space=pltpu.VMEM)] * len(shapes),
        out_shape=shapes,
        scratch_shapes=[pltpu.VMEM((16 * NODES, BZ), BF16), pltpu.VMEM((16 * NODES, BZ), BF16)],
        compiler_params=pltpu.CompilerParams(vmem_limit_bytes=16 << 20),
        cost_estimate=pl.CostEstimate(flops=15 * 10**8, transcendentals=0, bytes_accessed=2 * 10**6),
    )(place, *[vmem(x) for x in operands])


def corners_kernel(order, last, place_ref, sum_ref, v_ref, diag_ref, mask_ref, maskc_ref, ca_ref, cb_ref, w_ref, *rest):
    rest = list(rest)
    mom_ref = rest.pop(0) if order and not last else None
    o_ref = rest.pop(0)
    x_pairs, y_pairs = parity_weights(place_ref)
    sq = jnp.zeros((NODES, BZ), F32)
    cross = jnp.zeros((NODES, BZ), F32)
    masked = [[], []]
    for y in range(2):
        line = [blend(y_pairs[y], ca_ref[:, pl.ds(k * BZ, BZ)], cb_ref[:, pl.ds(k * BZ, BZ)]) for k in range(2)]
        for x in range(2):
            high, low = split(blend(x_pairs[x], line[0], line[1]))
            at = column(x, y)
            total = sum_ref[:, at] + product(w_ref, 2 * x, pl.ds(2 * y * NODES, NODES), high, low)
            v = v_ref[:, at]
            new = diag_ref[:, at] * v - maskc_ref[0:1, at] * total
            o_ref[:, at] = new
            if not last:
                masked[x].append(new * mask_ref[0:1, at])
                sq = sq + v * v
                cross = cross + v * new
    if not last:
        store_edges(place_ref, masked, *rest[1:])
        put_moments(order, mom_ref, rest[0], sq, cross)


def corners(order, place, operands, last):
    shapes = [FIELD] + ([] if last else [pltpu.VMEM((8, 128), F32)] + [EDGE] * 4)
    return pl.pallas_call(
        functools.partial(corners_kernel, order, last),
        name="corners",
        in_specs=in_specs(len(operands)),
        out_specs=[pl.BlockSpec(memory_space=pltpu.VMEM)] * len(shapes),
        out_shape=shapes,
        compiler_params=pltpu.CompilerParams(vmem_limit_bytes=16 << 20),
        cost_estimate=pl.CostEstimate(flops=5 * 10**8, transcendentals=0, bytes_accessed=2 * 10**6),
    )(place, *[vmem(x) for x in operands])


def apply_stiffness(order, place, v, diag, mask, maskc, centre, edges, weights, moments):
    last = order == 2
    ra, rb, ya, yb, ca, cb = exchange(place[1], *edges)
    operands = [v, mask, ra, rb, ya, yb, weights] + ([diag, maskc, centre, moments] if last else [])
    part, *shared = sides(place, operands, last)
    operands = [part, v, diag, mask, maskc, ca, cb, weights]
    if last:
        return corners(order, place, operands, last)[0], shared[0], []
    new, moments, *edges = corners(order, place, operands + ([] if moments is None else [moments]), last)
    return new, moments, edges


def finish_kernel(mom_ref, c_ref, v0_ref, v1_ref, v2_ref, v3_ref, x_ref, r_ref):
    row = jnp.sum(mom_ref[...], axis=0, keepdims=True)
    lanes = lane_iota((1, 128))
    m = [jnp.sum(jnp.where(lanes == k, row, 0.0), keepdims=True) for k in range(6)]
    zero = jnp.zeros((1, 1), F32)
    one = jnp.ones((1, 1), F32)

    def inner(f, g):
        total = zero
        for i, a in enumerate(f):
            for j, b in enumerate(g):
                if a is not None and b is not None:
                    total = total + a * b * m[i + j]
        return total

    r = [one, None, None, None]
    p = [one, None, None, None]
    x = [None, None, None]
    norm = m[0]

    def plus(a, b):
        if a is None:
            return b
        return a if b is None else a + b

    for step in range(3):
        image = [plus(p[k], p[k - 1] if k else None) for k in range(4)]
        alpha = norm / inner(p, image)
        for k in range(3):
            if p[k] is not None:
                x[k] = plus(x[k], alpha * p[k])
        for k in range(4):
            if image[k] is not None:
                r[k] = plus(r[k], -(alpha * image[k]))
        if step < 2:
            new = inner(r, r)
            beta = new / norm
            p = [plus(r[k], None if p[k] is None else beta * p[k]) for k in range(4)]
            norm = new
    inverse = 1.0 / c_ref[0:1, 0:1]
    x = [value * inverse for value in x]
    for chunk in range(8):
        bx, by, zt = chunk // 4, chunk // 2 % 2, chunk % 2
        spot = bx * 4 + zt * 2 + by
        at = pl.ds(chunk * 128, 128)
        v0, v1, v2, v3 = v0_ref[:, at], v1_ref[:, at], v2_ref[:, at], v3_ref[:, at]
        x_ref[:, spot, :] = x[0] * v0 + x[1] * v1 + x[2] * v2
        r_ref[:, spot, :] = r[0] * v0 + r[1] * v1 + r[2] * v2 + r[3] * v3


def finish(moments, centre, fields):
    out = jax.ShapeDtypeStruct((NODES, 8, 128), F32)
    return pl.pallas_call(
        finish_kernel,
        name="finish",
        in_specs=[pl.BlockSpec(memory_space=pltpu.VMEM)] * 6,
        out_specs=[pl.BlockSpec(memory_space=pltpu.VMEM)] * 2,
        out_shape=[out, out],
        compiler_params=pltpu.CompilerParams(vmem_limit_bytes=16 << 20),
    )(moments, *[vmem(x) for x in (centre, *fields)])


def swap(axis, first):
    count = lax.axis_size(axis)
    return [(i, (i + 1 if (i - first) % 2 == 0 else i - 1) % count) for i in range(count)]


def exchange(grp, ea, eb, oa, ob):
    yb = lax.ppermute(ob, "grp", swap("grp", 1))
    ra = lax.ppermute(ea, "slab", swap("slab", 0))
    rb = lax.ppermute(eb, "slab", swap("slab", 1))
    ya = lax.ppermute(oa, "grp", swap("grp", 0))
    up = grp % 2 == 0

    def line(upper):
        return jnp.concatenate([jnp.where(upper, r[:, BZ:], r[:, :BZ]) for r in (ra, rb)], axis=1)

    cb = lax.ppermute(line(jnp.logical_not(up)), "grp", swap("grp", 1))
    ca = lax.ppermute(line(up), "grp", swap("grp", 0))
    return ra, rb, ya, yb, ca, cb


def on_device(samples, block_ids, tile_counts, occupied, coupling):
    slab, grp = lax.axis_index("slab"), lax.axis_index("grp")
    place = jnp.stack([slab, grp, lax.axis_size("slab"), lax.axis_size("grp")]).astype(jnp.int32)
    payload = splat(samples, tile_counts, block_ids)
    recv = lax.all_to_all(payload.reshape(SENDERS, 1, ROWS * 128), AXES, split_axis=0, concat_axis=0, tiled=True)
    weights, rowabs, mask = prepare(coupling, occupied)
    v, diag, maskc, centre, *edges = assemble(place, recv.reshape(SENDERS * ROWS, 128), mask, rowabs)
    fields = [v]
    moments = None
    for order in range(3):
        v, moments, edges = apply_stiffness(
            order, place, v, diag, mask, maskc, centre, edges, weights, moments
        )
        fields.append(v)
    shared = lax.all_to_all(moments.reshape(SENDERS, 1, 128), AXES, split_axis=0, concat_axis=0, tiled=True)
    outs = finish(shared.reshape(SENDERS, 128), centre, fields)

    def settle(out):
        out = out.reshape(NODES, 2, 2, 2, 128)
        return jnp.transpose(out, (0, 1, 3, 2, 4)).reshape(NODES, 2, 2, BZ)

    return settle(outs[0]), settle(outs[1])


def solution(mesh):
    placed = (P(AXES, None, None), P(AXES), P(AXES), P("slab", "grp", None), P())
    return jax.shard_map(
        on_device,
        mesh=mesh,
        in_specs=placed,
        out_specs=(P(None, "slab", "grp", None), P(None, "slab", "grp", None)),
        check_vma=False,
    )
```

```python
import functools

import jax
import jax.numpy as jnp
from jax import lax
from jax.experimental import pallas as pl
from jax.experimental.pallas import tpu as pltpu
from jax.sharding import PartitionSpec as P

AXES = ("slab", "grp")
F32 = jnp.float32
BF16 = jnp.bfloat16
N_COLS = 4
BZ = 256
NODES = 64
SENDERS = 128
CAP = 8
ROWS = CAP + 1


def lane_iota(shape):
    return lax.broadcasted_iota(jnp.int32, shape, len(shape) - 1)


def row_iota(shape):
    return lax.broadcasted_iota(jnp.int32, shape, 0)


def basis_of(pos):
    u = 4.0 * pos
    w = u - jnp.floor(u)
    back = w - 1.0
    low = back * back
    high = w * w
    turn = w * back
    mid = 1.0 - (turn + turn)
    smid = -(w + back)
    in0, in1, in2 = u < 1.0, u < 2.0, u < 3.0
    zero = jnp.zeros_like(u)

    def nodes(below, at, above):
        return [
            jnp.where(in0, at, jnp.where(in1, below, zero)),
            jnp.where(in0, above, jnp.where(in1, at, jnp.where(in2, below, zero))),
            jnp.where(in0, zero, jnp.where(in1, above, jnp.where(in2, at, below))),
            jnp.where(in1, zero, jnp.where(in2, above, at)),
        ]

    return nodes(low, mid, high), nodes(back, smid, w)


def splat_kernel(samp_ref, cnt_ref, ids_ref, out_ref, held, sems, flip, basis, acc, stats):
    groups = out_ref.shape[0]

    def fetch(g):
        return pltpu.make_async_copy(samp_ref.at[:, pl.ds(g * 128, 128), :], held.at[g], sems.at[g])

    def turn(g):
        for k in range(6):
            flip[k] = held[g, k].T

    def evaluate(g):
        counts = cnt_ref[pl.ds(g, 1), :]
        for group in range(16):
            rows = pl.ds(group * 8, 8)
            live = row_iota((8, 128)) + group * 8 < counts
            n0 = jnp.where(live, flip[3, rows, :], 0.0)
            n1 = jnp.where(live, flip[4, rows, :], 0.0)
            n2 = jnp.where(live, flip[5, rows, :], 0.0)
            eighth = jnp.where(live, 0.125, 0.0)
            val, slo = basis_of(flip[0, rows, :])
            for i in range(4):
                basis[i, rows, :] = slo[i] * n0
                basis[4 + i, rows, :] = val[i] * n1
                basis[8 + i, rows, :] = val[i] * n2
                basis[12 + i, rows, :] = val[i] * eighth
            for d in (1, 2):
                val, slo = basis_of(flip[d, rows, :])
                for i in range(4):
                    basis[8 + 8 * d + i, rows, :] = val[i]
                    basis[12 + 8 * d + i, rows, :] = slo[i]

    def accumulate(i, js):
        rhs_sums, dens_sums = {}, {}
        for group in range(16):
            rows = pl.ds(group * 8, 8)
            a = basis[i, rows, :]
            b = basis[4 + i, rows, :]
            c = basis[8 + i, rows, :]
            d = basis[12 + i, rows, :]
            v2 = [basis[24 + l, rows, :] for l in range(4)]
            s2 = [basis[28 + l, rows, :] for l in range(4)]
            for j in js:
                v1 = basis[16 + j, rows, :]
                s1 = basis[20 + j, rows, :]
                first = a * v1 + b * s1
                second = c * v1
                dens = d * v1
                for l in range(4):
                    at = j * 4 + l
                    rhs = first * v2[l] + second * s2[l]
                    den = dens * v2[l]
                    rhs_sums[at] = rhs if group == 0 else rhs_sums[at] + rhs
                    dens_sums[at] = den if group == 0 else dens_sums[at] + den
        for at in rhs_sums:
            acc[pl.ds((i * 16 + at) * 8, 8), :] = rhs_sums[at]
            acc[pl.ds((64 + i * 16 + at) * 8, 8), :] = dens_sums[at]

    def settle(g, real):
        total = acc[pl.ds(0, 128, stride=8), :]
        for s in range(1, 8):
            total = total + acc[pl.ds(s, 128, stride=8), :]
        square = total[:64] * total[:64]
        weighted = total[64:] * square
        part, wpart = square[:8], weighted[:8]
        for k in range(1, 8):
            part = part + square[8 * k : 8 * k + 8]
            wpart = wpart + weighted[8 * k : 8 * k + 8]
        stats[0] = stats[0] + jnp.where(real, part, 0.0)
        stats[1] = stats[1] + jnp.where(real, wpart, 0.0)
        by_tile = total.T
        for d in range(16):
            out_ref[g, pl.ds(ROWS * d, 8), :] = by_tile[8 * d : 8 * d + 8]

    for g in range(groups):
        fetch(g).start()
    stats[...] = jnp.zeros_like(stats)
    acc[...] = jnp.zeros_like(acc)
    fetch(0).wait()
    turn(0)

    def advance(g, carry):
        following = jnp.minimum(g + 1, groups - 1)

        @pl.when(g + 1 < groups)
        def _():
            fetch(following).wait()

        settle(jnp.maximum(g - 1, 0), g > 0)
        evaluate(g)
        turn(following)
        for i in range(4):
            for js in ((0, 1), (2, 3)):
                accumulate(i, js)
        return carry

    lax.fori_loop(0, groups, advance, 0)
    settle(groups - 1, True)
    ids = ids_ref[...]
    local = ((ids >> 14) & 1) * 512 + ((ids >> 8) & 1) * 256 + (ids & 255)
    local = local.astype(F32)
    sum0 = jnp.sum(stats[0], keepdims=True)
    sum1 = jnp.sum(stats[1], keepdims=True)
    lanes = lane_iota((1, 128))
    both = jnp.where(lanes % 2 == 0, sum0, sum1)
    for g in range(groups):
        for d in range(16):
            row = jnp.where(lanes // 8 == d, local[g : g + 1], both)
            out_ref[g, pl.ds(ROWS * d + CAP, 1), :] = row


def splat(samples, counts, ids):
    tiles = samples.shape[0]
    groups = tiles // 128
    return pl.pallas_call(
        splat_kernel,
        name="splat",
        in_specs=[pl.BlockSpec(memory_space=pltpu.HBM)] + [pl.BlockSpec(memory_space=pltpu.VMEM)] * 2,
        out_specs=pl.BlockSpec(memory_space=pltpu.VMEM),
        out_shape=pltpu.VMEM((groups, 16 * ROWS, 128), F32),
        scratch_shapes=[
            pltpu.VMEM((groups, 6, 128, 128), F32),
            pltpu.SemaphoreType.DMA((groups,)),
            pltpu.VMEM((6, 128, 128), F32),
            pltpu.VMEM((32, 128, 128), F32),
            pltpu.VMEM((1024, 128), F32),
            pltpu.VMEM((2, 8, 128), F32),
        ],
        compiler_params=pltpu.CompilerParams(vmem_limit_bytes=24 << 20),
    )(pltpu.with_memory_space_constraint(jnp.transpose(samples, (1, 0, 2)), pltpu.HBM), counts.reshape(groups, 128), ids.reshape(groups, 128))


def vmem(x):
    return pltpu.with_memory_space_constraint(x, pltpu.VMEM)


def parity_weights(place_ref):
    slab, grp = place_ref[0], place_ref[1]
    slabs, grps = place_ref[2], place_ref[3]

    def pick(cond):
        return jnp.where(cond, 1.0, 0.0).astype(F32)

    def sides(at, count):
        odd = at % 2 == 1
        low = (pick(odd), pick(jnp.logical_and(jnp.logical_not(odd), at > 0)))
        high = (pick(jnp.logical_not(odd)), pick(jnp.logical_and(odd, at < count - 1)))
        return low, high

    return sides(slab, slabs), sides(grp, grps)


def blend(pair, a, b):
    return a * pair[0] + b * pair[1]


def column(x, y):
    return pl.ds((x * 2 + y) * BZ, BZ)


def store_edges(place_ref, masked, ea_ref, eb_ref, oa_ref, ob_ref):
    up_slab = place_ref[0] % 2 == 0
    up_grp = place_ref[1] % 2 == 0
    for k in range(2):
        at = pl.ds(k * BZ, BZ)
        ea_ref[:, at] = jnp.where(up_slab, masked[1][k], masked[0][k])
        eb_ref[:, at] = jnp.where(up_slab, masked[0][k], masked[1][k])
        oa_ref[:, at] = jnp.where(up_grp, masked[k][1], masked[k][0])
        ob_ref[:, at] = jnp.where(up_grp, masked[k][0], masked[k][1])


def prepare_kernel(coupling_ref, occ_ref, w_ref, rowabs_ref, mask_ref):
    total = jnp.zeros((NODES, NODES), F32)
    for dx in range(3):
        for dz in range(3):
            parts = []
            for dy in range(3):
                k = (dx * 3 + dy) * 3 + dz
                coupled = 0.5 * (coupling_ref[k] + coupling_ref[26 - k].T)
                total = total + jnp.abs(coupled)
                parts.append(coupled)
            wide = jnp.concatenate(parts, axis=1)
            high = wide.astype(BF16)
            w_ref[dx, pl.ds(dz * NODES, NODES), :] = high
            w_ref[dx, pl.ds((3 + dz) * NODES, NODES), :] = (wide - high.astype(F32)).astype(BF16)
    rowabs_ref[...] = jnp.broadcast_to(jnp.sum(total, axis=1, keepdims=True), (NODES, 128))
    for x in range(2):
        for y in range(2):
            mask_ref[:, column(x, y)] = jnp.broadcast_to(occ_ref[x, y : y + 1, :].astype(F32), (8, BZ))


def prepare(coupling, occupied):
    return pl.pallas_call(
        prepare_kernel,
        name="prepare",
        in_specs=[pl.BlockSpec(memory_space=pltpu.VMEM)] * 2,
        out_specs=[pl.BlockSpec(memory_space=pltpu.VMEM)] * 3,
        out_shape=[
            pltpu.VMEM((3, 6 * NODES, 3 * NODES), BF16),
            pltpu.VMEM((NODES, 128), F32),
            pltpu.VMEM((8, N_COLS * BZ), F32),
        ],
        compiler_params=pltpu.CompilerParams(vmem_limit_bytes=8 << 20),
        cost_estimate=pl.CostEstimate(flops=10**7, transcendentals=0, bytes_accessed=4 * 10**6),
    )(coupling, occupied)


def assemble_kernel(place_ref, recv_ref, mask_ref, rowabs_ref, v_ref, diag_ref, maskc_ref, c_ref,
                    ea_ref, eb_ref, oa_ref, ob_ref, turned):
    seat = place_ref[1] % 16
    turned[...] = recv_ref[pl.ds(CAP, SENDERS, stride=ROWS), :].T
    where = turned[pl.ds(pl.multiple_of(seat * 8, 8), 8), :].astype(jnp.int32)
    other = lax.rem(seat + 1, 16)
    sums = turned[pl.ds(pl.multiple_of(other * 8, 8), 8), :]
    sum0 = jnp.sum(sums[0:1, :], keepdims=True)
    sum1 = jnp.sum(sums[1:2, :], keepdims=True)
    rowabs = rowabs_ref[...]
    mean = jnp.sum(rowabs[:, 0:1], keepdims=True) * (1.0 / NODES)
    centre = mean + 0.5 + 4.0 * (sum1 / sum0)
    inverse = 1.0 / centre
    c_ref[...] = jnp.broadcast_to(centre, (8, 128))
    tiles = []
    for c in range(CAP):
        block = recv_ref[pl.ds(c, SENDERS, stride=ROWS), :]
        high = block.astype(BF16)
        low = (block - high.astype(F32)).astype(BF16)
        tiles.append(jnp.concatenate([high, low], axis=1))
    table = jnp.concatenate(tiles, axis=0)
    masked = []
    for x in range(2):
        masked.append([])
        for y in range(2):
            picks = []
            for c in range(CAP):
                hit = row_iota((BZ, SENDERS)) + (x * 2 + y) * BZ == where[c : c + 1, :]
                picks.append(hit.astype(F32).astype(BF16))
            pick = jnp.concatenate(picks, axis=1)
            both = jnp.dot(pick, table, preferred_element_type=F32)
            ordered = (both[:, :128] + both[:, 128:]).T
            rhs = ordered[:NODES]
            dens = ordered[NODES:]
            mask = mask_ref[0:1, column(x, y)]
            v_ref[:, column(x, y)] = rhs
            diag = rowabs[:, 0:1] + 0.5 + 4.0 * dens
            diag_ref[:, column(x, y)] = (diag - centre) * inverse
            maskc_ref[:, column(x, y)] = jnp.broadcast_to(mask * inverse, (8, BZ))
            masked[x].append(rhs * mask)
    store_edges(place_ref, masked, ea_ref, eb_ref, oa_ref, ob_ref)


FIELD = pltpu.VMEM((NODES, N_COLS * BZ), F32)
EDGE = pltpu.VMEM((NODES, 2 * BZ), F32)


def in_specs(count):
    return [pl.BlockSpec(memory_space=pltpu.SMEM)] + [pl.BlockSpec(memory_space=pltpu.VMEM)] * count


def assemble(place, recv, mask, rowabs):
    return pl.pallas_call(
        assemble_kernel,
        name="assemble",
        in_specs=in_specs(3),
        out_specs=[pl.BlockSpec(memory_space=pltpu.VMEM)] * 8,
        out_shape=[FIELD, FIELD, pltpu.VMEM((8, N_COLS * BZ), F32), pltpu.VMEM((8, 128), F32), EDGE, EDGE, EDGE, EDGE],
        scratch_shapes=[pltpu.VMEM((128, 128), F32)],
        compiler_params=pltpu.CompilerParams(vmem_limit_bytes=16 << 20),
    )(place, vmem(recv), vmem(mask), vmem(rowabs))


def spread(part):
    lanes = lane_iota((NODES, BZ))
    before = jnp.where(lanes == 0, 0.0, pltpu.roll(part[:NODES], 1, 1))
    after = jnp.where(lanes == BZ - 1, 0.0, pltpu.roll(part[2 * NODES :], BZ - 1, 1))
    return part[NODES : 2 * NODES] + before + after


def split(src):
    top = src.astype(BF16)
    return top, (src - top.astype(F32)).astype(BF16)


def product(w_ref, dx, cols, high, low):
    full = jnp.dot(w_ref[dx, :, cols], high, preferred_element_type=F32)
    half = jnp.dot(w_ref[dx, 0 : 3 * NODES, cols], low, preferred_element_type=F32)
    return spread(full[: 3 * NODES] + full[3 * NODES :] + half)


def put_moments(order, mom_ref, mom_out, sq, cross):
    sq = jnp.sum(sq, keepdims=True)
    cross = jnp.sum(cross, keepdims=True)
    spot = lane_iota((1, 128))
    before = jnp.zeros((1, 128), F32) if mom_ref is None else mom_ref[0:1, :]
    mom = jnp.where(spot == 2 * order, sq, jnp.where(spot == 2 * order + 1, cross, before))
    mom_out[...] = jnp.broadcast_to(mom, mom_out.shape)


def sides_kernel(last, place_ref, v_ref, mask_ref, ra_ref, rb_ref, ya_ref, yb_ref, w_ref, *rest):
    if last:
        diag_ref, maskc_ref, c_ref, mom_ref, o_ref, mom_out, high, low = rest
    else:
        o_ref, high, low = rest
    (x_low, x_high), (y_low, y_high) = parity_weights(place_ref)
    halo = {}

    def at_rows(px, py):
        return pl.ds((px * 4 + py) * NODES, NODES)

    def put(px, py, src):
        high[at_rows(px, py), :], low[at_rows(px, py), :] = split(src)

    for x in range(2):
        for y in range(2):
            put(x + 1, y + 1, v_ref[:, column(x, y)] * mask_ref[0:1, column(x, y)])
    for k in range(2):
        at = pl.ds(k * BZ, BZ)
        halo[k] = (blend(x_low, ra_ref[:, at], rb_ref[:, at]), blend(x_high, ra_ref[:, at], rb_ref[:, at]))
        put(0, k + 1, halo[k][0])
        put(3, k + 1, halo[k][1])
        put(k + 1, 0, blend(y_low, ya_ref[:, at], yb_ref[:, at]))
        put(k + 1, 3, blend(y_high, ya_ref[:, at], yb_ref[:, at]))
    nothing = jnp.zeros((NODES, BZ), BF16)
    for px in (0, 3):
        for py in (0, 3):
            high[at_rows(px, py), :] = nothing
            low[at_rows(px, py), :] = nothing
    sq = jnp.zeros((NODES, BZ), F32)
    cross = jnp.zeros((NODES, BZ), F32)
    for x in range(2):
        for y in range(2):
            full = jnp.zeros((6 * NODES, BZ), F32)
            half = jnp.zeros((3 * NODES, BZ), F32)
            for dx in range(3):
                rows = pl.ds(((x + dx) * 4 + y) * NODES, 3 * NODES)
                full = full + jnp.dot(w_ref[dx], high[rows, :], preferred_element_type=F32)
                half = half + jnp.dot(w_ref[dx, 0 : 3 * NODES, :], low[rows, :], preferred_element_type=F32)
            at = column(x, y)
            total = spread(full[: 3 * NODES] + full[3 * NODES :] + half)
            o_ref[:, at] = total
            if last:
                v = v_ref[:, at]
                sq = sq + v * v
                cross = cross + v * (diag_ref[:, at] * v - maskc_ref[0:1, at] * total)
    if not last:
        return
    energy = jnp.zeros((NODES, BZ), F32)
    for x in range(2):
        for y in range(2):
            near = at_rows(x + 1, 3 * y)
            cols = pl.ds(2 * y * NODES, NODES)
            energy = energy + halo[y][x] * product(w_ref, 2 - 2 * x, cols, high[near, :], low[near, :])
    cross = cross - energy * (1.0 / c_ref[0:1, 0:1])
    put_moments(2, mom_ref, mom_out, sq, cross)


def sides(place, operands, last):
    shapes = [FIELD] + ([pltpu.VMEM((SENDERS, 128), F32)] if last else [])
    return pl.pallas_call(
        functools.partial(sides_kernel, last),
        name="sides",
        in_specs=in_specs(len(operands)),
        out_specs=[pl.BlockSpec(memory_space=pltpu.VMEM)] * len(shapes),
        out_shape=shapes,
        scratch_shapes=[pltpu.VMEM((16 * NODES, BZ), BF16), pltpu.VMEM((16 * NODES, BZ), BF16)],
        compiler_params=pltpu.CompilerParams(vmem_limit_bytes=16 << 20),
        cost_estimate=pl.CostEstimate(flops=15 * 10**8, transcendentals=0, bytes_accessed=2 * 10**6),
    )(place, *[vmem(x) for x in operands])


def corners_kernel(order, last, place_ref, sum_ref, v_ref, diag_ref, mask_ref, maskc_ref, ca_ref, cb_ref, w_ref, *rest):
    rest = list(rest)
    mom_ref = rest.pop(0) if order and not last else None
    o_ref = rest.pop(0)
    x_pairs, y_pairs = parity_weights(place_ref)
    sq = jnp.zeros((NODES, BZ), F32)
    cross = jnp.zeros((NODES, BZ), F32)
    masked = [[], []]
    for y in range(2):
        line = [blend(y_pairs[y], ca_ref[:, pl.ds(k * BZ, BZ)], cb_ref[:, pl.ds(k * BZ, BZ)]) for k in range(2)]
        for x in range(2):
            high, low = split(blend(x_pairs[x], line[0], line[1]))
            at = column(x, y)
            total = sum_ref[:, at] + product(w_ref, 2 * x, pl.ds(2 * y * NODES, NODES), high, low)
            v = v_ref[:, at]
            new = diag_ref[:, at] * v - maskc_ref[0:1, at] * total
            o_ref[:, at] = new
            if not last:
                masked[x].append(new * mask_ref[0:1, at])
                sq = sq + v * v
                cross = cross + v * new
    if not last:
        store_edges(place_ref, masked, *rest[1:])
        put_moments(order, mom_ref, rest[0], sq, cross)


def corners(order, place, operands, last):
    shapes = [FIELD] + ([] if last else [pltpu.VMEM((8, 128), F32)] + [EDGE] * 4)
    return pl.pallas_call(
        functools.partial(corners_kernel, order, last),
        name="corners",
        in_specs=in_specs(len(operands)),
        out_specs=[pl.BlockSpec(memory_space=pltpu.VMEM)] * len(shapes),
        out_shape=shapes,
        compiler_params=pltpu.CompilerParams(vmem_limit_bytes=16 << 20),
        cost_estimate=pl.CostEstimate(flops=5 * 10**8, transcendentals=0, bytes_accessed=2 * 10**6),
    )(place, *[vmem(x) for x in operands])


def apply_stiffness(order, place, v, diag, mask, maskc, centre, edges, weights, moments):
    last = order == 2
    ra, rb, ya, yb, ca, cb = exchange(place[1], *edges)
    operands = [v, mask, ra, rb, ya, yb, weights] + ([diag, maskc, centre, moments] if last else [])
    part, *shared = sides(place, operands, last)
    operands = [part, v, diag, mask, maskc, ca, cb, weights]
    if last:
        return corners(order, place, operands, last)[0], shared[0], []
    new, moments, *edges = corners(order, place, operands + ([] if moments is None else [moments]), last)
    return new, moments, edges


def finish_kernel(mom_ref, c_ref, v0_ref, v1_ref, v2_ref, v3_ref, x_ref, r_ref):
    row = jnp.sum(mom_ref[...], axis=0, keepdims=True)
    lanes = lane_iota((1, 128))
    m = [jnp.sum(jnp.where(lanes == k, row, 0.0), keepdims=True) for k in range(6)]
    zero = jnp.zeros((1, 1), F32)
    one = jnp.ones((1, 1), F32)

    def inner(f, g):
        total = zero
        for i, a in enumerate(f):
            for j, b in enumerate(g):
                if a is not None and b is not None:
                    total = total + a * b * m[i + j]
        return total

    r = [one, None, None, None]
    p = [one, None, None, None]
    x = [None, None, None]
    norm = m[0]

    def plus(a, b):
        if a is None:
            return b
        return a if b is None else a + b

    for step in range(3):
        image = [plus(p[k], p[k - 1] if k else None) for k in range(4)]
        alpha = norm / inner(p, image)
        for k in range(3):
            if p[k] is not None:
                x[k] = plus(x[k], alpha * p[k])
        for k in range(4):
            if image[k] is not None:
                r[k] = plus(r[k], -(alpha * image[k]))
        if step < 2:
            new = inner(r, r)
            beta = new / norm
            p = [plus(r[k], None if p[k] is None else beta * p[k]) for k in range(4)]
            norm = new
    inverse = 1.0 / c_ref[0:1, 0:1]
    x = [value * inverse for value in x]
    for chunk in range(8):
        bx, by, zt = chunk // 4, chunk // 2 % 2, chunk % 2
        spot = bx * 4 + zt * 2 + by
        at = pl.ds(chunk * 128, 128)
        v0, v1, v2, v3 = v0_ref[:, at], v1_ref[:, at], v2_ref[:, at], v3_ref[:, at]
        x_ref[:, spot, :] = x[0] * v0 + x[1] * v1 + x[2] * v2
        r_ref[:, spot, :] = r[0] * v0 + r[1] * v1 + r[2] * v2 + r[3] * v3


def finish(moments, centre, fields):
    out = jax.ShapeDtypeStruct((NODES, 8, 128), F32)
    return pl.pallas_call(
        finish_kernel,
        name="finish",
        in_specs=[pl.BlockSpec(memory_space=pltpu.VMEM)] * 6,
        out_specs=[pl.BlockSpec(memory_space=pltpu.VMEM)] * 2,
        out_shape=[out, out],
        compiler_params=pltpu.CompilerParams(vmem_limit_bytes=16 << 20),
    )(moments, *[vmem(x) for x in (centre, *fields)])


def swap(axis, first):
    count = lax.axis_size(axis)
    return [(i, (i + 1 if (i - first) % 2 == 0 else i - 1) % count) for i in range(count)]


def odd_swap():
    slabs, grps = lax.axis_size("slab"), lax.axis_size("grp")
    pairs = []
    for s in range(slabs):
        for g in range(grps):
            if g in (0, grps - 1):
                pairs.append((s * grps + g, (s ^ 1) * grps + g))
            else:
                pairs.append((s * grps + g, s * grps + (g + 1 if g % 2 else g - 1)))
    return pairs


def exchange(grp, ea, eb, oa, ob):
    yb = lax.ppermute(ob, AXES, odd_swap())
    ra = lax.ppermute(ea, "slab", swap("slab", 0))
    rb = lax.ppermute(eb, "slab", swap("slab", 1))
    ya = lax.ppermute(oa, "grp", swap("grp", 0))
    up = grp % 2 == 0

    def line(upper):
        return jnp.concatenate([jnp.where(upper, r[:, BZ:], r[:, :BZ]) for r in (ra, rb)], axis=1)

    cb = lax.ppermute(line(jnp.logical_not(up)), AXES, odd_swap())
    ca = lax.ppermute(line(up), "grp", swap("grp", 0))
    return ra, rb, ya, yb, ca, cb


def on_device(samples, block_ids, tile_counts, occupied, coupling):
    slab, grp = lax.axis_index("slab"), lax.axis_index("grp")
    place = jnp.stack([slab, grp, lax.axis_size("slab"), lax.axis_size("grp")]).astype(jnp.int32)
    payload = splat(samples, tile_counts, block_ids)
    recv = lax.all_to_all(payload.reshape(SENDERS, 1, ROWS * 128), AXES, split_axis=0, concat_axis=0, tiled=True)
    weights, rowabs, mask = prepare(coupling, occupied)
    v, diag, maskc, centre, *edges = assemble(place, recv.reshape(SENDERS * ROWS, 128), mask, rowabs)
    fields = [v]
    moments = None
    for order in range(3):
        v, moments, edges = apply_stiffness(
            order, place, v, diag, mask, maskc, centre, edges, weights, moments
        )
        fields.append(v)
    shared = lax.all_to_all(moments.reshape(SENDERS, 1, 128), AXES, split_axis=0, concat_axis=0, tiled=True)
    outs = finish(shared.reshape(SENDERS, 128), centre, fields)

    def settle(out):
        out = out.reshape(NODES, 2, 2, 2, 128)
        return jnp.transpose(out, (0, 1, 3, 2, 4)).reshape(NODES, 2, 2, BZ)

    return settle(outs[0]), settle(outs[1])


def solution(mesh):
    placed = (P(AXES, None, None), P(AXES), P(AXES), P("slab", "grp", None), P())
    return jax.shard_map(
        on_device,
        mesh=mesh,
        in_specs=placed,
        out_specs=(P(None, "slab", "grp", None), P(None, "slab", "grp", None)),
        check_vma=False,
    )
```

```python
import functools

import jax
import jax.numpy as jnp
from jax import lax
from jax.experimental import pallas as pl
from jax.experimental.pallas import tpu as pltpu
from jax.sharding import PartitionSpec as P

AXES = ("slab", "grp")
F32 = jnp.float32
BF16 = jnp.bfloat16
N_COLS = 4
BZ = 256
NODES = 64
SENDERS = 128
CAP = 8
ROWS = CAP + 1


def lane_iota(shape):
    return lax.broadcasted_iota(jnp.int32, shape, len(shape) - 1)


def row_iota(shape):
    return lax.broadcasted_iota(jnp.int32, shape, 0)


def basis_of(pos):
    u = 4.0 * pos
    w = u - jnp.floor(u)
    back = w - 1.0
    low = back * back
    high = w * w
    turn = w * back
    mid = 1.0 - (turn + turn)
    smid = -(w + back)
    in0, in1, in2 = u < 1.0, u < 2.0, u < 3.0
    zero = jnp.zeros_like(u)

    def nodes(below, at, above):
        return [
            jnp.where(in0, at, jnp.where(in1, below, zero)),
            jnp.where(in0, above, jnp.where(in1, at, jnp.where(in2, below, zero))),
            jnp.where(in0, zero, jnp.where(in1, above, jnp.where(in2, at, below))),
            jnp.where(in1, zero, jnp.where(in2, above, at)),
        ]

    return nodes(low, mid, high), nodes(back, smid, w)


def splat_kernel(samp_ref, cnt_ref, ids_ref, out_ref, held, sems, flip, basis, acc, stats):
    groups = out_ref.shape[0]

    def fetch(g):
        return pltpu.make_async_copy(samp_ref.at[:, pl.ds(g * 128, 128), :], held.at[g], sems.at[g])

    def turn(g):
        for k in range(6):
            flip[k] = held[g, k].T

    def evaluate(g):
        counts = cnt_ref[pl.ds(g, 1), :]
        for group in range(16):
            rows = pl.ds(group * 8, 8)
            live = row_iota((8, 128)) + group * 8 < counts
            n0 = jnp.where(live, flip[3, rows, :], 0.0)
            n1 = jnp.where(live, flip[4, rows, :], 0.0)
            n2 = jnp.where(live, flip[5, rows, :], 0.0)
            eighth = jnp.where(live, 0.125, 0.0)
            val, slo = basis_of(flip[0, rows, :])
            for i in range(4):
                basis[i, rows, :] = slo[i] * n0
                basis[4 + i, rows, :] = val[i] * n1
                basis[8 + i, rows, :] = val[i] * n2
                basis[12 + i, rows, :] = val[i] * eighth
            for d in (1, 2):
                val, slo = basis_of(flip[d, rows, :])
                for i in range(4):
                    basis[8 + 8 * d + i, rows, :] = val[i]
                    basis[12 + 8 * d + i, rows, :] = slo[i]

    def accumulate(i, js):
        rhs_sums, dens_sums = {}, {}
        for group in range(16):
            rows = pl.ds(group * 8, 8)
            a = basis[i, rows, :]
            b = basis[4 + i, rows, :]
            c = basis[8 + i, rows, :]
            d = basis[12 + i, rows, :]
            v2 = [basis[24 + l, rows, :] for l in range(4)]
            s2 = [basis[28 + l, rows, :] for l in range(4)]
            for j in js:
                v1 = basis[16 + j, rows, :]
                s1 = basis[20 + j, rows, :]
                first = a * v1 + b * s1
                second = c * v1
                dens = d * v1
                for l in range(4):
                    at = j * 4 + l
                    rhs = first * v2[l] + second * s2[l]
                    den = dens * v2[l]
                    rhs_sums[at] = rhs if group == 0 else rhs_sums[at] + rhs
                    dens_sums[at] = den if group == 0 else dens_sums[at] + den
        for at in rhs_sums:
            acc[pl.ds((i * 16 + at) * 8, 8), :] = rhs_sums[at]
            acc[pl.ds((64 + i * 16 + at) * 8, 8), :] = dens_sums[at]

    def settle(g, real):
        total = acc[pl.ds(0, 128, stride=8), :]
        for s in range(1, 8):
            total = total + acc[pl.ds(s, 128, stride=8), :]
        square = total[:64] * total[:64]
        weighted = total[64:] * square
        part, wpart = square[:8], weighted[:8]
        for k in range(1, 8):
            part = part + square[8 * k : 8 * k + 8]
            wpart = wpart + weighted[8 * k : 8 * k + 8]
        stats[0] = stats[0] + jnp.where(real, part, 0.0)
        stats[1] = stats[1] + jnp.where(real, wpart, 0.0)
        by_tile = total.T
        for d in range(16):
            out_ref[g, pl.ds(ROWS * d, 8), :] = by_tile[8 * d : 8 * d + 8]

    for g in range(groups):
        fetch(g).start()
    stats[...] = jnp.zeros_like(stats)
    acc[...] = jnp.zeros_like(acc)
    fetch(0).wait()
    turn(0)

    def advance(g, carry):
        following = jnp.minimum(g + 1, groups - 1)

        @pl.when(g + 1 < groups)
        def _():
            fetch(following).wait()

        settle(jnp.maximum(g - 1, 0), g > 0)
        evaluate(g)
        turn(following)
        for i in range(4):
            for js in ((0, 1), (2, 3)):
                accumulate(i, js)
        return carry

    lax.fori_loop(0, groups, advance, 0)
    settle(groups - 1, True)
    ids = ids_ref[...]
    local = ((ids >> 14) & 1) * 512 + ((ids >> 8) & 1) * 256 + (ids & 255)
    local = local.astype(F32)
    sum0 = jnp.sum(stats[0], keepdims=True)
    sum1 = jnp.sum(stats[1], keepdims=True)
    lanes = lane_iota((1, 128))
    both = jnp.where(lanes % 2 == 0, sum0, sum1)
    for g in range(groups):
        for d in range(16):
            row = jnp.where(lanes // 8 == d, local[g : g + 1], both)
            out_ref[g, pl.ds(ROWS * d + CAP, 1), :] = row


def splat(samples, counts, ids):
    tiles = samples.shape[0]
    groups = tiles // 128
    return pl.pallas_call(
        splat_kernel,
        name="splat",
        in_specs=[pl.BlockSpec(memory_space=pltpu.HBM)] + [pl.BlockSpec(memory_space=pltpu.VMEM)] * 2,
        out_specs=pl.BlockSpec(memory_space=pltpu.VMEM),
        out_shape=pltpu.VMEM((groups, 16 * ROWS, 128), F32),
        scratch_shapes=[
            pltpu.VMEM((groups, 6, 128, 128), F32),
            pltpu.SemaphoreType.DMA((groups,)),
            pltpu.VMEM((6, 128, 128), F32),
            pltpu.VMEM((32, 128, 128), F32),
            pltpu.VMEM((1024, 128), F32),
            pltpu.VMEM((2, 8, 128), F32),
        ],
        compiler_params=pltpu.CompilerParams(vmem_limit_bytes=24 << 20),
    )(pltpu.with_memory_space_constraint(jnp.transpose(samples, (1, 0, 2)), pltpu.HBM), counts.reshape(groups, 128), ids.reshape(groups, 128))


def vmem(x):
    return pltpu.with_memory_space_constraint(x, pltpu.VMEM)


def parity_weights(place_ref):
    slab, grp = place_ref[0], place_ref[1]
    slabs, grps = place_ref[2], place_ref[3]

    def pick(cond):
        return jnp.where(cond, 1.0, 0.0).astype(F32)

    def sides(at, count):
        odd = at % 2 == 1
        low = (pick(odd), pick(jnp.logical_and(jnp.logical_not(odd), at > 0)))
        high = (pick(jnp.logical_not(odd)), pick(jnp.logical_and(odd, at < count - 1)))
        return low, high

    return sides(slab, slabs), sides(grp, grps)


def blend(pair, a, b):
    return a * pair[0] + b * pair[1]


def column(x, y):
    return pl.ds((x * 2 + y) * BZ, BZ)


def store_edges(place_ref, masked, ea_ref, eb_ref, oa_ref, ob_ref):
    up_slab = place_ref[0] % 2 == 0
    up_grp = place_ref[1] % 2 == 0
    for k in range(2):
        at = pl.ds(k * BZ, BZ)
        ea_ref[:, at] = jnp.where(up_slab, masked[1][k], masked[0][k])
        eb_ref[:, at] = jnp.where(up_slab, masked[0][k], masked[1][k])
        oa_ref[:, at] = jnp.where(up_grp, masked[k][1], masked[k][0])
        ob_ref[:, at] = jnp.where(up_grp, masked[k][0], masked[k][1])


def spread(part):
    lanes = lane_iota((NODES, BZ))
    before = jnp.where(lanes == 0, 0.0, pltpu.roll(part[:NODES], 1, 1))
    after = jnp.where(lanes == BZ - 1, 0.0, pltpu.roll(part[2 * NODES :], BZ - 1, 1))
    return part[NODES : 2 * NODES] + before + after


def split(src):
    top = src.astype(BF16)
    return top, (src - top.astype(F32)).astype(BF16)


def others(x, y):
    return [(dx, dy) for dx in range(3) for dy in range(3) if (dx, dy) != (2 * x, 2 * y)]


def prepare_kernel(coupling_ref, occ_ref, w_ref, corner_ref, rowabs_ref, mask_ref):
    total = jnp.zeros((NODES, NODES), F32)
    high, low = {}, {}
    for dz in range(3):
        for dx in range(3):
            for dy in range(3):
                k = (dx * 3 + dy) * 3 + dz
                coupled = 0.5 * (coupling_ref[k] + coupling_ref[26 - k].T)
                total = total + jnp.abs(coupled)
                high[dx, dy], low[dx, dy] = split(coupled)
        rows = pl.ds(dz * NODES, NODES)
        for x in range(2):
            for y in range(2):
                w_ref[x * 2 + y, rows, :] = jnp.concatenate([high[at] for at in others(x, y)], axis=1)
                w_ref[x * 2 + y, pl.ds((3 + dz) * NODES, NODES), :] = jnp.concatenate(
                    [low[at] for at in others(x, y)], axis=1
                )
                at = (2 * x, 2 * y)
                corner_ref[x * 2 + y, rows, :] = jnp.concatenate([high[at], low[at], high[at]], axis=1)
    rowabs_ref[...] = jnp.broadcast_to(jnp.sum(total, axis=1, keepdims=True), (NODES, 128))
    for x in range(2):
        for y in range(2):
            mask_ref[:, column(x, y)] = jnp.broadcast_to(occ_ref[x, y : y + 1, :].astype(F32), (8, BZ))


def prepare(coupling, occupied):
    return pl.pallas_call(
        prepare_kernel,
        name="prepare",
        in_specs=[pl.BlockSpec(memory_space=pltpu.VMEM)] * 2,
        out_specs=[pl.BlockSpec(memory_space=pltpu.VMEM)] * 4,
        out_shape=[
            pltpu.VMEM((4, 6 * NODES, 8 * NODES), BF16),
            pltpu.VMEM((4, 3 * NODES, 3 * NODES), BF16),
            pltpu.VMEM((NODES, 128), F32),
            pltpu.VMEM((8, N_COLS * BZ), F32),
        ],
        compiler_params=pltpu.CompilerParams(vmem_limit_bytes=12 << 20),
        cost_estimate=pl.CostEstimate(flops=10**7, transcendentals=0, bytes_accessed=4 * 10**6),
    )(coupling, occupied)


def assemble_kernel(place_ref, recv_ref, mask_ref, rowabs_ref, v_ref, diag_ref, maskc_ref, c_ref,
                    ea_ref, eb_ref, oa_ref, ob_ref, turned):
    seat = place_ref[1] % 16
    turned[...] = recv_ref[pl.ds(CAP, SENDERS, stride=ROWS), :].T
    where = turned[pl.ds(pl.multiple_of(seat * 8, 8), 8), :].astype(jnp.int32)
    other = lax.rem(seat + 1, 16)
    sums = turned[pl.ds(pl.multiple_of(other * 8, 8), 8), :]
    sum0 = jnp.sum(sums[0:1, :], keepdims=True)
    sum1 = jnp.sum(sums[1:2, :], keepdims=True)
    rowabs = rowabs_ref[...]
    mean = jnp.sum(rowabs[:, 0:1], keepdims=True) * (1.0 / NODES)
    centre = mean + 0.5 + 4.0 * (sum1 / sum0)
    inverse = 1.0 / centre
    c_ref[...] = jnp.broadcast_to(centre, (8, 128))
    tiles = []
    for c in range(CAP):
        block = recv_ref[pl.ds(c, SENDERS, stride=ROWS), :]
        high = block.astype(BF16)
        low = (block - high.astype(F32)).astype(BF16)
        tiles.append(jnp.concatenate([high, low], axis=1))
    table = jnp.concatenate(tiles, axis=0)
    masked = []
    for x in range(2):
        masked.append([])
        for y in range(2):
            picks = []
            for c in range(CAP):
                hit = row_iota((BZ, SENDERS)) + (x * 2 + y) * BZ == where[c : c + 1, :]
                picks.append(hit.astype(F32).astype(BF16))
            pick = jnp.concatenate(picks, axis=1)
            both = jnp.dot(pick, table, preferred_element_type=F32)
            ordered = (both[:, :128] + both[:, 128:]).T
            rhs = ordered[:NODES]
            dens = ordered[NODES:]
            mask = mask_ref[0:1, column(x, y)]
            v_ref[:, column(x, y)] = rhs
            diag = rowabs[:, 0:1] + 0.5 + 4.0 * dens
            diag_ref[:, column(x, y)] = (diag - centre) * inverse
            maskc_ref[:, column(x, y)] = jnp.broadcast_to(mask * inverse, (8, BZ))
            masked[x].append(rhs * mask)
    store_edges(place_ref, masked, ea_ref, eb_ref, oa_ref, ob_ref)


FIELD = pltpu.VMEM((NODES, N_COLS * BZ), F32)
EDGE = pltpu.VMEM((NODES, 2 * BZ), F32)


def in_specs(count):
    return [pl.BlockSpec(memory_space=pltpu.SMEM)] + [pl.BlockSpec(memory_space=pltpu.VMEM)] * count


def assemble(place, recv, mask, rowabs):
    return pl.pallas_call(
        assemble_kernel,
        name="assemble",
        in_specs=in_specs(3),
        out_specs=[pl.BlockSpec(memory_space=pltpu.VMEM)] * 8,
        out_shape=[FIELD, FIELD, pltpu.VMEM((8, N_COLS * BZ), F32), pltpu.VMEM((8, 128), F32), EDGE, EDGE, EDGE, EDGE],
        scratch_shapes=[pltpu.VMEM((128, 128), F32)],
        compiler_params=pltpu.CompilerParams(vmem_limit_bytes=16 << 20),
    )(place, vmem(recv), vmem(mask), vmem(rowabs))


def product(weights, source):
    high, low = split(source)
    stacked = jnp.concatenate([high, high, low], axis=0)
    return spread(jnp.dot(weights, stacked, preferred_element_type=F32))


def put_moments(order, mom_ref, mom_out, sq, cross):
    sq = jnp.sum(sq, keepdims=True)
    cross = jnp.sum(cross, keepdims=True)
    spot = lane_iota((1, 128))
    before = jnp.zeros((1, 128), F32) if mom_ref is None else mom_ref[0:1, :]
    mom = jnp.where(spot == 2 * order, sq, jnp.where(spot == 2 * order + 1, cross, before))
    mom_out[...] = jnp.broadcast_to(mom, mom_out.shape)


def sides_kernel(last, place_ref, v_ref, mask_ref, ra_ref, rb_ref, ya_ref, yb_ref, w_ref, *rest):
    if last:
        corner_ref, diag_ref, maskc_ref, c_ref, mom_ref, o_ref, mom_out, high, low = rest
    else:
        o_ref, high, low = rest
    (x_low, x_high), (y_low, y_high) = parity_weights(place_ref)
    halo, rise = {}, {}

    def at_rows(px, py):
        return pl.ds((px * 4 + py) * NODES, NODES)

    def put(px, py, src):
        high[at_rows(px, py), :], low[at_rows(px, py), :] = split(src)

    for x in range(2):
        for y in range(2):
            put(x + 1, y + 1, v_ref[:, column(x, y)] * mask_ref[0:1, column(x, y)])
    for k in range(2):
        at = pl.ds(k * BZ, BZ)
        halo[k] = (blend(x_low, ra_ref[:, at], rb_ref[:, at]), blend(x_high, ra_ref[:, at], rb_ref[:, at]))
        put(0, k + 1, halo[k][0])
        put(3, k + 1, halo[k][1])
        rise[k] = (blend(y_low, ya_ref[:, at], yb_ref[:, at]), blend(y_high, ya_ref[:, at], yb_ref[:, at]))
        put(k + 1, 0, rise[k][0])
        put(k + 1, 3, rise[k][1])
    sq = jnp.zeros((NODES, BZ), F32)
    cross = jnp.zeros((NODES, BZ), F32)
    for x in range(2):
        for y in range(2):
            spots = [at_rows(x + dx, y + dy) for dx, dy in others(x, y)]
            tops = jnp.concatenate([high[rows, :] for rows in spots], axis=0)
            rests = jnp.concatenate([low[rows, :] for rows in spots], axis=0)
            full = jnp.dot(w_ref[x * 2 + y], tops, preferred_element_type=F32)
            half = jnp.dot(w_ref[x * 2 + y, 0 : 3 * NODES, :], rests, preferred_element_type=F32)
            at = column(x, y)
            total = spread(full[: 3 * NODES] + full[3 * NODES :] + half)
            o_ref[:, at] = total
            if last:
                v = v_ref[:, at]
                sq = sq + v * v
                cross = cross + v * (diag_ref[:, at] * v - maskc_ref[0:1, at] * total)
    if not last:
        return
    energy = jnp.zeros((NODES, BZ), F32)
    for x in range(2):
        for y in range(2):
            energy = energy + halo[y][x] * product(corner_ref[(1 - x) * 2 + y], rise[x][y])
    cross = cross - energy * (1.0 / c_ref[0:1, 0:1])
    put_moments(2, mom_ref, mom_out, sq, cross)


def sides(place, operands, last):
    shapes = [FIELD] + ([pltpu.VMEM((SENDERS, 128), F32)] if last else [])
    return pl.pallas_call(
        functools.partial(sides_kernel, last),
        name="sides",
        in_specs=in_specs(len(operands)),
        out_specs=[pl.BlockSpec(memory_space=pltpu.VMEM)] * len(shapes),
        out_shape=shapes,
        scratch_shapes=[pltpu.VMEM((16 * NODES, BZ), BF16), pltpu.VMEM((16 * NODES, BZ), BF16)],
        compiler_params=pltpu.CompilerParams(vmem_limit_bytes=16 << 20),
        cost_estimate=pl.CostEstimate(flops=15 * 10**8, transcendentals=0, bytes_accessed=2 * 10**6),
    )(place, *[vmem(x) for x in operands])


def corners_kernel(order, last, place_ref, sum_ref, v_ref, diag_ref, mask_ref, maskc_ref, ca_ref, cb_ref, corner_ref, *rest):
    rest = list(rest)
    mom_ref = rest.pop(0) if order and not last else None
    o_ref = rest.pop(0)
    x_pairs, y_pairs = parity_weights(place_ref)
    sq = jnp.zeros((NODES, BZ), F32)
    cross = jnp.zeros((NODES, BZ), F32)
    masked = [[], []]
    for y in range(2):
        line = [blend(y_pairs[y], ca_ref[:, pl.ds(k * BZ, BZ)], cb_ref[:, pl.ds(k * BZ, BZ)]) for k in range(2)]
        for x in range(2):
            at = column(x, y)
            total = sum_ref[:, at] + product(corner_ref[x * 2 + y], blend(x_pairs[x], line[0], line[1]))
            v = v_ref[:, at]
            new = diag_ref[:, at] * v - maskc_ref[0:1, at] * total
            o_ref[:, at] = new
            if not last:
                masked[x].append(new * mask_ref[0:1, at])
                sq = sq + v * v
                cross = cross + v * new
    if not last:
        store_edges(place_ref, masked, *rest[1:])
        put_moments(order, mom_ref, rest[0], sq, cross)


def corners(order, place, operands, last):
    shapes = [FIELD] + ([] if last else [pltpu.VMEM((8, 128), F32)] + [EDGE] * 4)
    return pl.pallas_call(
        functools.partial(corners_kernel, order, last),
        name="corners",
        in_specs=in_specs(len(operands)),
        out_specs=[pl.BlockSpec(memory_space=pltpu.VMEM)] * len(shapes),
        out_shape=shapes,
        compiler_params=pltpu.CompilerParams(vmem_limit_bytes=16 << 20),
        cost_estimate=pl.CostEstimate(flops=5 * 10**8, transcendentals=0, bytes_accessed=2 * 10**6),
    )(place, *[vmem(x) for x in operands])


def apply_stiffness(order, place, v, diag, mask, maskc, centre, edges, weights, corner, moments):
    last = order == 2
    ra, rb, ya, yb, ca, cb = exchange(place[1], *edges)
    operands = [v, mask, ra, rb, ya, yb, weights] + ([corner, diag, maskc, centre, moments] if last else [])
    part, *shared = sides(place, operands, last)
    operands = [part, v, diag, mask, maskc, ca, cb, corner]
    if last:
        return corners(order, place, operands, last)[0], shared[0], []
    new, moments, *edges = corners(order, place, operands + ([] if moments is None else [moments]), last)
    return new, moments, edges


def finish_kernel(mom_ref, c_ref, v0_ref, v1_ref, v2_ref, v3_ref, x_ref, r_ref):
    row = jnp.sum(mom_ref[...], axis=0, keepdims=True)
    lanes = lane_iota((1, 128))
    m = [jnp.sum(jnp.where(lanes == k, row, 0.0), keepdims=True) for k in range(6)]
    zero = jnp.zeros((1, 1), F32)
    one = jnp.ones((1, 1), F32)

    def inner(f, g):
        total = zero
        for i, a in enumerate(f):
            for j, b in enumerate(g):
                if a is not None and b is not None:
                    total = total + a * b * m[i + j]
        return total

    r = [one, None, None, None]
    p = [one, None, None, None]
    x = [None, None, None]
    norm = m[0]

    def plus(a, b):
        if a is None:
            return b
        return a if b is None else a + b

    for step in range(3):
        image = [plus(p[k], p[k - 1] if k else None) for k in range(4)]
        alpha = norm / inner(p, image)
        for k in range(3):
            if p[k] is not None:
                x[k] = plus(x[k], alpha * p[k])
        for k in range(4):
            if image[k] is not None:
                r[k] = plus(r[k], -(alpha * image[k]))
        if step < 2:
            new = inner(r, r)
            beta = new / norm
            p = [plus(r[k], None if p[k] is None else beta * p[k]) for k in range(4)]
            norm = new
    inverse = 1.0 / c_ref[0:1, 0:1]
    x = [value * inverse for value in x]
    for chunk in range(8):
        bx, by, zt = chunk // 4, chunk // 2 % 2, chunk % 2
        spot = bx * 4 + zt * 2 + by
        at = pl.ds(chunk * 128, 128)
        v0, v1, v2, v3 = v0_ref[:, at], v1_ref[:, at], v2_ref[:, at], v3_ref[:, at]
        x_ref[:, spot, :] = x[0] * v0 + x[1] * v1 + x[2] * v2
        r_ref[:, spot, :] = r[0] * v0 + r[1] * v1 + r[2] * v2 + r[3] * v3


def finish(moments, centre, fields):
    out = jax.ShapeDtypeStruct((NODES, 8, 128), F32)
    return pl.pallas_call(
        finish_kernel,
        name="finish",
        in_specs=[pl.BlockSpec(memory_space=pltpu.VMEM)] * 6,
        out_specs=[pl.BlockSpec(memory_space=pltpu.VMEM)] * 2,
        out_shape=[out, out],
        compiler_params=pltpu.CompilerParams(vmem_limit_bytes=16 << 20),
    )(moments, *[vmem(x) for x in (centre, *fields)])


def swap(axis, first):
    count = lax.axis_size(axis)
    return [(i, (i + 1 if (i - first) % 2 == 0 else i - 1) % count) for i in range(count)]


def odd_swap():
    slabs, grps = lax.axis_size("slab"), lax.axis_size("grp")
    pairs = []
    for s in range(slabs):
        for g in range(grps):
            if g in (0, grps - 1):
                pairs.append((s * grps + g, (s ^ 1) * grps + g))
            else:
                pairs.append((s * grps + g, s * grps + (g + 1 if g % 2 else g - 1)))
    return pairs


def exchange(grp, ea, eb, oa, ob):
    yb = lax.ppermute(ob, AXES, odd_swap())
    ra = lax.ppermute(ea, "slab", swap("slab", 0))
    rb = lax.ppermute(eb, "slab", swap("slab", 1))
    ya = lax.ppermute(oa, "grp", swap("grp", 0))
    up = grp % 2 == 0

    def line(upper):
        return jnp.concatenate([jnp.where(upper, r[:, BZ:], r[:, :BZ]) for r in (ra, rb)], axis=1)

    cb = lax.ppermute(line(jnp.logical_not(up)), AXES, odd_swap())
    ca = lax.ppermute(line(up), "grp", swap("grp", 0))
    return ra, rb, ya, yb, ca, cb


def on_device(samples, block_ids, tile_counts, occupied, coupling):
    slab, grp = lax.axis_index("slab"), lax.axis_index("grp")
    place = jnp.stack([slab, grp, lax.axis_size("slab"), lax.axis_size("grp")]).astype(jnp.int32)
    payload = splat(samples, tile_counts, block_ids)
    recv = lax.all_to_all(payload.reshape(SENDERS, 1, ROWS * 128), AXES, split_axis=0, concat_axis=0, tiled=True)
    weights, corner, rowabs, mask = prepare(coupling, occupied)
    v, diag, maskc, centre, *edges = assemble(place, recv.reshape(SENDERS * ROWS, 128), mask, rowabs)
    fields = [v]
    moments = None
    for order in range(3):
        v, moments, edges = apply_stiffness(
            order, place, v, diag, mask, maskc, centre, edges, weights, corner, moments
        )
        fields.append(v)
    shared = lax.all_to_all(moments.reshape(SENDERS, 1, 128), AXES, split_axis=0, concat_axis=0, tiled=True)
    outs = finish(shared.reshape(SENDERS, 128), centre, fields)

    def settle(out):
        out = out.reshape(NODES, 2, 2, 2, 128)
        return jnp.transpose(out, (0, 1, 3, 2, 4)).reshape(NODES, 2, 2, BZ)

    return settle(outs[0]), settle(outs[1])


def solution(mesh):
    placed = (P(AXES, None, None), P(AXES), P(AXES), P("slab", "grp", None), P())
    return jax.shard_map(
        on_device,
        mesh=mesh,
        in_specs=placed,
        out_specs=(P(None, "slab", "grp", None), P(None, "slab", "grp", None)),
        check_vma=False,
    )
```

```python
import functools

import jax
import jax.numpy as jnp
from jax import lax
from jax.experimental import pallas as pl
from jax.experimental.pallas import tpu as pltpu
from jax.sharding import PartitionSpec as P

AXES = ("slab", "grp")
F32 = jnp.float32
BF16 = jnp.bfloat16
N_COLS = 4
BZ = 256
NODES = 64
SENDERS = 128
CAP = 8
ROWS = CAP + 1


def lane_iota(shape):
    return lax.broadcasted_iota(jnp.int32, shape, len(shape) - 1)


def row_iota(shape):
    return lax.broadcasted_iota(jnp.int32, shape, 0)


def basis_of(pos):
    u = 4.0 * pos
    w = u - jnp.floor(u)
    back = w - 1.0
    low = back * back
    high = w * w
    turn = w * back
    mid = 1.0 - (turn + turn)
    smid = -(w + back)
    in0, in1, in2 = u < 1.0, u < 2.0, u < 3.0
    zero = jnp.zeros_like(u)

    def nodes(below, at, above):
        return [
            jnp.where(in0, at, jnp.where(in1, below, zero)),
            jnp.where(in0, above, jnp.where(in1, at, jnp.where(in2, below, zero))),
            jnp.where(in0, zero, jnp.where(in1, above, jnp.where(in2, at, below))),
            jnp.where(in1, zero, jnp.where(in2, above, at)),
        ]

    return nodes(low, mid, high), nodes(back, smid, w)


def splat_kernel(samp_ref, cnt_hbm, ids_hbm, out_ref, held, sems, cnt_ref, ids_ref, small_sems, flip, basis, acc, stats):
    groups = out_ref.shape[0]

    def fetch(g):
        return pltpu.make_async_copy(samp_ref.at[:, pl.ds(g * 128, 128), :], held.at[g], sems.at[g])

    def turn(g):
        for k in range(6):
            flip[k] = held[g, k].T

    def evaluate(g):
        counts = cnt_ref[pl.ds(g, 1), :]
        for group in range(16):
            rows = pl.ds(group * 8, 8)
            live = row_iota((8, 128)) + group * 8 < counts
            n0 = jnp.where(live, flip[3, rows, :], 0.0)
            n1 = jnp.where(live, flip[4, rows, :], 0.0)
            n2 = jnp.where(live, flip[5, rows, :], 0.0)
            eighth = jnp.where(live, 0.125, 0.0)
            val, slo = basis_of(flip[0, rows, :])
            for i in range(4):
                basis[i, rows, :] = slo[i] * n0
                basis[4 + i, rows, :] = val[i] * n1
                basis[8 + i, rows, :] = val[i] * n2
                basis[12 + i, rows, :] = val[i] * eighth
            for d in (1, 2):
                val, slo = basis_of(flip[d, rows, :])
                for i in range(4):
                    basis[8 + 8 * d + i, rows, :] = val[i]
                    basis[12 + 8 * d + i, rows, :] = slo[i]

    def accumulate(i, js):
        rhs_sums, dens_sums = {}, {}
        for group in range(16):
            rows = pl.ds(group * 8, 8)
            a = basis[i, rows, :]
            b = basis[4 + i, rows, :]
            c = basis[8 + i, rows, :]
            d = basis[12 + i, rows, :]
            v2 = [basis[24 + l, rows, :] for l in range(4)]
            s2 = [basis[28 + l, rows, :] for l in range(4)]
            for j in js:
                v1 = basis[16 + j, rows, :]
                s1 = basis[20 + j, rows, :]
                first = a * v1 + b * s1
                second = c * v1
                dens = d * v1
                for l in range(4):
                    at = j * 4 + l
                    rhs = first * v2[l] + second * s2[l]
                    den = dens * v2[l]
                    rhs_sums[at] = rhs if group == 0 else rhs_sums[at] + rhs
                    dens_sums[at] = den if group == 0 else dens_sums[at] + den
        for at in rhs_sums:
            acc[pl.ds((i * 16 + at) * 8, 8), :] = rhs_sums[at]
            acc[pl.ds((64 + i * 16 + at) * 8, 8), :] = dens_sums[at]

    def settle(g, real):
        total = acc[pl.ds(0, 128, stride=8), :]
        for s in range(1, 8):
            total = total + acc[pl.ds(s, 128, stride=8), :]
        square = total[:64] * total[:64]
        weighted = total[64:] * square
        part, wpart = square[:8], weighted[:8]
        for k in range(1, 8):
            part = part + square[8 * k : 8 * k + 8]
            wpart = wpart + weighted[8 * k : 8 * k + 8]
        stats[0] = stats[0] + jnp.where(real, part, 0.0)
        stats[1] = stats[1] + jnp.where(real, wpart, 0.0)
        by_tile = total.T
        for d in range(16):
            out_ref[g, pl.ds(ROWS * d, 8), :] = by_tile[8 * d : 8 * d + 8]

    counts_copy = pltpu.make_async_copy(cnt_hbm, cnt_ref, small_sems.at[0])
    ids_copy = pltpu.make_async_copy(ids_hbm, ids_ref, small_sems.at[1])
    counts_copy.start()
    for g in range(groups):
        fetch(g).start()
    ids_copy.start()
    stats[...] = jnp.zeros_like(stats)
    acc[...] = jnp.zeros_like(acc)
    counts_copy.wait()
    fetch(0).wait()
    turn(0)

    def advance(g, carry):
        following = jnp.minimum(g + 1, groups - 1)

        @pl.when(g + 1 < groups)
        def _():
            fetch(following).wait()

        settle(jnp.maximum(g - 1, 0), g > 0)
        evaluate(g)
        turn(following)
        for i in range(4):
            for js in ((0, 1), (2, 3)):
                accumulate(i, js)
        return carry

    lax.fori_loop(0, groups, advance, 0)
    settle(groups - 1, True)
    ids_copy.wait()
    ids = ids_ref[...]
    local = ((ids >> 14) & 1) * 512 + ((ids >> 8) & 1) * 256 + (ids & 255)
    local = local.astype(F32)
    sum0 = jnp.sum(stats[0], keepdims=True)
    sum1 = jnp.sum(stats[1], keepdims=True)
    lanes = lane_iota((1, 128))
    both = jnp.where(lanes % 2 == 0, sum0, sum1)
    for g in range(groups):
        for d in range(16):
            row = jnp.where(lanes // 8 == d, local[g : g + 1], both)
            out_ref[g, pl.ds(ROWS * d + CAP, 1), :] = row


def splat(samples, counts, ids):
    tiles = samples.shape[0]
    groups = tiles // 128
    return pl.pallas_call(
        splat_kernel,
        name="splat",
        in_specs=[pl.BlockSpec(memory_space=pltpu.HBM)] * 3,
        out_specs=pl.BlockSpec(memory_space=pltpu.VMEM),
        out_shape=pltpu.VMEM((groups, 16 * ROWS, 128), F32),
        scratch_shapes=[
            pltpu.VMEM((groups, 6, 128, 128), F32),
            pltpu.SemaphoreType.DMA((groups,)),
            pltpu.VMEM((groups, 128), jnp.int32),
            pltpu.VMEM((groups, 128), jnp.int32),
            pltpu.SemaphoreType.DMA((2,)),
            pltpu.VMEM((6, 128, 128), F32),
            pltpu.VMEM((32, 128, 128), F32),
            pltpu.VMEM((1024, 128), F32),
            pltpu.VMEM((2, 8, 128), F32),
        ],
        compiler_params=pltpu.CompilerParams(vmem_limit_bytes=24 << 20),
    )(hbm(jnp.transpose(samples, (1, 0, 2))), hbm(counts.reshape(groups, 128)), hbm(ids.reshape(groups, 128)))


def hbm(x):
    return pltpu.with_memory_space_constraint(x, pltpu.HBM)


def vmem(x):
    return pltpu.with_memory_space_constraint(x, pltpu.VMEM)


def parity_weights(place_ref):
    slab, grp = place_ref[0], place_ref[1]
    slabs, grps = place_ref[2], place_ref[3]

    def pick(cond):
        return jnp.where(cond, 1.0, 0.0).astype(F32)

    def sides(at, count):
        odd = at % 2 == 1
        low = (pick(odd), pick(jnp.logical_and(jnp.logical_not(odd), at > 0)))
        high = (pick(jnp.logical_not(odd)), pick(jnp.logical_and(odd, at < count - 1)))
        return low, high

    return sides(slab, slabs), sides(grp, grps)


def blend(pair, a, b):
    return a * pair[0] + b * pair[1]


def column(x, y):
    return pl.ds((x * 2 + y) * BZ, BZ)


def store_edges(place_ref, masked, ea_ref, eb_ref, oa_ref, ob_ref):
    up_slab = place_ref[0] % 2 == 0
    up_grp = place_ref[1] % 2 == 0
    for k in range(2):
        at = pl.ds(k * BZ, BZ)
        ea_ref[:, at] = jnp.where(up_slab, masked[1][k], masked[0][k])
        eb_ref[:, at] = jnp.where(up_slab, masked[0][k], masked[1][k])
        oa_ref[:, at] = jnp.where(up_grp, masked[k][1], masked[k][0])
        ob_ref[:, at] = jnp.where(up_grp, masked[k][0], masked[k][1])


def spread(part):
    lanes = lane_iota((NODES, BZ))
    before = jnp.where(lanes == 0, 0.0, pltpu.roll(part[:NODES], 1, 1))
    after = jnp.where(lanes == BZ - 1, 0.0, pltpu.roll(part[2 * NODES :], BZ - 1, 1))
    return part[NODES : 2 * NODES] + before + after


def split(src):
    top = src.astype(BF16)
    return top, (src - top.astype(F32)).astype(BF16)


def prepare_kernel(coupling_ref, occ_ref, w_ref, corner_ref, rowabs_ref, mask_ref):
    total = jnp.zeros((NODES, NODES), F32)
    high, low = {}, {}
    for dz in range(3):
        rows = pl.ds(dz * NODES, NODES)
        for dx in range(3):
            for dy in range(3):
                k = (dx * 3 + dy) * 3 + dz
                coupled = 0.5 * (coupling_ref[k] + coupling_ref[26 - k].T)
                total = total + jnp.abs(coupled)
                high[dx, dy], low[dx, dy] = split(coupled)
            w_ref[dx, rows, :] = jnp.concatenate([high[dx, dy] for dy in range(3)], axis=1)
            w_ref[dx, pl.ds((3 + dz) * NODES, NODES), :] = jnp.concatenate([low[dx, dy] for dy in range(3)], axis=1)
        for x in range(2):
            for y in range(2):
                at = (2 * x, 2 * y)
                corner_ref[x * 2 + y, rows, :] = jnp.concatenate([high[at], low[at], high[at]], axis=1)
    rowabs_ref[...] = jnp.broadcast_to(jnp.sum(total, axis=1, keepdims=True), (NODES, 128))
    for x in range(2):
        for y in range(2):
            mask_ref[:, column(x, y)] = jnp.broadcast_to(occ_ref[x, y : y + 1, :].astype(F32), (8, BZ))


def prepare(coupling, occupied):
    return pl.pallas_call(
        prepare_kernel,
        name="prepare",
        in_specs=[pl.BlockSpec(memory_space=pltpu.VMEM)] * 2,
        out_specs=[pl.BlockSpec(memory_space=pltpu.VMEM)] * 4,
        out_shape=[
            pltpu.VMEM((3, 6 * NODES, 3 * NODES), BF16),
            pltpu.VMEM((4, 3 * NODES, 3 * NODES), BF16),
            pltpu.VMEM((NODES, 128), F32),
            pltpu.VMEM((8, N_COLS * BZ), F32),
        ],
        compiler_params=pltpu.CompilerParams(vmem_limit_bytes=12 << 20),
        cost_estimate=pl.CostEstimate(flops=10**7, transcendentals=0, bytes_accessed=4 * 10**6),
    )(coupling, occupied)


def assemble_kernel(place_ref, recv_ref, mask_ref, rowabs_ref, v_ref, diag_ref, maskc_ref, c_ref,
                    ea_ref, eb_ref, oa_ref, ob_ref, turned):
    seat = place_ref[1] % 16
    turned[...] = recv_ref[pl.ds(CAP, SENDERS, stride=ROWS), :].T
    where = turned[pl.ds(pl.multiple_of(seat * 8, 8), 8), :].astype(jnp.int32)
    other = lax.rem(seat + 1, 16)
    sums = turned[pl.ds(pl.multiple_of(other * 8, 8), 8), :]
    sum0 = jnp.sum(sums[0:1, :], keepdims=True)
    sum1 = jnp.sum(sums[1:2, :], keepdims=True)
    rowabs = rowabs_ref[...]
    mean = jnp.sum(rowabs[:, 0:1], keepdims=True) * (1.0 / NODES)
    centre = mean + 0.5 + 4.0 * (sum1 / sum0)
    inverse = 1.0 / centre
    c_ref[...] = jnp.broadcast_to(centre, (8, 128))
    tiles = []
    for c in range(CAP):
        block = recv_ref[pl.ds(c, SENDERS, stride=ROWS), :]
        high = block.astype(BF16)
        low = (block - high.astype(F32)).astype(BF16)
        tiles.append(jnp.concatenate([high, low], axis=1))
    table = jnp.concatenate(tiles, axis=0)
    masked = []
    for x in range(2):
        masked.append([])
        for y in range(2):
            picks = []
            for c in range(CAP):
                hit = row_iota((BZ, SENDERS)) + (x * 2 + y) * BZ == where[c : c + 1, :]
                picks.append(hit.astype(F32).astype(BF16))
            pick = jnp.concatenate(picks, axis=1)
            both = jnp.dot(pick, table, preferred_element_type=F32)
            ordered = (both[:, :128] + both[:, 128:]).T
            rhs = ordered[:NODES]
            dens = ordered[NODES:]
            mask = mask_ref[0:1, column(x, y)]
            v_ref[:, column(x, y)] = rhs
            diag = rowabs[:, 0:1] + 0.5 + 4.0 * dens
            diag_ref[:, column(x, y)] = (diag - centre) * inverse
            maskc_ref[:, column(x, y)] = jnp.broadcast_to(mask * inverse, (8, BZ))
            masked[x].append(rhs * mask)
    store_edges(place_ref, masked, ea_ref, eb_ref, oa_ref, ob_ref)


FIELD = pltpu.VMEM((NODES, N_COLS * BZ), F32)
EDGE = pltpu.VMEM((NODES, 2 * BZ), F32)


def in_specs(count):
    return [pl.BlockSpec(memory_space=pltpu.SMEM)] + [pl.BlockSpec(memory_space=pltpu.VMEM)] * count


def assemble(place, recv, mask, rowabs):
    return pl.pallas_call(
        assemble_kernel,
        name="assemble",
        in_specs=in_specs(3),
        out_specs=[pl.BlockSpec(memory_space=pltpu.VMEM)] * 8,
        out_shape=[FIELD, FIELD, pltpu.VMEM((8, N_COLS * BZ), F32), pltpu.VMEM((8, 128), F32), EDGE, EDGE, EDGE, EDGE],
        scratch_shapes=[pltpu.VMEM((128, 128), F32)],
        compiler_params=pltpu.CompilerParams(vmem_limit_bytes=16 << 20),
    )(place, vmem(recv), vmem(mask), vmem(rowabs))


def product(weights, source):
    high, low = split(source)
    stacked = jnp.concatenate([high, high, low], axis=0)
    return spread(jnp.dot(weights, stacked, preferred_element_type=F32))


def put_moments(order, mom_ref, mom_out, sq, cross):
    sq = jnp.sum(sq, keepdims=True)
    cross = jnp.sum(cross, keepdims=True)
    spot = lane_iota((1, 128))
    before = jnp.zeros((1, 128), F32) if mom_ref is None else mom_ref[0:1, :]
    mom = jnp.where(spot == 2 * order, sq, jnp.where(spot == 2 * order + 1, cross, before))
    mom_out[...] = jnp.broadcast_to(mom, mom_out.shape)


def sides_kernel(last, place_ref, v_ref, mask_ref, ra_ref, rb_ref, ya_ref, yb_ref, w_ref, *rest):
    if last:
        corner_ref, diag_ref, maskc_ref, c_ref, mom_ref, o_ref, mom_out, high, low = rest
    else:
        o_ref, high, low = rest
    (x_low, x_high), (y_low, y_high) = parity_weights(place_ref)
    halo, rise = {}, {}

    def at_rows(px, py):
        return pl.ds((px * 4 + py) * NODES, NODES)

    def put(px, py, src):
        high[at_rows(px, py), :], low[at_rows(px, py), :] = split(src)

    for x in range(2):
        for y in range(2):
            put(x + 1, y + 1, v_ref[:, column(x, y)] * mask_ref[0:1, column(x, y)])
    for k in range(2):
        at = pl.ds(k * BZ, BZ)
        halo[k] = (blend(x_low, ra_ref[:, at], rb_ref[:, at]), blend(x_high, ra_ref[:, at], rb_ref[:, at]))
        put(0, k + 1, halo[k][0])
        put(3, k + 1, halo[k][1])
        rise[k] = (blend(y_low, ya_ref[:, at], yb_ref[:, at]), blend(y_high, ya_ref[:, at], yb_ref[:, at]))
        put(k + 1, 0, rise[k][0])
        put(k + 1, 3, rise[k][1])
    nothing = jnp.zeros((NODES, BZ), BF16)
    for px in (0, 3):
        for py in (0, 3):
            high[at_rows(px, py), :] = nothing
            low[at_rows(px, py), :] = nothing
    sq = jnp.zeros((NODES, BZ), F32)
    cross = jnp.zeros((NODES, BZ), F32)
    for x in range(2):
        for y in range(2):
            full = jnp.zeros((6 * NODES, BZ), F32)
            half = jnp.zeros((3 * NODES, BZ), F32)
            for dx in range(3):
                rows = pl.ds(((x + dx) * 4 + y) * NODES, 3 * NODES)
                full = full + jnp.dot(w_ref[dx], high[rows, :], preferred_element_type=F32)
                half = half + jnp.dot(w_ref[dx, 0 : 3 * NODES, :], low[rows, :], preferred_element_type=F32)
            at = column(x, y)
            total = spread(full[: 3 * NODES] + full[3 * NODES :] + half)
            o_ref[:, at] = total
            if last:
                v = v_ref[:, at]
                sq = sq + v * v
                cross = cross + v * (diag_ref[:, at] * v - maskc_ref[0:1, at] * total)
    if not last:
        return
    energy = jnp.zeros((NODES, BZ), F32)
    for x in range(2):
        for y in range(2):
            energy = energy + halo[y][x] * product(corner_ref[(1 - x) * 2 + y], rise[x][y])
    cross = cross - energy * (1.0 / c_ref[0:1, 0:1])
    put_moments(2, mom_ref, mom_out, sq, cross)


def sides(place, operands, last):
    shapes = [FIELD] + ([pltpu.VMEM((SENDERS, 128), F32)] if last else [])
    return pl.pallas_call(
        functools.partial(sides_kernel, last),
        name="sides",
        in_specs=in_specs(len(operands)),
        out_specs=[pl.BlockSpec(memory_space=pltpu.VMEM)] * len(shapes),
        out_shape=shapes,
        scratch_shapes=[pltpu.VMEM((16 * NODES, BZ), BF16), pltpu.VMEM((16 * NODES, BZ), BF16)],
        compiler_params=pltpu.CompilerParams(vmem_limit_bytes=16 << 20),
        cost_estimate=pl.CostEstimate(flops=15 * 10**8, transcendentals=0, bytes_accessed=2 * 10**6),
    )(place, *[vmem(x) for x in operands])


def corners_kernel(order, last, place_ref, sum_ref, v_ref, diag_ref, mask_ref, maskc_ref, ca_ref, cb_ref, corner_ref, *rest):
    rest = list(rest)
    mom_ref = rest.pop(0) if order and not last else None
    o_ref = rest.pop(0)
    x_pairs, y_pairs = parity_weights(place_ref)
    sq = jnp.zeros((NODES, BZ), F32)
    cross = jnp.zeros((NODES, BZ), F32)
    masked = [[], []]
    for y in range(2):
        line = [blend(y_pairs[y], ca_ref[:, pl.ds(k * BZ, BZ)], cb_ref[:, pl.ds(k * BZ, BZ)]) for k in range(2)]
        for x in range(2):
            at = column(x, y)
            total = sum_ref[:, at] + product(corner_ref[x * 2 + y], blend(x_pairs[x], line[0], line[1]))
            v = v_ref[:, at]
            new = diag_ref[:, at] * v - maskc_ref[0:1, at] * total
            o_ref[:, at] = new
            if not last:
                masked[x].append(new * mask_ref[0:1, at])
                sq = sq + v * v
                cross = cross + v * new
    if not last:
        store_edges(place_ref, masked, *rest[1:])
        put_moments(order, mom_ref, rest[0], sq, cross)


def corners(order, place, operands, last):
    shapes = [FIELD] + ([] if last else [pltpu.VMEM((8, 128), F32)] + [EDGE] * 4)
    return pl.pallas_call(
        functools.partial(corners_kernel, order, last),
        name="corners",
        in_specs=in_specs(len(operands)),
        out_specs=[pl.BlockSpec(memory_space=pltpu.VMEM)] * len(shapes),
        out_shape=shapes,
        compiler_params=pltpu.CompilerParams(vmem_limit_bytes=16 << 20),
        cost_estimate=pl.CostEstimate(flops=5 * 10**8, transcendentals=0, bytes_accessed=2 * 10**6),
    )(place, *[vmem(x) for x in operands])


def apply_stiffness(order, place, v, diag, mask, maskc, centre, edges, weights, corner, moments):
    last = order == 2
    ra, rb, ya, yb, ca, cb = exchange(place[1], *edges)
    operands = [v, mask, ra, rb, ya, yb, weights] + ([corner, diag, maskc, centre, moments] if last else [])
    part, *shared = sides(place, operands, last)
    operands = [part, v, diag, mask, maskc, ca, cb, corner]
    if last:
        return corners(order, place, operands, last)[0], shared[0], []
    new, moments, *edges = corners(order, place, operands + ([] if moments is None else [moments]), last)
    return new, moments, edges


def finish_kernel(mom_ref, c_ref, v0_ref, v1_ref, v2_ref, v3_ref, x_ref, r_ref):
    row = jnp.sum(mom_ref[...], axis=0, keepdims=True)
    lanes = lane_iota((1, 128))
    m = [jnp.sum(jnp.where(lanes == k, row, 0.0), keepdims=True) for k in range(6)]
    zero = jnp.zeros((1, 1), F32)
    one = jnp.ones((1, 1), F32)

    def inner(f, g):
        total = zero
        for i, a in enumerate(f):
            for j, b in enumerate(g):
                if a is not None and b is not None:
                    total = total + a * b * m[i + j]
        return total

    r = [one, None, None, None]
    p = [one, None, None, None]
    x = [None, None, None]
    norm = m[0]

    def plus(a, b):
        if a is None:
            return b
        return a if b is None else a + b

    for step in range(3):
        image = [plus(p[k], p[k - 1] if k else None) for k in range(4)]
        alpha = norm / inner(p, image)
        for k in range(3):
            if p[k] is not None:
                x[k] = plus(x[k], alpha * p[k])
        for k in range(4):
            if image[k] is not None:
                r[k] = plus(r[k], -(alpha * image[k]))
        if step < 2:
            new = inner(r, r)
            beta = new / norm
            p = [plus(r[k], None if p[k] is None else beta * p[k]) for k in range(4)]
            norm = new
    inverse = 1.0 / c_ref[0:1, 0:1]
    x = [value * inverse for value in x]
    for chunk in range(8):
        bx, by, zt = chunk // 4, chunk // 2 % 2, chunk % 2
        spot = bx * 4 + zt * 2 + by
        at = pl.ds(chunk * 128, 128)
        v0, v1, v2, v3 = v0_ref[:, at], v1_ref[:, at], v2_ref[:, at], v3_ref[:, at]
        x_ref[:, spot, :] = x[0] * v0 + x[1] * v1 + x[2] * v2
        r_ref[:, spot, :] = r[0] * v0 + r[1] * v1 + r[2] * v2 + r[3] * v3


def finish(moments, centre, fields):
    out = jax.ShapeDtypeStruct((NODES, 8, 128), F32)
    return pl.pallas_call(
        finish_kernel,
        name="finish",
        in_specs=[pl.BlockSpec(memory_space=pltpu.VMEM)] * 6,
        out_specs=[pl.BlockSpec(memory_space=pltpu.VMEM)] * 2,
        out_shape=[out, out],
        compiler_params=pltpu.CompilerParams(vmem_limit_bytes=16 << 20),
    )(moments, *[vmem(x) for x in (centre, *fields)])


def swap(axis, first):
    count = lax.axis_size(axis)
    return [(i, (i + 1 if (i - first) % 2 == 0 else i - 1) % count) for i in range(count)]


def odd_swap():
    slabs, grps = lax.axis_size("slab"), lax.axis_size("grp")
    pairs = []
    for s in range(slabs):
        for g in range(grps):
            if g in (0, grps - 1):
                pairs.append((s * grps + g, (s ^ 1) * grps + g))
            else:
                pairs.append((s * grps + g, s * grps + (g + 1 if g % 2 else g - 1)))
    return pairs


def exchange(grp, ea, eb, oa, ob):
    yb = lax.ppermute(ob, AXES, odd_swap())
    ra = lax.ppermute(ea, "slab", swap("slab", 0))
    rb = lax.ppermute(eb, "slab", swap("slab", 1))
    ya = lax.ppermute(oa, "grp", swap("grp", 0))
    up = grp % 2 == 0

    def line(upper):
        return jnp.concatenate([jnp.where(upper, r[:, BZ:], r[:, :BZ]) for r in (ra, rb)], axis=1)

    cb = lax.ppermute(line(jnp.logical_not(up)), AXES, odd_swap())
    ca = lax.ppermute(line(up), "grp", swap("grp", 0))
    return ra, rb, ya, yb, ca, cb


def on_device(samples, block_ids, tile_counts, occupied, coupling):
    slab, grp = lax.axis_index("slab"), lax.axis_index("grp")
    place = jnp.stack([slab, grp, lax.axis_size("slab"), lax.axis_size("grp")]).astype(jnp.int32)
    payload = splat(samples, tile_counts, block_ids)
    recv = lax.all_to_all(payload.reshape(SENDERS, 1, ROWS * 128), AXES, split_axis=0, concat_axis=0, tiled=True)
    weights, corner, rowabs, mask = prepare(coupling, occupied)
    v, diag, maskc, centre, *edges = assemble(place, recv.reshape(SENDERS * ROWS, 128), mask, rowabs)
    fields = [v]
    moments = None
    for order in range(3):
        v, moments, edges = apply_stiffness(
            order, place, v, diag, mask, maskc, centre, edges, weights, corner, moments
        )
        fields.append(v)
    shared = lax.all_to_all(moments.reshape(SENDERS, 1, 128), AXES, split_axis=0, concat_axis=0, tiled=True)
    outs = finish(shared.reshape(SENDERS, 128), centre, fields)

    def settle(out):
        out = out.reshape(NODES, 2, 2, 2, 128)
        return jnp.transpose(out, (0, 1, 3, 2, 4)).reshape(NODES, 2, 2, BZ)

    return settle(outs[0]), settle(outs[1])


def solution(mesh):
    placed = (P(AXES, None, None), P(AXES), P(AXES), P("slab", "grp", None), P())
    return jax.shard_map(
        on_device,
        mesh=mesh,
        in_specs=placed,
        out_specs=(P(None, "slab", "grp", None), P(None, "slab", "grp", None)),
        check_vma=False,
    )
```

```python
import functools

import jax
import jax.numpy as jnp
from jax import lax
from jax.experimental import pallas as pl
from jax.experimental.pallas import tpu as pltpu
from jax.sharding import PartitionSpec as P

AXES = ("slab", "grp")
F32 = jnp.float32
BF16 = jnp.bfloat16
N_COLS = 4
BZ = 256
NODES = 64
SENDERS = 128
CAP = 8
ROWS = CAP + 1


def lane_iota(shape):
    return lax.broadcasted_iota(jnp.int32, shape, len(shape) - 1)


def row_iota(shape):
    return lax.broadcasted_iota(jnp.int32, shape, 0)


def basis_of(pos):
    u = 4.0 * pos
    w = u - jnp.floor(u)
    back = w - 1.0
    low = back * back
    high = w * w
    turn = w * back
    mid = 1.0 - (turn + turn)
    smid = -(w + back)
    in0, in1, in2 = u < 1.0, u < 2.0, u < 3.0
    zero = jnp.zeros_like(u)

    def nodes(below, at, above):
        return [
            jnp.where(in0, at, jnp.where(in1, below, zero)),
            jnp.where(in0, above, jnp.where(in1, at, jnp.where(in2, below, zero))),
            jnp.where(in0, zero, jnp.where(in1, above, jnp.where(in2, at, below))),
            jnp.where(in1, zero, jnp.where(in2, above, at)),
        ]

    return nodes(low, mid, high), nodes(back, smid, w)


def splat_kernel(samp_ref, cnt_hbm, ids_hbm, out_ref, held, sems, cnt_ref, ids_ref, small_sems, flip, basis, acc, stats):
    groups = out_ref.shape[0]

    def fetch(g):
        return pltpu.make_async_copy(samp_ref.at[:, pl.ds(g * 128, 128), :], held.at[g], sems.at[g])

    def turn(g, k):
        flip[k] = held[g, k].T

    def evaluate(g):
        counts = cnt_ref[pl.ds(g, 1), :]
        for group in range(16):
            rows = pl.ds(group * 8, 8)
            live = row_iota((8, 128)) + group * 8 < counts
            n0 = jnp.where(live, flip[3, rows, :], 0.0)
            n1 = jnp.where(live, flip[4, rows, :], 0.0)
            n2 = jnp.where(live, flip[5, rows, :], 0.0)
            eighth = jnp.where(live, 0.125, 0.0)
            val, slo = basis_of(flip[0, rows, :])
            for i in range(4):
                basis[i, rows, :] = slo[i] * n0
                basis[4 + i, rows, :] = val[i] * n1
                basis[8 + i, rows, :] = val[i] * n2
                basis[12 + i, rows, :] = val[i] * eighth
            for d in (1, 2):
                val, slo = basis_of(flip[d, rows, :])
                for i in range(4):
                    basis[8 + 8 * d + i, rows, :] = val[i]
                    basis[12 + 8 * d + i, rows, :] = slo[i]

    def accumulate(block):
        i = block
        rhs_sums, dens_sums = {}, {}
        for group in range(16):
            rows = pl.ds(group * 8, 8)
            a = basis[i, rows, :]
            b = basis[4 + i, rows, :]
            c = basis[8 + i, rows, :]
            d = basis[12 + i, rows, :]
            v2 = [basis[24 + l, rows, :] for l in range(4)]
            s2 = [basis[28 + l, rows, :] for l in range(4)]
            for j in range(4):
                v1 = basis[16 + j, rows, :]
                s1 = basis[20 + j, rows, :]
                first = a * v1 + b * s1
                second = c * v1
                dens = d * v1
                for l in range(4):
                    at = j * 4 + l
                    rhs = first * v2[l] + second * s2[l]
                    den = dens * v2[l]
                    rhs_sums[at] = rhs if group == 0 else rhs_sums[at] + rhs
                    dens_sums[at] = den if group == 0 else dens_sums[at] + den
        for at in range(16):
            acc[pl.ds(pl.multiple_of(block * 128, 128) + at * 8, 8), :] = rhs_sums[at]
            acc[pl.ds(pl.multiple_of(block * 128, 128) + 512 + at * 8, 8), :] = dens_sums[at]

    def settle(g, real):
        total = acc[pl.ds(0, 128, stride=8), :]
        for s in range(1, 8):
            total = total + acc[pl.ds(s, 128, stride=8), :]
        square = total[:64] * total[:64]
        weighted = total[64:] * square
        part, wpart = square[:8], weighted[:8]
        for k in range(1, 8):
            part = part + square[8 * k : 8 * k + 8]
            wpart = wpart + weighted[8 * k : 8 * k + 8]
        stats[0] = stats[0] + jnp.where(real, part, 0.0)
        stats[1] = stats[1] + jnp.where(real, wpart, 0.0)
        by_tile = total.T
        for d in range(16):
            out_ref[g, pl.ds(ROWS * d, 8), :] = by_tile[8 * d : 8 * d + 8]

    counts_copy = pltpu.make_async_copy(cnt_hbm, cnt_ref, small_sems.at[0])
    ids_copy = pltpu.make_async_copy(ids_hbm, ids_ref, small_sems.at[1])
    counts_copy.start()
    for g in range(groups):
        fetch(g).start()
    ids_copy.start()
    stats[...] = jnp.zeros_like(stats)
    acc[...] = jnp.zeros_like(acc)
    counts_copy.wait()
    fetch(0).wait()
    for k in range(6):
        turn(0, k)

    def advance(g, carry):
        following = jnp.minimum(g + 1, groups - 1)

        @pl.when(g + 1 < groups)
        def _():
            fetch(following).wait()

        settle(jnp.maximum(g - 1, 0), g > 0)
        evaluate(g)

        def block_sums(block, kept):
            turn(following, block)
            turn(following, 4 + block % 2)
            accumulate(block)
            return kept

        lax.fori_loop(0, 4, block_sums, 0)
        return carry

    lax.fori_loop(0, groups, advance, 0)
    settle(groups - 1, True)
    ids_copy.wait()
    ids = ids_ref[...]
    local = ((ids >> 14) & 1) * 512 + ((ids >> 8) & 1) * 256 + (ids & 255)
    local = local.astype(F32)
    sum0 = jnp.sum(stats[0], keepdims=True)
    sum1 = jnp.sum(stats[1], keepdims=True)
    lanes = lane_iota((1, 128))
    both = jnp.where(lanes % 2 == 0, sum0, sum1)
    for g in range(groups):
        for d in range(16):
            row = jnp.where(lanes // 8 == d, local[g : g + 1], both)
            out_ref[g, pl.ds(ROWS * d + CAP, 1), :] = row


def splat(samples, counts, ids):
    tiles = samples.shape[0]
    groups = tiles // 128
    return pl.pallas_call(
        splat_kernel,
        name="splat",
        in_specs=[pl.BlockSpec(memory_space=pltpu.HBM)] * 3,
        out_specs=pl.BlockSpec(memory_space=pltpu.VMEM),
        out_shape=pltpu.VMEM((groups, 16 * ROWS, 128), F32),
        scratch_shapes=[
            pltpu.VMEM((groups, 6, 128, 128), F32),
            pltpu.SemaphoreType.DMA((groups,)),
            pltpu.VMEM((groups, 128), jnp.int32),
            pltpu.VMEM((groups, 128), jnp.int32),
            pltpu.SemaphoreType.DMA((2,)),
            pltpu.VMEM((6, 128, 128), F32),
            pltpu.VMEM((32, 128, 128), F32),
            pltpu.VMEM((1024, 128), F32),
            pltpu.VMEM((2, 8, 128), F32),
        ],
        compiler_params=pltpu.CompilerParams(vmem_limit_bytes=24 << 20),
    )(hbm(jnp.transpose(samples, (1, 0, 2))), hbm(counts.reshape(groups, 128)), hbm(ids.reshape(groups, 128)))


def hbm(x):
    return pltpu.with_memory_space_constraint(x, pltpu.HBM)


def vmem(x):
    return pltpu.with_memory_space_constraint(x, pltpu.VMEM)


def parity_weights(place_ref):
    slab, grp = place_ref[0], place_ref[1]
    slabs, grps = place_ref[2], place_ref[3]

    def pick(cond):
        return jnp.where(cond, 1.0, 0.0).astype(F32)

    def sides(at, count):
        odd = at % 2 == 1
        low = (pick(odd), pick(jnp.logical_and(jnp.logical_not(odd), at > 0)))
        high = (pick(jnp.logical_not(odd)), pick(jnp.logical_and(odd, at < count - 1)))
        return low, high

    return sides(slab, slabs), sides(grp, grps)


def blend(pair, a, b):
    return a * pair[0] + b * pair[1]


def column(x, y):
    return pl.ds((x * 2 + y) * BZ, BZ)


def store_edges(place_ref, masked, ea_ref, eb_ref, oa_ref, ob_ref):
    up_slab = place_ref[0] % 2 == 0
    up_grp = place_ref[1] % 2 == 0
    for k in range(2):
        at = pl.ds(k * BZ, BZ)
        ea_ref[:, at] = jnp.where(up_slab, masked[1][k], masked[0][k])
        eb_ref[:, at] = jnp.where(up_slab, masked[0][k], masked[1][k])
        oa_ref[:, at] = jnp.where(up_grp, masked[k][1], masked[k][0])
        ob_ref[:, at] = jnp.where(up_grp, masked[k][0], masked[k][1])


def spread(part):
    lanes = lane_iota((NODES, BZ))
    before = jnp.where(lanes == 0, 0.0, pltpu.roll(part[:NODES], 1, 1))
    after = jnp.where(lanes == BZ - 1, 0.0, pltpu.roll(part[2 * NODES :], BZ - 1, 1))
    return part[NODES : 2 * NODES] + before + after


def split(src):
    top = src.astype(BF16)
    return top, (src - top.astype(F32)).astype(BF16)


def prepare_kernel(coupling_ref, occ_ref, w_ref, corner_ref, rowabs_ref, mask_ref):
    total = jnp.zeros((NODES, NODES), F32)
    high, low = {}, {}
    for dz in range(3):
        rows = pl.ds(dz * NODES, NODES)
        for dx in range(3):
            for dy in range(3):
                k = (dx * 3 + dy) * 3 + dz
                coupled = 0.5 * (coupling_ref[k] + coupling_ref[26 - k].T)
                total = total + jnp.abs(coupled)
                high[dx, dy], low[dx, dy] = split(coupled)
            w_ref[dx, rows, :] = jnp.concatenate([high[dx, dy] for dy in range(3)], axis=1)
            w_ref[dx, pl.ds((3 + dz) * NODES, NODES), :] = jnp.concatenate([low[dx, dy] for dy in range(3)], axis=1)
        for x in range(2):
            for y in range(2):
                at = (2 * x, 2 * y)
                corner_ref[x * 2 + y, rows, :] = jnp.concatenate([high[at], low[at], high[at]], axis=1)
    rowabs_ref[...] = jnp.broadcast_to(jnp.sum(total, axis=1, keepdims=True), (NODES, 128))
    for x in range(2):
        for y in range(2):
            mask_ref[:, column(x, y)] = jnp.broadcast_to(occ_ref[x, y : y + 1, :].astype(F32), (8, BZ))


def prepare(coupling, occupied):
    return pl.pallas_call(
        prepare_kernel,
        name="prepare",
        in_specs=[pl.BlockSpec(memory_space=pltpu.VMEM)] * 2,
        out_specs=[pl.BlockSpec(memory_space=pltpu.VMEM)] * 4,
        out_shape=[
            pltpu.VMEM((3, 6 * NODES, 3 * NODES), BF16),
            pltpu.VMEM((4, 3 * NODES, 3 * NODES), BF16),
            pltpu.VMEM((NODES, 128), F32),
            pltpu.VMEM((8, N_COLS * BZ), F32),
        ],
        compiler_params=pltpu.CompilerParams(vmem_limit_bytes=12 << 20),
        cost_estimate=pl.CostEstimate(flops=10**7, transcendentals=0, bytes_accessed=4 * 10**6),
    )(coupling, occupied)


def assemble_kernel(place_ref, recv_ref, mask_ref, rowabs_ref, v_ref, diag_ref, maskc_ref, c_ref,
                    ea_ref, eb_ref, oa_ref, ob_ref, turned):
    seat = place_ref[1] % 16
    turned[...] = recv_ref[pl.ds(CAP, SENDERS, stride=ROWS), :].T
    where = turned[pl.ds(pl.multiple_of(seat * 8, 8), 8), :].astype(jnp.int32)
    other = lax.rem(seat + 1, 16)
    sums = turned[pl.ds(pl.multiple_of(other * 8, 8), 8), :]
    sum0 = jnp.sum(sums[0:1, :], keepdims=True)
    sum1 = jnp.sum(sums[1:2, :], keepdims=True)
    rowabs = rowabs_ref[...]
    mean = jnp.sum(rowabs[:, 0:1], keepdims=True) * (1.0 / NODES)
    centre = mean + 0.5 + 4.0 * (sum1 / sum0)
    inverse = 1.0 / centre
    c_ref[...] = jnp.broadcast_to(centre, (8, 128))
    tiles = []
    for c in range(CAP):
        block = recv_ref[pl.ds(c, SENDERS, stride=ROWS), :]
        high = block.astype(BF16)
        low = (block - high.astype(F32)).astype(BF16)
        tiles.append(jnp.concatenate([high, low], axis=1))
    table = jnp.concatenate(tiles, axis=0)
    masked = []
    for x in range(2):
        masked.append([])
        for y in range(2):
            picks = []
            for c in range(CAP):
                hit = row_iota((BZ, SENDERS)) + (x * 2 + y) * BZ == where[c : c + 1, :]
                picks.append(hit.astype(F32).astype(BF16))
            pick = jnp.concatenate(picks, axis=1)
            both = jnp.dot(pick, table, preferred_element_type=F32)
            ordered = (both[:, :128] + both[:, 128:]).T
            rhs = ordered[:NODES]
            dens = ordered[NODES:]
            mask = mask_ref[0:1, column(x, y)]
            v_ref[:, column(x, y)] = rhs
            diag = rowabs[:, 0:1] + 0.5 + 4.0 * dens
            diag_ref[:, column(x, y)] = (diag - centre) * inverse
            maskc_ref[:, column(x, y)] = jnp.broadcast_to(mask * inverse, (8, BZ))
            masked[x].append(rhs * mask)
    store_edges(place_ref, masked, ea_ref, eb_ref, oa_ref, ob_ref)


FIELD = pltpu.VMEM((NODES, N_COLS * BZ), F32)
EDGE = pltpu.VMEM((NODES, 2 * BZ), F32)


def in_specs(count):
    return [pl.BlockSpec(memory_space=pltpu.SMEM)] + [pl.BlockSpec(memory_space=pltpu.VMEM)] * count


def assemble(place, recv, mask, rowabs):
    return pl.pallas_call(
        assemble_kernel,
        name="assemble",
        in_specs=in_specs(3),
        out_specs=[pl.BlockSpec(memory_space=pltpu.VMEM)] * 8,
        out_shape=[FIELD, FIELD, pltpu.VMEM((8, N_COLS * BZ), F32), pltpu.VMEM((8, 128), F32), EDGE, EDGE, EDGE, EDGE],
        scratch_shapes=[pltpu.VMEM((128, 128), F32)],
        compiler_params=pltpu.CompilerParams(vmem_limit_bytes=16 << 20),
    )(place, vmem(recv), vmem(mask), vmem(rowabs))


def product(weights, source):
    high, low = split(source)
    stacked = jnp.concatenate([high, high, low], axis=0)
    return spread(jnp.dot(weights, stacked, preferred_element_type=F32))


def put_moments(order, mom_ref, mom_out, sq, cross):
    sq = jnp.sum(sq, keepdims=True)
    cross = jnp.sum(cross, keepdims=True)
    spot = lane_iota((1, 128))
    before = jnp.zeros((1, 128), F32) if mom_ref is None else mom_ref[0:1, :]
    mom = jnp.where(spot == 2 * order, sq, jnp.where(spot == 2 * order + 1, cross, before))
    mom_out[...] = jnp.broadcast_to(mom, mom_out.shape)


def sides_kernel(last, place_ref, v_ref, mask_ref, ra_ref, rb_ref, ya_ref, yb_ref, w_ref, *rest):
    if last:
        corner_ref, diag_ref, maskc_ref, c_ref, mom_ref, o_ref, mom_out, high, low = rest
    else:
        o_ref, high, low = rest
    (x_low, x_high), (y_low, y_high) = parity_weights(place_ref)
    halo, rise = {}, {}

    def at_rows(px, py):
        return pl.ds((px * 4 + py) * NODES, NODES)

    def put(px, py, src):
        high[at_rows(px, py), :], low[at_rows(px, py), :] = split(src)

    for x in range(2):
        for y in range(2):
            put(x + 1, y + 1, v_ref[:, column(x, y)] * mask_ref[0:1, column(x, y)])
    for k in range(2):
        at = pl.ds(k * BZ, BZ)
        halo[k] = (blend(x_low, ra_ref[:, at], rb_ref[:, at]), blend(x_high, ra_ref[:, at], rb_ref[:, at]))
        put(0, k + 1, halo[k][0])
        put(3, k + 1, halo[k][1])
        rise[k] = (blend(y_low, ya_ref[:, at], yb_ref[:, at]), blend(y_high, ya_ref[:, at], yb_ref[:, at]))
        put(k + 1, 0, rise[k][0])
        put(k + 1, 3, rise[k][1])
    nothing = jnp.zeros((NODES, BZ), BF16)
    for px in (0, 3):
        for py in (0, 3):
            high[at_rows(px, py), :] = nothing
            low[at_rows(px, py), :] = nothing
    sq = jnp.zeros((NODES, BZ), F32)
    cross = jnp.zeros((NODES, BZ), F32)
    for x in range(2):
        for y in range(2):
            full = jnp.zeros((6 * NODES, BZ), F32)
            half = jnp.zeros((3 * NODES, BZ), F32)
            for dx in range(3):
                rows = pl.ds(((x + dx) * 4 + y) * NODES, 3 * NODES)
                full = full + jnp.dot(w_ref[dx], high[rows, :], preferred_element_type=F32)
                half = half + jnp.dot(w_ref[dx, 0 : 3 * NODES, :], low[rows, :], preferred_element_type=F32)
            at = column(x, y)
            total = spread(full[: 3 * NODES] + full[3 * NODES :] + half)
            o_ref[:, at] = total
            if last:
                v = v_ref[:, at]
                sq = sq + v * v
                cross = cross + v * (diag_ref[:, at] * v - maskc_ref[0:1, at] * total)
    if not last:
        return
    energy = jnp.zeros((NODES, BZ), F32)
    for x in range(2):
        for y in range(2):
            energy = energy + halo[y][x] * product(corner_ref[(1 - x) * 2 + y], rise[x][y])
    cross = cross - energy * (1.0 / c_ref[0:1, 0:1])
    put_moments(2, mom_ref, mom_out, sq, cross)


def sides(place, operands, last):
    shapes = [FIELD] + ([pltpu.VMEM((SENDERS, 128), F32)] if last else [])
    return pl.pallas_call(
        functools.partial(sides_kernel, last),
        name="sides",
        in_specs=in_specs(len(operands)),
        out_specs=[pl.BlockSpec(memory_space=pltpu.VMEM)] * len(shapes),
        out_shape=shapes,
        scratch_shapes=[pltpu.VMEM((16 * NODES, BZ), BF16), pltpu.VMEM((16 * NODES, BZ), BF16)],
        compiler_params=pltpu.CompilerParams(vmem_limit_bytes=16 << 20),
        cost_estimate=pl.CostEstimate(flops=15 * 10**8, transcendentals=0, bytes_accessed=2 * 10**6),
    )(place, *[vmem(x) for x in operands])


def corners_kernel(order, last, place_ref, sum_ref, v_ref, diag_ref, mask_ref, maskc_ref, ca_ref, cb_ref, corner_ref, *rest):
    rest = list(rest)
    mom_ref = rest.pop(0) if order and not last else None
    o_ref = rest.pop(0)
    x_pairs, y_pairs = parity_weights(place_ref)
    sq = jnp.zeros((NODES, BZ), F32)
    cross = jnp.zeros((NODES, BZ), F32)
    masked = [[], []]
    for y in range(2):
        line = [blend(y_pairs[y], ca_ref[:, pl.ds(k * BZ, BZ)], cb_ref[:, pl.ds(k * BZ, BZ)]) for k in range(2)]
        for x in range(2):
            at = column(x, y)
            total = sum_ref[:, at] + product(corner_ref[x * 2 + y], blend(x_pairs[x], line[0], line[1]))
            v = v_ref[:, at]
            new = diag_ref[:, at] * v - maskc_ref[0:1, at] * total
            o_ref[:, at] = new
            if not last:
                masked[x].append(new * mask_ref[0:1, at])
                sq = sq + v * v
                cross = cross + v * new
    if not last:
        store_edges(place_ref, masked, *rest[1:])
        put_moments(order, mom_ref, rest[0], sq, cross)


def corners(order, place, operands, last):
    shapes = [FIELD] + ([] if last else [pltpu.VMEM((8, 128), F32)] + [EDGE] * 4)
    return pl.pallas_call(
        functools.partial(corners_kernel, order, last),
        name="corners",
        in_specs=in_specs(len(operands)),
        out_specs=[pl.BlockSpec(memory_space=pltpu.VMEM)] * len(shapes),
        out_shape=shapes,
        compiler_params=pltpu.CompilerParams(vmem_limit_bytes=16 << 20),
        cost_estimate=pl.CostEstimate(flops=5 * 10**8, transcendentals=0, bytes_accessed=2 * 10**6),
    )(place, *[vmem(x) for x in operands])


def apply_stiffness(order, place, v, diag, mask, maskc, centre, edges, weights, corner, moments):
    last = order == 2
    ra, rb, ya, yb, ca, cb = exchange(place[1], *edges)
    operands = [v, mask, ra, rb, ya, yb, weights] + ([corner, diag, maskc, centre, moments] if last else [])
    part, *shared = sides(place, operands, last)
    operands = [part, v, diag, mask, maskc, ca, cb, corner]
    if last:
        return corners(order, place, operands, last)[0], shared[0], []
    new, moments, *edges = corners(order, place, operands + ([] if moments is None else [moments]), last)
    return new, moments, edges


def finish_kernel(mom_ref, c_ref, v0_ref, v1_ref, v2_ref, v3_ref, x_ref, r_ref):
    row = jnp.sum(mom_ref[...], axis=0, keepdims=True)
    lanes = lane_iota((1, 128))
    m = [jnp.sum(jnp.where(lanes == k, row, 0.0), keepdims=True) for k in range(6)]
    zero = jnp.zeros((1, 1), F32)
    one = jnp.ones((1, 1), F32)

    def inner(f, g):
        total = zero
        for i, a in enumerate(f):
            for j, b in enumerate(g):
                if a is not None and b is not None:
                    total = total + a * b * m[i + j]
        return total

    r = [one, None, None, None]
    p = [one, None, None, None]
    x = [None, None, None]
    norm = m[0]

    def plus(a, b):
        if a is None:
            return b
        return a if b is None else a + b

    for step in range(3):
        image = [plus(p[k], p[k - 1] if k else None) for k in range(4)]
        alpha = norm / inner(p, image)
        for k in range(3):
            if p[k] is not None:
                x[k] = plus(x[k], alpha * p[k])
        for k in range(4):
            if image[k] is not None:
                r[k] = plus(r[k], -(alpha * image[k]))
        if step < 2:
            new = inner(r, r)
            beta = new / norm
            p = [plus(r[k], None if p[k] is None else beta * p[k]) for k in range(4)]
            norm = new
    inverse = 1.0 / c_ref[0:1, 0:1]
    x = [value * inverse for value in x]
    for chunk in range(8):
        bx, by, zt = chunk // 4, chunk // 2 % 2, chunk % 2
        spot = bx * 4 + zt * 2 + by
        at = pl.ds(chunk * 128, 128)
        v0, v1, v2, v3 = v0_ref[:, at], v1_ref[:, at], v2_ref[:, at], v3_ref[:, at]
        x_ref[:, spot, :] = x[0] * v0 + x[1] * v1 + x[2] * v2
        r_ref[:, spot, :] = r[0] * v0 + r[1] * v1 + r[2] * v2 + r[3] * v3


def finish(moments, centre, fields):
    out = jax.ShapeDtypeStruct((NODES, 8, 128), F32)
    return pl.pallas_call(
        finish_kernel,
        name="finish",
        in_specs=[pl.BlockSpec(memory_space=pltpu.VMEM)] * 6,
        out_specs=[pl.BlockSpec(memory_space=pltpu.VMEM)] * 2,
        out_shape=[out, out],
        compiler_params=pltpu.CompilerParams(vmem_limit_bytes=16 << 20),
    )(moments, *[vmem(x) for x in (centre, *fields)])


def swap(axis, first):
    count = lax.axis_size(axis)
    return [(i, (i + 1 if (i - first) % 2 == 0 else i - 1) % count) for i in range(count)]


def odd_swap():
    slabs, grps = lax.axis_size("slab"), lax.axis_size("grp")
    pairs = []
    for s in range(slabs):
        for g in range(grps):
            if g in (0, grps - 1):
                pairs.append((s * grps + g, (s ^ 1) * grps + g))
            else:
                pairs.append((s * grps + g, s * grps + (g + 1 if g % 2 else g - 1)))
    return pairs


def exchange(grp, ea, eb, oa, ob):
    yb = lax.ppermute(ob, AXES, odd_swap())
    ra = lax.ppermute(ea, "slab", swap("slab", 0))
    rb = lax.ppermute(eb, "slab", swap("slab", 1))
    ya = lax.ppermute(oa, "grp", swap("grp", 0))
    up = grp % 2 == 0

    def line(upper):
        return jnp.concatenate([jnp.where(upper, r[:, BZ:], r[:, :BZ]) for r in (ra, rb)], axis=1)

    cb = lax.ppermute(line(jnp.logical_not(up)), AXES, odd_swap())
    ca = lax.ppermute(line(up), "grp", swap("grp", 0))
    return ra, rb, ya, yb, ca, cb


def on_device(samples, block_ids, tile_counts, occupied, coupling):
    slab, grp = lax.axis_index("slab"), lax.axis_index("grp")
    place = jnp.stack([slab, grp, lax.axis_size("slab"), lax.axis_size("grp")]).astype(jnp.int32)
    payload = splat(samples, tile_counts, block_ids)
    recv = lax.all_to_all(payload.reshape(SENDERS, 1, ROWS * 128), AXES, split_axis=0, concat_axis=0, tiled=True)
    weights, corner, rowabs, mask = prepare(coupling, occupied)
    v, diag, maskc, centre, *edges = assemble(place, recv.reshape(SENDERS * ROWS, 128), mask, rowabs)
    fields = [v]
    moments = None
    for order in range(3):
        v, moments, edges = apply_stiffness(
            order, place, v, diag, mask, maskc, centre, edges, weights, corner, moments
        )
        fields.append(v)
    shared = lax.all_to_all(moments.reshape(SENDERS, 1, 128), AXES, split_axis=0, concat_axis=0, tiled=True)
    outs = finish(shared.reshape(SENDERS, 128), centre, fields)

    def settle(out):
        out = out.reshape(NODES, 2, 2, 2, 128)
        return jnp.transpose(out, (0, 1, 3, 2, 4)).reshape(NODES, 2, 2, BZ)

    return settle(outs[0]), settle(outs[1])


def solution(mesh):
    placed = (P(AXES, None, None), P(AXES), P(AXES), P("slab", "grp", None), P())
    return jax.shard_map(
        on_device,
        mesh=mesh,
        in_specs=placed,
        out_specs=(P(None, "slab", "grp", None), P(None, "slab", "grp", None)),
        check_vma=False,
    )
```

```python
import functools

import jax
import jax.numpy as jnp
from jax import lax
from jax.experimental import pallas as pl
from jax.experimental.pallas import tpu as pltpu
from jax.sharding import PartitionSpec as P

AXES = ("slab", "grp")
F32 = jnp.float32
BF16 = jnp.bfloat16
N_COLS = 4
BZ = 256
NODES = 64
SENDERS = 128
CAP = 8
ROWS = CAP + 1


def lane_iota(shape):
    return lax.broadcasted_iota(jnp.int32, shape, len(shape) - 1)


def row_iota(shape):
    return lax.broadcasted_iota(jnp.int32, shape, 0)


def basis_of(pos):
    u = 4.0 * pos
    w = u - jnp.floor(u)
    back = w - 1.0
    low = back * back
    high = w * w
    turn = w * back
    mid = 1.0 - (turn + turn)
    smid = -(w + back)
    in0, in1, in2 = u < 1.0, u < 2.0, u < 3.0
    zero = jnp.zeros_like(u)

    def nodes(below, at, above):
        return [
            jnp.where(in0, at, jnp.where(in1, below, zero)),
            jnp.where(in0, above, jnp.where(in1, at, jnp.where(in2, below, zero))),
            jnp.where(in0, zero, jnp.where(in1, above, jnp.where(in2, at, below))),
            jnp.where(in1, zero, jnp.where(in2, above, at)),
        ]

    return nodes(low, mid, high), nodes(back, smid, w)


def splat_kernel(samp_ref, cnt_hbm, ids_hbm, out_ref, held, sems, cnt_ref, ids_ref, small_sems, flip, basis, acc, stats):
    groups = out_ref.shape[0]

    def fetch(g):
        return pltpu.make_async_copy(samp_ref.at[:, pl.ds(g * 128, 128), :], held.at[g], sems.at[g])

    def turn(g):
        for k in range(6):
            flip[k] = held[g, k].T

    def evaluate(g):
        counts = cnt_ref[pl.ds(g, 1), :]
        for group in range(16):
            rows = pl.ds(group * 8, 8)
            live = row_iota((8, 128)) + group * 8 < counts
            n0 = jnp.where(live, flip[3, rows, :], 0.0)
            n1 = jnp.where(live, flip[4, rows, :], 0.0)
            n2 = jnp.where(live, flip[5, rows, :], 0.0)
            eighth = jnp.where(live, 0.125, 0.0)
            val, slo = basis_of(flip[0, rows, :])
            for i in range(4):
                basis[i, rows, :] = slo[i] * n0
                basis[4 + i, rows, :] = val[i] * n1
                basis[8 + i, rows, :] = val[i] * n2
                basis[12 + i, rows, :] = val[i] * eighth
            for d in (1, 2):
                val, slo = basis_of(flip[d, rows, :])
                for i in range(4):
                    basis[8 + 8 * d + i, rows, :] = val[i]
                    basis[12 + 8 * d + i, rows, :] = slo[i]

    def accumulate(i, js):
        rhs_sums, dens_sums = {}, {}
        for group in range(16):
            rows = pl.ds(group * 8, 8)
            a = basis[i, rows, :]
            b = basis[4 + i, rows, :]
            c = basis[8 + i, rows, :]
            d = basis[12 + i, rows, :]
            v2 = [basis[24 + l, rows, :] for l in range(4)]
            s2 = [basis[28 + l, rows, :] for l in range(4)]
            for j in js:
                v1 = basis[16 + j, rows, :]
                s1 = basis[20 + j, rows, :]
                first = a * v1 + b * s1
                second = c * v1
                dens = d * v1
                for l in range(4):
                    at = j * 4 + l
                    rhs = first * v2[l] + second * s2[l]
                    den = dens * v2[l]
                    rhs_sums[at] = rhs if group == 0 else rhs_sums[at] + rhs
                    dens_sums[at] = den if group == 0 else dens_sums[at] + den
        for at in rhs_sums:
            acc[pl.ds((i * 16 + at) * 8, 8), :] = rhs_sums[at]
            acc[pl.ds((64 + i * 16 + at) * 8, 8), :] = dens_sums[at]

    def settle(g, real):
        total = acc[pl.ds(0, 128, stride=8), :]
        for s in range(1, 8):
            total = total + acc[pl.ds(s, 128, stride=8), :]
        square = total[:64] * total[:64]
        weighted = total[64:] * square
        part, wpart = square[:8], weighted[:8]
        for k in range(1, 8):
            part = part + square[8 * k : 8 * k + 8]
            wpart = wpart + weighted[8 * k : 8 * k + 8]
        stats[0] = stats[0] + jnp.where(real, part, 0.0)
        stats[1] = stats[1] + jnp.where(real, wpart, 0.0)
        by_tile = total.T
        for d in range(16):
            out_ref[g, pl.ds(ROWS * d, 8), :] = by_tile[8 * d : 8 * d + 8]

    counts_copy = pltpu.make_async_copy(cnt_hbm, cnt_ref, small_sems.at[0])
    ids_copy = pltpu.make_async_copy(ids_hbm, ids_ref, small_sems.at[1])
    counts_copy.start()
    for g in range(groups):
        fetch(g).start()
    ids_copy.start()
    stats[...] = jnp.zeros_like(stats)
    acc[...] = jnp.zeros_like(acc)
    counts_copy.wait()
    fetch(0).wait()
    turn(0)

    def advance(g, carry):
        following = jnp.minimum(g + 1, groups - 1)

        @pl.when(g + 1 < groups)
        def _():
            fetch(following).wait()

        settle(jnp.maximum(g - 1, 0), g > 0)
        evaluate(g)
        turn(following)
        for i in range(4):
            for js in ((0, 1), (2, 3)):
                accumulate(i, js)
        return carry

    lax.fori_loop(0, groups, advance, 0)
    settle(groups - 1, True)
    ids_copy.wait()
    ids = ids_ref[...]
    local = ((ids >> 14) & 1) * 512 + ((ids >> 8) & 1) * 256 + (ids & 255)
    local = local.astype(F32)
    sum0 = jnp.sum(stats[0], keepdims=True)
    sum1 = jnp.sum(stats[1], keepdims=True)
    lanes = lane_iota((1, 128))
    both = jnp.where(lanes % 2 == 0, sum0, sum1)
    for g in range(groups):
        for d in range(16):
            row = jnp.where(lanes // 8 == d, local[g : g + 1], both)
            out_ref[g, pl.ds(ROWS * d + CAP, 1), :] = row


def splat(samples, counts, ids):
    tiles = samples.shape[0]
    groups = tiles // 128
    return pl.pallas_call(
        splat_kernel,
        name="splat",
        in_specs=[pl.BlockSpec(memory_space=pltpu.HBM)] * 3,
        out_specs=pl.BlockSpec(memory_space=pltpu.VMEM),
        out_shape=pltpu.VMEM((groups, 16 * ROWS, 128), F32),
        scratch_shapes=[
            pltpu.VMEM((groups, 6, 128, 128), F32),
            pltpu.SemaphoreType.DMA((groups,)),
            pltpu.VMEM((groups, 128), jnp.int32),
            pltpu.VMEM((groups, 128), jnp.int32),
            pltpu.SemaphoreType.DMA((2,)),
            pltpu.VMEM((6, 128, 128), F32),
            pltpu.VMEM((32, 128, 128), F32),
            pltpu.VMEM((1024, 128), F32),
            pltpu.VMEM((2, 8, 128), F32),
        ],
        compiler_params=pltpu.CompilerParams(vmem_limit_bytes=24 << 20),
    )(hbm(jnp.transpose(samples, (1, 0, 2))), hbm(counts.reshape(groups, 128)), hbm(ids.reshape(groups, 128)))


def hbm(x):
    return pltpu.with_memory_space_constraint(x, pltpu.HBM)


def vmem(x):
    return pltpu.with_memory_space_constraint(x, pltpu.VMEM)


def parity_weights():
    slab, grp = lax.axis_index("slab"), lax.axis_index("grp")
    slabs, grps = lax.axis_size("slab"), lax.axis_size("grp")

    def pick(cond):
        return jnp.where(cond, 1.0, 0.0).astype(F32)

    def sides(at, count):
        odd = at % 2 == 1
        low = (pick(odd), pick(jnp.logical_and(jnp.logical_not(odd), at > 0)))
        high = (pick(jnp.logical_not(odd)), pick(jnp.logical_and(odd, at < count - 1)))
        return low, high

    return sides(slab, slabs), sides(grp, grps)


def blend(pair, a, b):
    return a * pair[0] + b * pair[1]


def column(x, y):
    return pl.ds((x * 2 + y) * BZ, BZ)


def store_edges(masked, ea_ref, eb_ref, oa_ref, ob_ref):
    up_slab = lax.axis_index("slab") % 2 == 0
    up_grp = lax.axis_index("grp") % 2 == 0
    for k in range(2):
        at = pl.ds(k * BZ, BZ)
        ea_ref[:, at] = jnp.where(up_slab, masked[1][k], masked[0][k])
        eb_ref[:, at] = jnp.where(up_slab, masked[0][k], masked[1][k])
        oa_ref[:, at] = jnp.where(up_grp, masked[k][1], masked[k][0])
        ob_ref[:, at] = jnp.where(up_grp, masked[k][0], masked[k][1])


def spread(part):
    lanes = lane_iota((NODES, BZ))
    before = jnp.where(lanes == 0, 0.0, pltpu.roll(part[:NODES], 1, 1))
    after = jnp.where(lanes == BZ - 1, 0.0, pltpu.roll(part[2 * NODES :], BZ - 1, 1))
    return part[NODES : 2 * NODES] + before + after


def split(src):
    top = src.astype(BF16)
    return top, (src - top.astype(F32)).astype(BF16)


def prepare_kernel(coupling_ref, occ_ref, w_ref, corner_ref, rowabs_ref, mask_ref):
    total = jnp.zeros((NODES, NODES), F32)
    high, low = {}, {}
    for dz in range(3):
        rows = pl.ds(dz * NODES, NODES)
        for dx in range(3):
            for dy in range(3):
                k = (dx * 3 + dy) * 3 + dz
                coupled = 0.5 * (coupling_ref[k] + coupling_ref[26 - k].T)
                total = total + jnp.abs(coupled)
                high[dx, dy], low[dx, dy] = split(coupled)
            w_ref[dx, rows, :] = jnp.concatenate([high[dx, dy] for dy in range(3)], axis=1)
            w_ref[dx, pl.ds((3 + dz) * NODES, NODES), :] = jnp.concatenate([low[dx, dy] for dy in range(3)], axis=1)
        for x in range(2):
            for y in range(2):
                at = (2 * x, 2 * y)
                corner_ref[x * 2 + y, rows, :] = jnp.concatenate([high[at], low[at], high[at]], axis=1)
    rowabs_ref[...] = jnp.broadcast_to(jnp.sum(total, axis=1, keepdims=True), (NODES, 128))
    for x in range(2):
        for y in range(2):
            mask_ref[:, column(x, y)] = jnp.broadcast_to(occ_ref[x, y : y + 1, :].astype(F32), (8, BZ))


def prepare(coupling, occupied):
    return pl.pallas_call(
        prepare_kernel,
        name="prepare",
        in_specs=[pl.BlockSpec(memory_space=pltpu.VMEM)] * 2,
        out_specs=[pl.BlockSpec(memory_space=pltpu.VMEM)] * 4,
        out_shape=[
            pltpu.VMEM((3, 6 * NODES, 3 * NODES), BF16),
            pltpu.VMEM((4, 3 * NODES, 3 * NODES), BF16),
            pltpu.VMEM((NODES, 128), F32),
            pltpu.VMEM((8, N_COLS * BZ), F32),
        ],
        compiler_params=pltpu.CompilerParams(vmem_limit_bytes=12 << 20),
        cost_estimate=pl.CostEstimate(flops=10**7, transcendentals=0, bytes_accessed=4 * 10**6),
    )(coupling, occupied)


def assemble_kernel(recv_ref, mask_ref, rowabs_ref, v_ref, diag_ref, maskc_ref, c_ref,
                    ea_ref, eb_ref, oa_ref, ob_ref, turned):
    seat = lax.axis_index("grp") % 16
    turned[...] = recv_ref[pl.ds(CAP, SENDERS, stride=ROWS), :].T
    where = turned[pl.ds(pl.multiple_of(seat * 8, 8), 8), :].astype(jnp.int32)
    other = lax.rem(seat + 1, 16)
    sums = turned[pl.ds(pl.multiple_of(other * 8, 8), 8), :]
    sum0 = jnp.sum(sums[0:1, :], keepdims=True)
    sum1 = jnp.sum(sums[1:2, :], keepdims=True)
    rowabs = rowabs_ref[...]
    mean = jnp.sum(rowabs[:, 0:1], keepdims=True) * (1.0 / NODES)
    centre = mean + 0.5 + 4.0 * (sum1 / sum0)
    inverse = 1.0 / centre
    c_ref[...] = jnp.broadcast_to(centre, (8, 128))
    tiles = []
    for c in range(CAP):
        block = recv_ref[pl.ds(c, SENDERS, stride=ROWS), :]
        high = block.astype(BF16)
        low = (block - high.astype(F32)).astype(BF16)
        tiles.append(jnp.concatenate([high, low], axis=1))
    table = jnp.concatenate(tiles, axis=0)
    masked = []
    for x in range(2):
        masked.append([])
        for y in range(2):
            picks = []
            for c in range(CAP):
                hit = row_iota((BZ, SENDERS)) + (x * 2 + y) * BZ == where[c : c + 1, :]
                picks.append(hit.astype(F32).astype(BF16))
            pick = jnp.concatenate(picks, axis=1)
            both = jnp.dot(pick, table, preferred_element_type=F32)
            ordered = (both[:, :128] + both[:, 128:]).T
            rhs = ordered[:NODES]
            dens = ordered[NODES:]
            mask = mask_ref[0:1, column(x, y)]
            v_ref[:, column(x, y)] = rhs
            diag = rowabs[:, 0:1] + 0.5 + 4.0 * dens
            diag_ref[:, column(x, y)] = (diag - centre) * inverse
            maskc_ref[:, column(x, y)] = jnp.broadcast_to(mask * inverse, (8, BZ))
            masked[x].append(rhs * mask)
    store_edges(masked, ea_ref, eb_ref, oa_ref, ob_ref)


FIELD = pltpu.VMEM((NODES, N_COLS * BZ), F32)
EDGE = pltpu.VMEM((NODES, 2 * BZ), F32)


def in_specs(count):
    return [pl.BlockSpec(memory_space=pltpu.VMEM)] * count


def assemble(recv, mask, rowabs):
    return pl.pallas_call(
        assemble_kernel,
        name="assemble",
        in_specs=in_specs(3),
        out_specs=[pl.BlockSpec(memory_space=pltpu.VMEM)] * 8,
        out_shape=[FIELD, FIELD, pltpu.VMEM((8, N_COLS * BZ), F32), pltpu.VMEM((8, 128), F32), EDGE, EDGE, EDGE, EDGE],
        scratch_shapes=[pltpu.VMEM((128, 128), F32)],
        compiler_params=pltpu.CompilerParams(vmem_limit_bytes=16 << 20),
    )(vmem(recv), vmem(mask), vmem(rowabs))


def product(weights, source):
    high, low = split(source)
    stacked = jnp.concatenate([high, high, low], axis=0)
    return spread(jnp.dot(weights, stacked, preferred_element_type=F32))


def put_moments(order, mom_ref, mom_out, sq, cross):
    sq = jnp.sum(sq, keepdims=True)
    cross = jnp.sum(cross, keepdims=True)
    spot = lane_iota((1, 128))
    before = jnp.zeros((1, 128), F32) if mom_ref is None else mom_ref[0:1, :]
    mom = jnp.where(spot == 2 * order, sq, jnp.where(spot == 2 * order + 1, cross, before))
    mom_out[...] = jnp.broadcast_to(mom, mom_out.shape)


def sides_kernel(last, v_ref, mask_ref, ra_ref, rb_ref, ya_ref, yb_ref, w_ref, *rest):
    if last:
        corner_ref, diag_ref, maskc_ref, c_ref, mom_ref, o_ref, mom_out, high, low = rest
    else:
        o_ref, high, low = rest
    (x_low, x_high), (y_low, y_high) = parity_weights()
    halo, rise = {}, {}

    def at_rows(px, py):
        return pl.ds((px * 4 + py) * NODES, NODES)

    def put(px, py, src):
        high[at_rows(px, py), :], low[at_rows(px, py), :] = split(src)

    for x in range(2):
        for y in range(2):
            put(x + 1, y + 1, v_ref[:, column(x, y)] * mask_ref[0:1, column(x, y)])
    for k in range(2):
        at = pl.ds(k * BZ, BZ)
        halo[k] = (blend(x_low, ra_ref[:, at], rb_ref[:, at]), blend(x_high, ra_ref[:, at], rb_ref[:, at]))
        put(0, k + 1, halo[k][0])
        put(3, k + 1, halo[k][1])
        rise[k] = (blend(y_low, ya_ref[:, at], yb_ref[:, at]), blend(y_high, ya_ref[:, at], yb_ref[:, at]))
        put(k + 1, 0, rise[k][0])
        put(k + 1, 3, rise[k][1])
    nothing = jnp.zeros((NODES, BZ), BF16)
    for px in (0, 3):
        for py in (0, 3):
            high[at_rows(px, py), :] = nothing
            low[at_rows(px, py), :] = nothing
    sq = jnp.zeros((NODES, BZ), F32)
    cross = jnp.zeros((NODES, BZ), F32)
    for x in range(2):
        for y in range(2):
            full = jnp.zeros((6 * NODES, BZ), F32)
            half = jnp.zeros((3 * NODES, BZ), F32)
            for dx in range(3):
                rows = pl.ds(((x + dx) * 4 + y) * NODES, 3 * NODES)
                full = full + jnp.dot(w_ref[dx], high[rows, :], preferred_element_type=F32)
                half = half + jnp.dot(w_ref[dx, 0 : 3 * NODES, :], low[rows, :], preferred_element_type=F32)
            at = column(x, y)
            total = spread(full[: 3 * NODES] + full[3 * NODES :] + half)
            o_ref[:, at] = total
            if last:
                v = v_ref[:, at]
                sq = sq + v * v
                cross = cross + v * (diag_ref[:, at] * v - maskc_ref[0:1, at] * total)
    if not last:
        return
    energy = jnp.zeros((NODES, BZ), F32)
    for x in range(2):
        for y in range(2):
            energy = energy + halo[y][x] * product(corner_ref[(1 - x) * 2 + y], rise[x][y])
    cross = cross - energy * (1.0 / c_ref[0:1, 0:1])
    put_moments(2, mom_ref, mom_out, sq, cross)


def sides(operands, last):
    shapes = [FIELD] + ([pltpu.VMEM((SENDERS, 128), F32)] if last else [])
    return pl.pallas_call(
        functools.partial(sides_kernel, last),
        name="sides",
        in_specs=in_specs(len(operands)),
        out_specs=[pl.BlockSpec(memory_space=pltpu.VMEM)] * len(shapes),
        out_shape=shapes,
        scratch_shapes=[pltpu.VMEM((16 * NODES, BZ), BF16), pltpu.VMEM((16 * NODES, BZ), BF16)],
        compiler_params=pltpu.CompilerParams(vmem_limit_bytes=16 << 20),
        cost_estimate=pl.CostEstimate(flops=15 * 10**8, transcendentals=0, bytes_accessed=2 * 10**6),
    )(*[vmem(x) for x in operands])


def corners_kernel(order, last, sum_ref, v_ref, diag_ref, mask_ref, maskc_ref, ca_ref, cb_ref, corner_ref, *rest):
    rest = list(rest)
    mom_ref = rest.pop(0) if order and not last else None
    o_ref = rest.pop(0)
    x_pairs, y_pairs = parity_weights()
    sq = jnp.zeros((NODES, BZ), F32)
    cross = jnp.zeros((NODES, BZ), F32)
    masked = [[], []]
    for y in range(2):
        line = [blend(y_pairs[y], ca_ref[:, pl.ds(k * BZ, BZ)], cb_ref[:, pl.ds(k * BZ, BZ)]) for k in range(2)]
        for x in range(2):
            at = column(x, y)
            total = sum_ref[:, at] + product(corner_ref[x * 2 + y], blend(x_pairs[x], line[0], line[1]))
            v = v_ref[:, at]
            new = diag_ref[:, at] * v - maskc_ref[0:1, at] * total
            o_ref[:, at] = new
            if not last:
                masked[x].append(new * mask_ref[0:1, at])
                sq = sq + v * v
                cross = cross + v * new
    if not last:
        store_edges(masked, *rest[1:])
        put_moments(order, mom_ref, rest[0], sq, cross)


def corners(order, operands, last):
    shapes = [FIELD] + ([] if last else [pltpu.VMEM((8, 128), F32)] + [EDGE] * 4)
    return pl.pallas_call(
        functools.partial(corners_kernel, order, last),
        name="corners",
        in_specs=in_specs(len(operands)),
        out_specs=[pl.BlockSpec(memory_space=pltpu.VMEM)] * len(shapes),
        out_shape=shapes,
        compiler_params=pltpu.CompilerParams(vmem_limit_bytes=16 << 20),
        cost_estimate=pl.CostEstimate(flops=5 * 10**8, transcendentals=0, bytes_accessed=2 * 10**6),
    )(*[vmem(x) for x in operands])


def apply_stiffness(order, v, diag, mask, maskc, centre, edges, weights, corner, moments):
    last = order == 2
    ra, rb, ya, yb, ca, cb = exchange(lax.axis_index("grp"), *edges)
    operands = [v, mask, ra, rb, ya, yb, weights] + ([corner, diag, maskc, centre, moments] if last else [])
    part, *shared = sides(operands, last)
    operands = [part, v, diag, mask, maskc, ca, cb, corner]
    if last:
        return corners(order, operands, last)[0], shared[0], []
    new, moments, *edges = corners(order, operands + ([] if moments is None else [moments]), last)
    return new, moments, edges


def finish_kernel(mom_ref, c_ref, v0_ref, v1_ref, v2_ref, v3_ref, x_ref, r_ref):
    row = jnp.sum(mom_ref[...], axis=0, keepdims=True)
    lanes = lane_iota((1, 128))
    m = [jnp.sum(jnp.where(lanes == k, row, 0.0), keepdims=True) for k in range(6)]
    zero = jnp.zeros((1, 1), F32)
    one = jnp.ones((1, 1), F32)

    def inner(f, g):
        total = zero
        for i, a in enumerate(f):
            for j, b in enumerate(g):
                if a is not None and b is not None:
                    total = total + a * b * m[i + j]
        return total

    r = [one, None, None, None]
    p = [one, None, None, None]
    x = [None, None, None]
    norm = m[0]

    def plus(a, b):
        if a is None:
            return b
        return a if b is None else a + b

    for step in range(3):
        image = [plus(p[k], p[k - 1] if k else None) for k in range(4)]
        alpha = norm / inner(p, image)
        for k in range(3):
            if p[k] is not None:
                x[k] = plus(x[k], alpha * p[k])
        for k in range(4):
            if image[k] is not None:
                r[k] = plus(r[k], -(alpha * image[k]))
        if step < 2:
            new = inner(r, r)
            beta = new / norm
            p = [plus(r[k], None if p[k] is None else beta * p[k]) for k in range(4)]
            norm = new
    inverse = 1.0 / c_ref[0:1, 0:1]
    x = [value * inverse for value in x]
    for chunk in range(8):
        bx, by, zt = chunk // 4, chunk // 2 % 2, chunk % 2
        spot = bx * 4 + zt * 2 + by
        at = pl.ds(chunk * 128, 128)
        v0, v1, v2, v3 = v0_ref[:, at], v1_ref[:, at], v2_ref[:, at], v3_ref[:, at]
        x_ref[:, spot, :] = x[0] * v0 + x[1] * v1 + x[2] * v2
        r_ref[:, spot, :] = r[0] * v0 + r[1] * v1 + r[2] * v2 + r[3] * v3


def finish(moments, centre, fields):
    out = jax.ShapeDtypeStruct((NODES, 8, 128), F32)
    return pl.pallas_call(
        finish_kernel,
        name="finish",
        in_specs=[pl.BlockSpec(memory_space=pltpu.VMEM)] * 6,
        out_specs=[pl.BlockSpec(memory_space=pltpu.VMEM)] * 2,
        out_shape=[out, out],
        compiler_params=pltpu.CompilerParams(vmem_limit_bytes=16 << 20),
    )(moments, *[vmem(x) for x in (centre, *fields)])


def swap(axis, first):
    count = lax.axis_size(axis)
    return [(i, (i + 1 if (i - first) % 2 == 0 else i - 1) % count) for i in range(count)]


def odd_swap():
    slabs, grps = lax.axis_size("slab"), lax.axis_size("grp")
    pairs = []
    for s in range(slabs):
        for g in range(grps):
            if g in (0, grps - 1):
                pairs.append((s * grps + g, (s ^ 1) * grps + g))
            else:
                pairs.append((s * grps + g, s * grps + (g + 1 if g % 2 else g - 1)))
    return pairs


def exchange(grp, ea, eb, oa, ob):
    yb = lax.ppermute(ob, AXES, odd_swap())
    ra = lax.ppermute(ea, "slab", swap("slab", 0))
    rb = lax.ppermute(eb, "slab", swap("slab", 1))
    ya = lax.ppermute(oa, "grp", swap("grp", 0))
    up = grp % 2 == 0

    def line(upper):
        return jnp.concatenate([jnp.where(upper, r[:, BZ:], r[:, :BZ]) for r in (ra, rb)], axis=1)

    cb = lax.ppermute(line(jnp.logical_not(up)), AXES, odd_swap())
    ca = lax.ppermute(line(up), "grp", swap("grp", 0))
    return ra, rb, ya, yb, ca, cb


def on_device(samples, block_ids, tile_counts, occupied, coupling):
    payload = splat(samples, tile_counts, block_ids)
    recv = lax.all_to_all(payload.reshape(SENDERS, 1, ROWS * 128), AXES, split_axis=0, concat_axis=0, tiled=True)
    weights, corner, rowabs, mask = prepare(coupling, occupied)
    v, diag, maskc, centre, *edges = assemble(recv.reshape(SENDERS * ROWS, 128), mask, rowabs)
    fields = [v]
    moments = None
    for order in range(3):
        v, moments, edges = apply_stiffness(
            order, v, diag, mask, maskc, centre, edges, weights, corner, moments
        )
        fields.append(v)
    shared = lax.all_to_all(moments.reshape(SENDERS, 1, 128), AXES, split_axis=0, concat_axis=0, tiled=True)
    outs = finish(shared.reshape(SENDERS, 128), centre, fields)

    def settle(out):
        out = out.reshape(NODES, 2, 2, 2, 128)
        return jnp.transpose(out, (0, 1, 3, 2, 4)).reshape(NODES, 2, 2, BZ)

    return settle(outs[0]), settle(outs[1])


def solution(mesh):
    placed = (P(AXES, None, None), P(AXES), P(AXES), P("slab", "grp", None), P())
    return jax.shard_map(
        on_device,
        mesh=mesh,
        in_specs=placed,
        out_specs=(P(None, "slab", "grp", None), P(None, "slab", "grp", None)),
        check_vma=False,
    )
```

```python
import functools

import jax
import jax.numpy as jnp
from jax import lax
from jax.experimental import pallas as pl
from jax.experimental.pallas import tpu as pltpu
from jax.sharding import PartitionSpec as P

AXES = ("slab", "grp")
F32 = jnp.float32
BF16 = jnp.bfloat16
N_COLS = 4
BZ = 256
NODES = 64
SENDERS = 128
CAP = 8
ROWS = CAP + 1


def lane_iota(shape):
    return lax.broadcasted_iota(jnp.int32, shape, len(shape) - 1)


def row_iota(shape):
    return lax.broadcasted_iota(jnp.int32, shape, 0)


def basis_of(pos):
    u = 4.0 * pos
    w = u - jnp.floor(u)
    back = w - 1.0
    low = back * back
    high = w * w
    turn = w * back
    mid = 1.0 - (turn + turn)
    smid = -(w + back)
    in0, in1, in2 = u < 1.0, u < 2.0, u < 3.0
    zero = jnp.zeros_like(u)

    def nodes(below, at, above):
        return [
            jnp.where(in0, at, jnp.where(in1, below, zero)),
            jnp.where(in0, above, jnp.where(in1, at, jnp.where(in2, below, zero))),
            jnp.where(in0, zero, jnp.where(in1, above, jnp.where(in2, at, below))),
            jnp.where(in1, zero, jnp.where(in2, above, at)),
        ]

    return nodes(low, mid, high), nodes(back, smid, w)


def splat_kernel(samp_ref, cnt_hbm, ids_hbm, out_ref, held, sems, cnt_ref, ids_ref, small_sems, flip, basis, acc, stats):
    groups = out_ref.shape[0]

    def fetch(g):
        return pltpu.make_async_copy(samp_ref.at[:, pl.ds(g * 128, 128), :], held.at[g], sems.at[g])

    def turn(g):
        for k in range(6):
            flip[k] = held[g, k].T

    def evaluate(g):
        counts = cnt_ref[pl.ds(g, 1), :]
        for group in range(16):
            rows = pl.ds(group * 8, 8)
            live = row_iota((8, 128)) + group * 8 < counts
            n0 = jnp.where(live, flip[3, rows, :], 0.0)
            n1 = jnp.where(live, flip[4, rows, :], 0.0)
            n2 = jnp.where(live, flip[5, rows, :], 0.0)
            eighth = jnp.where(live, 0.125, 0.0)
            val, slo = basis_of(flip[0, rows, :])
            for i in range(4):
                basis[i, rows, :] = slo[i] * n0
                basis[4 + i, rows, :] = val[i] * n1
                basis[8 + i, rows, :] = val[i] * n2
                basis[12 + i, rows, :] = val[i] * eighth
            for d in (1, 2):
                val, slo = basis_of(flip[d, rows, :])
                for i in range(4):
                    basis[8 + 8 * d + i, rows, :] = val[i]
                    basis[12 + 8 * d + i, rows, :] = slo[i]

    def accumulate(i, js):
        rhs_sums, dens_sums = {}, {}
        for group in range(16):
            rows = pl.ds(group * 8, 8)
            a = basis[i, rows, :]
            b = basis[4 + i, rows, :]
            c = basis[8 + i, rows, :]
            d = basis[12 + i, rows, :]
            v2 = [basis[24 + l, rows, :] for l in range(4)]
            s2 = [basis[28 + l, rows, :] for l in range(4)]
            for j in js:
                v1 = basis[16 + j, rows, :]
                s1 = basis[20 + j, rows, :]
                first = a * v1 + b * s1
                second = c * v1
                dens = d * v1
                for l in range(4):
                    at = j * 4 + l
                    rhs = first * v2[l] + second * s2[l]
                    den = dens * v2[l]
                    rhs_sums[at] = rhs if group == 0 else rhs_sums[at] + rhs
                    dens_sums[at] = den if group == 0 else dens_sums[at] + den
        for at in rhs_sums:
            acc[pl.ds((i * 16 + at) * 8, 8), :] = rhs_sums[at]
            acc[pl.ds((64 + i * 16 + at) * 8, 8), :] = dens_sums[at]

    def settle(g, real):
        total = acc[pl.ds(0, 128, stride=8), :]
        for s in range(1, 8):
            total = total + acc[pl.ds(s, 128, stride=8), :]
        square = total[:64] * total[:64]
        weighted = total[64:] * square
        part, wpart = square[:8], weighted[:8]
        for k in range(1, 8):
            part = part + square[8 * k : 8 * k + 8]
            wpart = wpart + weighted[8 * k : 8 * k + 8]
        stats[0] = stats[0] + jnp.where(real, part, 0.0)
        stats[1] = stats[1] + jnp.where(real, wpart, 0.0)
        by_tile = total.T
        for d in range(16):
            out_ref[g, pl.ds(ROWS * d, 8), :] = by_tile[8 * d : 8 * d + 8]

    counts_copy = pltpu.make_async_copy(cnt_hbm, cnt_ref, small_sems.at[0])
    ids_copy = pltpu.make_async_copy(ids_hbm, ids_ref, small_sems.at[1])
    fetch(0).start()
    counts_copy.start()
    for g in range(1, groups):
        fetch(g).start()
    ids_copy.start()
    stats[...] = jnp.zeros_like(stats)
    acc[...] = jnp.zeros_like(acc)
    fetch(0).wait()
    turn(0)
    counts_copy.wait()

    def advance(g, carry):
        following = jnp.minimum(g + 1, groups - 1)

        @pl.when(g + 1 < groups)
        def _():
            fetch(following).wait()

        settle(jnp.maximum(g - 1, 0), g > 0)
        evaluate(g)
        turn(following)
        for i in range(4):
            for js in ((0, 1), (2, 3)):
                accumulate(i, js)
        return carry

    lax.fori_loop(0, groups, advance, 0)
    settle(groups - 1, True)
    ids_copy.wait()
    ids = ids_ref[...]
    local = ((ids >> 14) & 1) * 512 + ((ids >> 8) & 1) * 256 + (ids & 255)
    local = local.astype(F32)
    sum0 = jnp.sum(stats[0], keepdims=True)
    sum1 = jnp.sum(stats[1], keepdims=True)
    lanes = lane_iota((1, 128))
    both = jnp.where(lanes % 2 == 0, sum0, sum1)
    for g in range(groups):
        for d in range(16):
            row = jnp.where(lanes // 8 == d, local[g : g + 1], both)
            out_ref[g, pl.ds(ROWS * d + CAP, 1), :] = row


def splat(samples, counts, ids):
    tiles = samples.shape[0]
    groups = tiles // 128
    return pl.pallas_call(
        splat_kernel,
        name="splat",
        in_specs=[pl.BlockSpec(memory_space=pltpu.HBM)] * 3,
        out_specs=pl.BlockSpec(memory_space=pltpu.VMEM),
        out_shape=pltpu.VMEM((groups, 16 * ROWS, 128), F32),
        scratch_shapes=[
            pltpu.VMEM((groups, 6, 128, 128), F32),
            pltpu.SemaphoreType.DMA((groups,)),
            pltpu.VMEM((groups, 128), jnp.int32),
            pltpu.VMEM((groups, 128), jnp.int32),
            pltpu.SemaphoreType.DMA((2,)),
            pltpu.VMEM((6, 128, 128), F32),
            pltpu.VMEM((32, 128, 128), F32),
            pltpu.VMEM((1024, 128), F32),
            pltpu.VMEM((2, 8, 128), F32),
        ],
        compiler_params=pltpu.CompilerParams(vmem_limit_bytes=24 << 20),
    )(hbm(jnp.transpose(samples, (1, 0, 2))), hbm(counts.reshape(groups, 128)), hbm(ids.reshape(groups, 128)))


def hbm(x):
    return pltpu.with_memory_space_constraint(x, pltpu.HBM)


def vmem(x):
    return pltpu.with_memory_space_constraint(x, pltpu.VMEM)


def parity_weights():
    slab, grp = lax.axis_index("slab"), lax.axis_index("grp")
    slabs, grps = lax.axis_size("slab"), lax.axis_size("grp")

    def pick(cond):
        return jnp.where(cond, 1.0, 0.0).astype(F32)

    def sides(at, count):
        odd = at % 2 == 1
        low = (pick(odd), pick(jnp.logical_and(jnp.logical_not(odd), at > 0)))
        high = (pick(jnp.logical_not(odd)), pick(jnp.logical_and(odd, at < count - 1)))
        return low, high

    return sides(slab, slabs), sides(grp, grps)


def blend(pair, a, b):
    return a * pair[0] + b * pair[1]


def column(x, y):
    return pl.ds((x * 2 + y) * BZ, BZ)


def store_edges(masked, ea_ref, eb_ref, oa_ref, ob_ref):
    up_slab = lax.axis_index("slab") % 2 == 0
    up_grp = lax.axis_index("grp") % 2 == 0
    for k in range(2):
        at = pl.ds(k * BZ, BZ)
        ea_ref[:, at] = jnp.where(up_slab, masked[1][k], masked[0][k])
        eb_ref[:, at] = jnp.where(up_slab, masked[0][k], masked[1][k])
        oa_ref[:, at] = jnp.where(up_grp, masked[k][1], masked[k][0])
        ob_ref[:, at] = jnp.where(up_grp, masked[k][0], masked[k][1])


def spread(part):
    lanes = lane_iota((NODES, BZ))
    before = jnp.where(lanes == 0, 0.0, pltpu.roll(part[:NODES], 1, 1))
    after = jnp.where(lanes == BZ - 1, 0.0, pltpu.roll(part[2 * NODES :], BZ - 1, 1))
    return part[NODES : 2 * NODES] + before + after


def split(src):
    top = src.astype(BF16)
    return top, (src - top.astype(F32)).astype(BF16)


def prepare_kernel(coupling_ref, occ_ref, w_ref, corner_ref, rowabs_ref, mask_ref):
    total = jnp.zeros((NODES, NODES), F32)
    high, low = {}, {}
    for dz in range(3):
        rows = pl.ds(dz * NODES, NODES)
        for dx in range(3):
            for dy in range(3):
                k = (dx * 3 + dy) * 3 + dz
                coupled = 0.5 * (coupling_ref[k] + coupling_ref[26 - k].T)
                total = total + jnp.abs(coupled)
                high[dx, dy], low[dx, dy] = split(coupled)
            w_ref[dx, rows, :] = jnp.concatenate([high[dx, dy] for dy in range(3)], axis=1)
            w_ref[dx, pl.ds((3 + dz) * NODES, NODES), :] = jnp.concatenate([low[dx, dy] for dy in range(3)], axis=1)
        for x in range(2):
            for y in range(2):
                at = (2 * x, 2 * y)
                corner_ref[x * 2 + y, rows, :] = jnp.concatenate([high[at], low[at], high[at]], axis=1)
    rowabs_ref[...] = jnp.broadcast_to(jnp.sum(total, axis=1, keepdims=True), (NODES, 128))
    for x in range(2):
        for y in range(2):
            mask_ref[:, column(x, y)] = jnp.broadcast_to(occ_ref[x, y : y + 1, :].astype(F32), (8, BZ))


def prepare(coupling, occupied):
    return pl.pallas_call(
        prepare_kernel,
        name="prepare",
        in_specs=[pl.BlockSpec(memory_space=pltpu.VMEM)] * 2,
        out_specs=[pl.BlockSpec(memory_space=pltpu.VMEM)] * 4,
        out_shape=[
            pltpu.VMEM((3, 6 * NODES, 3 * NODES), BF16),
            pltpu.VMEM((4, 3 * NODES, 3 * NODES), BF16),
            pltpu.VMEM((NODES, 128), F32),
            pltpu.VMEM((8, N_COLS * BZ), F32),
        ],
        compiler_params=pltpu.CompilerParams(vmem_limit_bytes=12 << 20),
        cost_estimate=pl.CostEstimate(flops=10**7, transcendentals=0, bytes_accessed=4 * 10**6),
    )(coupling, occupied)


def assemble_kernel(recv_ref, mask_ref, rowabs_ref, v_ref, diag_ref, maskc_ref, c_ref,
                    ea_ref, eb_ref, oa_ref, ob_ref, turned):
    seat = lax.axis_index("grp") % 16
    turned[...] = recv_ref[pl.ds(CAP, SENDERS, stride=ROWS), :].T
    where = turned[pl.ds(pl.multiple_of(seat * 8, 8), 8), :].astype(jnp.int32)
    other = lax.rem(seat + 1, 16)
    sums = turned[pl.ds(pl.multiple_of(other * 8, 8), 8), :]
    sum0 = jnp.sum(sums[0:1, :], keepdims=True)
    sum1 = jnp.sum(sums[1:2, :], keepdims=True)
    rowabs = rowabs_ref[...]
    mean = jnp.sum(rowabs[:, 0:1], keepdims=True) * (1.0 / NODES)
    centre = mean + 0.5 + 4.0 * (sum1 / sum0)
    inverse = 1.0 / centre
    c_ref[...] = jnp.broadcast_to(centre, (8, 128))
    tiles = []
    for c in range(CAP):
        block = recv_ref[pl.ds(c, SENDERS, stride=ROWS), :]
        high = block.astype(BF16)
        low = (block - high.astype(F32)).astype(BF16)
        tiles.append(jnp.concatenate([high, low], axis=1))
    table = jnp.concatenate(tiles, axis=0)
    masked = []
    for x in range(2):
        masked.append([])
        for y in range(2):
            picks = []
            for c in range(CAP):
                hit = row_iota((BZ, SENDERS)) + (x * 2 + y) * BZ == where[c : c + 1, :]
                picks.append(hit.astype(F32).astype(BF16))
            pick = jnp.concatenate(picks, axis=1)
            both = jnp.dot(pick, table, preferred_element_type=F32)
            ordered = (both[:, :128] + both[:, 128:]).T
            rhs = ordered[:NODES]
            dens = ordered[NODES:]
            mask = mask_ref[0:1, column(x, y)]
            v_ref[:, column(x, y)] = rhs
            diag = rowabs[:, 0:1] + 0.5 + 4.0 * dens
            diag_ref[:, column(x, y)] = (diag - centre) * inverse
            maskc_ref[:, column(x, y)] = jnp.broadcast_to(mask * inverse, (8, BZ))
            masked[x].append(rhs * mask)
    store_edges(masked, ea_ref, eb_ref, oa_ref, ob_ref)


FIELD = pltpu.VMEM((NODES, N_COLS * BZ), F32)
EDGE = pltpu.VMEM((NODES, 2 * BZ), F32)


def in_specs(count):
    return [pl.BlockSpec(memory_space=pltpu.VMEM)] * count


def assemble(recv, mask, rowabs):
    return pl.pallas_call(
        assemble_kernel,
        name="assemble",
        in_specs=in_specs(3),
        out_specs=[pl.BlockSpec(memory_space=pltpu.VMEM)] * 8,
        out_shape=[FIELD, FIELD, pltpu.VMEM((8, N_COLS * BZ), F32), pltpu.VMEM((8, 128), F32), EDGE, EDGE, EDGE, EDGE],
        scratch_shapes=[pltpu.VMEM((128, 128), F32)],
        compiler_params=pltpu.CompilerParams(vmem_limit_bytes=16 << 20),
    )(vmem(recv), vmem(mask), vmem(rowabs))


def product(weights, source):
    high, low = split(source)
    stacked = jnp.concatenate([high, high, low], axis=0)
    return spread(jnp.dot(weights, stacked, preferred_element_type=F32))


def put_moments(order, mom_ref, mom_out, sq, cross):
    sq = jnp.sum(sq, keepdims=True)
    cross = jnp.sum(cross, keepdims=True)
    spot = lane_iota((1, 128))
    before = jnp.zeros((1, 128), F32) if mom_ref is None else mom_ref[0:1, :]
    mom = jnp.where(spot == 2 * order, sq, jnp.where(spot == 2 * order + 1, cross, before))
    mom_out[...] = jnp.broadcast_to(mom, mom_out.shape)


def sides_kernel(last, v_ref, mask_ref, ra_ref, rb_ref, ya_ref, yb_ref, w_ref, *rest):
    if last:
        corner_ref, diag_ref, maskc_ref, c_ref, mom_ref, o_ref, mom_out, high, low = rest
    else:
        o_ref, high, low = rest
    (x_low, x_high), (y_low, y_high) = parity_weights()
    halo, rise = {}, {}

    def at_rows(px, py):
        return pl.ds((px * 4 + py) * NODES, NODES)

    def put(px, py, src):
        high[at_rows(px, py), :], low[at_rows(px, py), :] = split(src)

    for x in range(2):
        for y in range(2):
            put(x + 1, y + 1, v_ref[:, column(x, y)] * mask_ref[0:1, column(x, y)])
    for k in range(2):
        at = pl.ds(k * BZ, BZ)
        halo[k] = (blend(x_low, ra_ref[:, at], rb_ref[:, at]), blend(x_high, ra_ref[:, at], rb_ref[:, at]))
        put(0, k + 1, halo[k][0])
        put(3, k + 1, halo[k][1])
        rise[k] = (blend(y_low, ya_ref[:, at], yb_ref[:, at]), blend(y_high, ya_ref[:, at], yb_ref[:, at]))
        put(k + 1, 0, rise[k][0])
        put(k + 1, 3, rise[k][1])
    nothing = jnp.zeros((NODES, BZ), BF16)
    for px in (0, 3):
        for py in (0, 3):
            high[at_rows(px, py), :] = nothing
            low[at_rows(px, py), :] = nothing
    sq = jnp.zeros((NODES, BZ), F32)
    cross = jnp.zeros((NODES, BZ), F32)
    for x in range(2):
        for y in range(2):
            full = jnp.zeros((6 * NODES, BZ), F32)
            half = jnp.zeros((3 * NODES, BZ), F32)
            for dx in range(3):
                rows = pl.ds(((x + dx) * 4 + y) * NODES, 3 * NODES)
                full = full + jnp.dot(w_ref[dx], high[rows, :], preferred_element_type=F32)
                half = half + jnp.dot(w_ref[dx, 0 : 3 * NODES, :], low[rows, :], preferred_element_type=F32)
            at = column(x, y)
            total = spread(full[: 3 * NODES] + full[3 * NODES :] + half)
            o_ref[:, at] = total
            if last:
                v = v_ref[:, at]
                sq = sq + v * v
                cross = cross + v * (diag_ref[:, at] * v - maskc_ref[0:1, at] * total)
    if not last:
        return
    energy = jnp.zeros((NODES, BZ), F32)
    for x in range(2):
        for y in range(2):
            energy = energy + halo[y][x] * product(corner_ref[(1 - x) * 2 + y], rise[x][y])
    cross = cross - energy * (1.0 / c_ref[0:1, 0:1])
    put_moments(2, mom_ref, mom_out, sq, cross)


def sides(operands, last):
    shapes = [FIELD] + ([pltpu.VMEM((SENDERS, 128), F32)] if last else [])
    return pl.pallas_call(
        functools.partial(sides_kernel, last),
        name="sides",
        in_specs=in_specs(len(operands)),
        out_specs=[pl.BlockSpec(memory_space=pltpu.VMEM)] * len(shapes),
        out_shape=shapes,
        scratch_shapes=[pltpu.VMEM((16 * NODES, BZ), BF16), pltpu.VMEM((16 * NODES, BZ), BF16)],
        compiler_params=pltpu.CompilerParams(vmem_limit_bytes=16 << 20),
        cost_estimate=pl.CostEstimate(flops=15 * 10**8, transcendentals=0, bytes_accessed=2 * 10**6),
    )(*[vmem(x) for x in operands])


def corners_kernel(order, last, sum_ref, v_ref, diag_ref, mask_ref, maskc_ref, ca_ref, cb_ref, corner_ref, *rest):
    rest = list(rest)
    mom_ref = rest.pop(0) if order and not last else None
    o_ref = rest.pop(0)
    x_pairs, y_pairs = parity_weights()
    sq = jnp.zeros((NODES, BZ), F32)
    cross = jnp.zeros((NODES, BZ), F32)
    masked = [[], []]
    for y in range(2):
        line = [blend(y_pairs[y], ca_ref[:, pl.ds(k * BZ, BZ)], cb_ref[:, pl.ds(k * BZ, BZ)]) for k in range(2)]
        for x in range(2):
            at = column(x, y)
            total = sum_ref[:, at] + product(corner_ref[x * 2 + y], blend(x_pairs[x], line[0], line[1]))
            v = v_ref[:, at]
            new = diag_ref[:, at] * v - maskc_ref[0:1, at] * total
            o_ref[:, at] = new
            if not last:
                masked[x].append(new * mask_ref[0:1, at])
                sq = sq + v * v
                cross = cross + v * new
    if not last:
        store_edges(masked, *rest[1:])
        put_moments(order, mom_ref, rest[0], sq, cross)


def corners(order, operands, last):
    shapes = [FIELD] + ([] if last else [pltpu.VMEM((8, 128), F32)] + [EDGE] * 4)
    return pl.pallas_call(
        functools.partial(corners_kernel, order, last),
        name="corners",
        in_specs=in_specs(len(operands)),
        out_specs=[pl.BlockSpec(memory_space=pltpu.VMEM)] * len(shapes),
        out_shape=shapes,
        compiler_params=pltpu.CompilerParams(vmem_limit_bytes=16 << 20),
        cost_estimate=pl.CostEstimate(flops=5 * 10**8, transcendentals=0, bytes_accessed=2 * 10**6),
    )(*[vmem(x) for x in operands])


def apply_stiffness(order, v, diag, mask, maskc, centre, edges, weights, corner, moments):
    last = order == 2
    ra, rb, ya, yb, ca, cb = exchange(lax.axis_index("grp"), *edges)
    operands = [v, mask, ra, rb, ya, yb, weights] + ([corner, diag, maskc, centre, moments] if last else [])
    part, *shared = sides(operands, last)
    operands = [part, v, diag, mask, maskc, ca, cb, corner]
    if last:
        return corners(order, operands, last)[0], shared[0], []
    new, moments, *edges = corners(order, operands + ([] if moments is None else [moments]), last)
    return new, moments, edges


def finish_kernel(mom_ref, c_ref, v0_ref, v1_ref, v2_ref, v3_ref, x_hbm, r_hbm, x_ref, r_ref, sems):
    row = jnp.sum(mom_ref[...], axis=0, keepdims=True)
    lanes = lane_iota((1, 128))
    m = [jnp.sum(jnp.where(lanes == k, row, 0.0), keepdims=True) for k in range(6)]
    zero = jnp.zeros((1, 1), F32)
    one = jnp.ones((1, 1), F32)

    def inner(f, g):
        total = zero
        for i, a in enumerate(f):
            for j, b in enumerate(g):
                if a is not None and b is not None:
                    total = total + a * b * m[i + j]
        return total

    r = [one, None, None, None]
    p = [one, None, None, None]
    x = [None, None, None]
    norm = m[0]

    def plus(a, b):
        if a is None:
            return b
        return a if b is None else a + b

    for step in range(3):
        image = [plus(p[k], p[k - 1] if k else None) for k in range(4)]
        alpha = norm / inner(p, image)
        for k in range(3):
            if p[k] is not None:
                x[k] = plus(x[k], alpha * p[k])
        for k in range(4):
            if image[k] is not None:
                r[k] = plus(r[k], -(alpha * image[k]))
        if step < 2:
            new = inner(r, r)
            beta = new / norm
            p = [plus(r[k], None if p[k] is None else beta * p[k]) for k in range(4)]
            norm = new
    inverse = 1.0 / c_ref[0:1, 0:1]
    x = [value * inverse for value in x]
    send_x = pltpu.make_async_copy(x_ref, x_hbm, sems.at[0])
    send_r = pltpu.make_async_copy(r_ref, r_hbm, sems.at[1])

    def spots():
        for chunk in range(8):
            bx, by, zt = chunk // 4, chunk // 2 % 2, chunk % 2
            yield bx * 4 + zt * 2 + by, pl.ds(chunk * 128, 128)

    for spot, at in spots():
        x_ref[:, spot, :] = x[0] * v0_ref[:, at] + x[1] * v1_ref[:, at] + x[2] * v2_ref[:, at]
    send_x.start()
    for spot, at in spots():
        r_ref[:, spot, :] = r[0] * v0_ref[:, at] + r[1] * v1_ref[:, at] + r[2] * v2_ref[:, at] + r[3] * v3_ref[:, at]
    send_r.start()
    send_x.wait()
    send_r.wait()


def finish(moments, centre, fields):
    out = jax.ShapeDtypeStruct((NODES, 8, 128), F32)
    return pl.pallas_call(
        finish_kernel,
        name="finish",
        in_specs=[pl.BlockSpec(memory_space=pltpu.VMEM)] * 6,
        out_specs=[pl.BlockSpec(memory_space=pltpu.HBM)] * 2,
        out_shape=[out, out],
        scratch_shapes=[pltpu.VMEM((NODES, 8, 128), F32)] * 2 + [pltpu.SemaphoreType.DMA((2,))],
        compiler_params=pltpu.CompilerParams(vmem_limit_bytes=16 << 20),
    )(moments, *[vmem(x) for x in (centre, *fields)])


def swap(axis, first):
    count = lax.axis_size(axis)
    return [(i, (i + 1 if (i - first) % 2 == 0 else i - 1) % count) for i in range(count)]


def odd_swap():
    slabs, grps = lax.axis_size("slab"), lax.axis_size("grp")
    pairs = []
    for s in range(slabs):
        for g in range(grps):
            if g in (0, grps - 1):
                pairs.append((s * grps + g, (s ^ 1) * grps + g))
            else:
                pairs.append((s * grps + g, s * grps + (g + 1 if g % 2 else g - 1)))
    return pairs


def exchange(grp, ea, eb, oa, ob):
    yb = lax.ppermute(ob, AXES, odd_swap())
    ra = lax.ppermute(ea, "slab", swap("slab", 0))
    rb = lax.ppermute(eb, "slab", swap("slab", 1))
    ya = lax.ppermute(oa, "grp", swap("grp", 0))
    up = grp % 2 == 0

    def line(upper):
        return jnp.concatenate([jnp.where(upper, r[:, BZ:], r[:, :BZ]) for r in (ra, rb)], axis=1)

    cb = lax.ppermute(line(jnp.logical_not(up)), AXES, odd_swap())
    ca = lax.ppermute(line(up), "grp", swap("grp", 0))
    return ra, rb, ya, yb, ca, cb


def on_device(samples, block_ids, tile_counts, occupied, coupling):
    payload = splat(samples, tile_counts, block_ids)
    recv = lax.all_to_all(payload.reshape(SENDERS, 1, ROWS * 128), AXES, split_axis=0, concat_axis=0, tiled=True)
    weights, corner, rowabs, mask = prepare(coupling, occupied)
    v, diag, maskc, centre, *edges = assemble(recv.reshape(SENDERS * ROWS, 128), mask, rowabs)
    fields = [v]
    moments = None
    for order in range(3):
        v, moments, edges = apply_stiffness(
            order, v, diag, mask, maskc, centre, edges, weights, corner, moments
        )
        fields.append(v)
    shared = lax.all_to_all(moments.reshape(SENDERS, 1, 128), AXES, split_axis=0, concat_axis=0, tiled=True)
    outs = finish(shared.reshape(SENDERS, 128), centre, fields)

    def settle(out):
        out = out.reshape(NODES, 2, 2, 2, 128)
        return jnp.transpose(out, (0, 1, 3, 2, 4)).reshape(NODES, 2, 2, BZ)

    return settle(outs[0]), settle(outs[1])


def solution(mesh):
    placed = (P(AXES, None, None), P(AXES), P(AXES), P("slab", "grp", None), P())
    return jax.shard_map(
        on_device,
        mesh=mesh,
        in_specs=placed,
        out_specs=(P(None, "slab", "grp", None), P(None, "slab", "grp", None)),
        check_vma=False,
    )
```

```python
import functools

import jax
import jax.numpy as jnp
from jax import lax
from jax.experimental import pallas as pl
from jax.experimental.pallas import tpu as pltpu
from jax.sharding import PartitionSpec as P

AXES = ("slab", "grp")
F32 = jnp.float32
BF16 = jnp.bfloat16
N_COLS = 4
BZ = 256
NODES = 64
SENDERS = 128
CAP = 8
ROWS = CAP + 1


def lane_iota(shape):
    return lax.broadcasted_iota(jnp.int32, shape, len(shape) - 1)


def row_iota(shape):
    return lax.broadcasted_iota(jnp.int32, shape, 0)


def basis_of(pos):
    u = 4.0 * pos
    w = u - jnp.floor(u)
    back = w - 1.0
    low = back * back
    high = w * w
    turn = w * back
    mid = 1.0 - (turn + turn)
    smid = -(w + back)
    in0, in1, in2 = u < 1.0, u < 2.0, u < 3.0
    zero = jnp.zeros_like(u)

    def nodes(below, at, above):
        return [
            jnp.where(in0, at, jnp.where(in1, below, zero)),
            jnp.where(in0, above, jnp.where(in1, at, jnp.where(in2, below, zero))),
            jnp.where(in0, zero, jnp.where(in1, above, jnp.where(in2, at, below))),
            jnp.where(in1, zero, jnp.where(in2, above, at)),
        ]

    return nodes(low, mid, high), nodes(back, smid, w)


def splat_kernel(samp_ref, cnt_hbm, ids_hbm, out_ref, held, sems, cnt_ref, ids_ref, small_sems, flip, basis, acc, stats):
    groups = out_ref.shape[0]

    def fetch(g):
        return pltpu.make_async_copy(samp_ref.at[:, pl.ds(g * 128, 128), :], held.at[g], sems.at[g])

    def turn(g):
        for k in range(6):
            flip[k] = held[g, k].T

    def evaluate(g):
        counts = cnt_ref[pl.ds(g, 1), :]
        for group in range(16):
            rows = pl.ds(group * 8, 8)
            live = row_iota((8, 128)) + group * 8 < counts
            n0 = jnp.where(live, flip[3, rows, :], 0.0)
            n1 = jnp.where(live, flip[4, rows, :], 0.0)
            n2 = jnp.where(live, flip[5, rows, :], 0.0)
            eighth = jnp.where(live, 0.125, 0.0)
            val, slo = basis_of(flip[0, rows, :])
            for i in range(4):
                basis[i, rows, :] = slo[i] * n0
                basis[4 + i, rows, :] = val[i] * n1
                basis[8 + i, rows, :] = val[i] * n2
                basis[12 + i, rows, :] = val[i] * eighth
            for d in (1, 2):
                val, slo = basis_of(flip[d, rows, :])
                for i in range(4):
                    basis[8 + 8 * d + i, rows, :] = val[i]
                    basis[12 + 8 * d + i, rows, :] = slo[i]

    def accumulate(i, js):
        rhs_sums, dens_sums = {}, {}
        for group in range(16):
            rows = pl.ds(group * 8, 8)
            a = basis[i, rows, :]
            b = basis[4 + i, rows, :]
            c = basis[8 + i, rows, :]
            d = basis[12 + i, rows, :]
            v2 = [basis[24 + l, rows, :] for l in range(4)]
            s2 = [basis[28 + l, rows, :] for l in range(4)]
            for j in js:
                v1 = basis[16 + j, rows, :]
                s1 = basis[20 + j, rows, :]
                first = a * v1 + b * s1
                second = c * v1
                dens = d * v1
                for l in range(4):
                    at = j * 4 + l
                    rhs = first * v2[l] + second * s2[l]
                    den = dens * v2[l]
                    rhs_sums[at] = rhs if group == 0 else rhs_sums[at] + rhs
                    dens_sums[at] = den if group == 0 else dens_sums[at] + den
        for at in rhs_sums:
            acc[pl.ds((i * 16 + at) * 8, 8), :] = rhs_sums[at]
            acc[pl.ds((64 + i * 16 + at) * 8, 8), :] = dens_sums[at]

    def settle(g, real):
        total = acc[pl.ds(0, 128, stride=8), :]
        for s in range(1, 8):
            total = total + acc[pl.ds(s, 128, stride=8), :]
        square = total[:64] * total[:64]
        weighted = total[64:] * square
        part, wpart = square[:8], weighted[:8]
        for k in range(1, 8):
            part = part + square[8 * k : 8 * k + 8]
            wpart = wpart + weighted[8 * k : 8 * k + 8]
        stats[0] = stats[0] + jnp.where(real, part, 0.0)
        stats[1] = stats[1] + jnp.where(real, wpart, 0.0)
        by_tile = total.T
        for d in range(16):
            out_ref[g, pl.ds(ROWS * d, 8), :] = by_tile[8 * d : 8 * d + 8]

    counts_copy = pltpu.make_async_copy(cnt_hbm, cnt_ref, small_sems.at[0])
    ids_copy = pltpu.make_async_copy(ids_hbm, ids_ref, small_sems.at[1])
    fetch(0).start()
    counts_copy.start()
    for g in range(1, groups):
        fetch(g).start()
    ids_copy.start()
    stats[...] = jnp.zeros_like(stats)
    acc[...] = jnp.zeros_like(acc)
    fetch(0).wait()
    turn(0)
    counts_copy.wait()

    def advance(g, carry):
        following = jnp.minimum(g + 1, groups - 1)

        @pl.when(g + 1 < groups)
        def _():
            fetch(following).wait()

        settle(jnp.maximum(g - 1, 0), g > 0)
        evaluate(g)
        turn(following)
        for i in range(4):
            for js in ((0, 1), (2, 3)):
                accumulate(i, js)
        return carry

    lax.fori_loop(0, groups, advance, 0)
    settle(groups - 1, True)
    ids_copy.wait()
    ids = ids_ref[...]
    local = ((ids >> 14) & 1) * 512 + ((ids >> 8) & 1) * 256 + (ids & 255)
    local = local.astype(F32)
    sum0 = jnp.sum(stats[0], keepdims=True)
    sum1 = jnp.sum(stats[1], keepdims=True)
    lanes = lane_iota((1, 128))
    both = jnp.where(lanes % 2 == 0, sum0, sum1)
    for g in range(groups):
        for d in range(16):
            row = jnp.where(lanes // 8 == d, local[g : g + 1], both)
            out_ref[g, pl.ds(ROWS * d + CAP, 1), :] = row


def splat(samples, counts, ids):
    tiles = samples.shape[0]
    groups = tiles // 128
    return pl.pallas_call(
        splat_kernel,
        name="splat",
        in_specs=[pl.BlockSpec(memory_space=pltpu.HBM)] * 3,
        out_specs=pl.BlockSpec(memory_space=pltpu.VMEM),
        out_shape=pltpu.VMEM((groups, 16 * ROWS, 128), F32),
        scratch_shapes=[
            pltpu.VMEM((groups, 6, 128, 128), F32),
            pltpu.SemaphoreType.DMA((groups,)),
            pltpu.VMEM((groups, 128), jnp.int32),
            pltpu.VMEM((groups, 128), jnp.int32),
            pltpu.SemaphoreType.DMA((2,)),
            pltpu.VMEM((6, 128, 128), F32),
            pltpu.VMEM((32, 128, 128), F32),
            pltpu.VMEM((1024, 128), F32),
            pltpu.VMEM((2, 8, 128), F32),
        ],
        compiler_params=pltpu.CompilerParams(vmem_limit_bytes=24 << 20),
    )(hbm(jnp.transpose(samples, (1, 0, 2))), hbm(counts.reshape(groups, 128)), hbm(ids.reshape(groups, 128)))


def hbm(x):
    return pltpu.with_memory_space_constraint(x, pltpu.HBM)


def vmem(x):
    return pltpu.with_memory_space_constraint(x, pltpu.VMEM)


def parity_weights():
    slab, grp = lax.axis_index("slab"), lax.axis_index("grp")
    slabs, grps = lax.axis_size("slab"), lax.axis_size("grp")

    def pick(cond):
        return jnp.where(cond, 1.0, 0.0).astype(F32)

    def sides(at, count):
        odd = at % 2 == 1
        low = (pick(odd), pick(jnp.logical_and(jnp.logical_not(odd), at > 0)))
        high = (pick(jnp.logical_not(odd)), pick(jnp.logical_and(odd, at < count - 1)))
        return low, high

    return sides(slab, slabs), sides(grp, grps)


def blend(pair, a, b):
    return a * pair[0] + b * pair[1]


def column(x, y):
    return pl.ds((x * 2 + y) * BZ, BZ)


def store_edges(masked, ea_ref, eb_ref, oa_ref, ob_ref):
    up_slab = lax.axis_index("slab") % 2 == 0
    up_grp = lax.axis_index("grp") % 2 == 0
    for k in range(2):
        at = pl.ds(k * BZ, BZ)
        ea_ref[:, at] = jnp.where(up_slab, masked[1][k], masked[0][k])
        eb_ref[:, at] = jnp.where(up_slab, masked[0][k], masked[1][k])
        oa_ref[:, at] = jnp.where(up_grp, masked[k][1], masked[k][0])
        ob_ref[:, at] = jnp.where(up_grp, masked[k][0], masked[k][1])


def spread(part):
    lanes = lane_iota((NODES, BZ))
    before = jnp.where(lanes == 0, 0.0, pltpu.roll(part[:NODES], 1, 1))
    after = jnp.where(lanes == BZ - 1, 0.0, pltpu.roll(part[2 * NODES :], BZ - 1, 1))
    return part[NODES : 2 * NODES] + before + after


def split(src):
    top = src.astype(BF16)
    return top, (src - top.astype(F32)).astype(BF16)


def prepare_kernel(coupling_ref, occ_ref, w_ref, corner_ref, rowabs_ref, mask_ref):
    total = jnp.zeros((NODES, NODES), F32)
    high, low = {}, {}
    for dz in range(3):
        rows = pl.ds(dz * NODES, NODES)
        for dx in range(3):
            for dy in range(3):
                k = (dx * 3 + dy) * 3 + dz
                coupled = 0.5 * (coupling_ref[k] + coupling_ref[26 - k].T)
                total = total + jnp.abs(coupled)
                high[dx, dy], low[dx, dy] = split(coupled)
            w_ref[dx, rows, :] = jnp.concatenate([high[dx, dy] for dy in range(3)], axis=1)
            w_ref[dx, pl.ds((3 + dz) * NODES, NODES), :] = jnp.concatenate([low[dx, dy] for dy in range(3)], axis=1)
        for x in range(2):
            for y in range(2):
                at = (2 * x, 2 * y)
                corner_ref[x * 2 + y, rows, :] = jnp.concatenate([high[at], low[at], high[at]], axis=1)
    rowabs_ref[...] = jnp.broadcast_to(jnp.sum(total, axis=1, keepdims=True), (NODES, 128))
    for x in range(2):
        for y in range(2):
            mask_ref[:, column(x, y)] = jnp.broadcast_to(occ_ref[x, y : y + 1, :].astype(F32), (8, BZ))


def prepare(coupling, occupied):
    return pl.pallas_call(
        prepare_kernel,
        name="prepare",
        in_specs=[pl.BlockSpec(memory_space=pltpu.VMEM)] * 2,
        out_specs=[pl.BlockSpec(memory_space=pltpu.VMEM)] * 4,
        out_shape=[
            pltpu.VMEM((3, 6 * NODES, 3 * NODES), BF16),
            pltpu.VMEM((4, 3 * NODES, 3 * NODES), BF16),
            pltpu.VMEM((NODES, 128), F32),
            pltpu.VMEM((8, N_COLS * BZ), F32),
        ],
        compiler_params=pltpu.CompilerParams(vmem_limit_bytes=12 << 20),
        cost_estimate=pl.CostEstimate(flops=10**7, transcendentals=0, bytes_accessed=4 * 10**6),
    )(coupling, occupied)


def assemble_kernel(recv_ref, mask_ref, rowabs_ref, v_ref, diag_ref, maskc_ref, c_ref,
                    ea_ref, eb_ref, oa_ref, ob_ref, turned):
    seat = lax.axis_index("grp") % 16
    turned[...] = recv_ref[pl.ds(CAP, SENDERS, stride=ROWS), :].T
    where = turned[pl.ds(pl.multiple_of(seat * 8, 8), 8), :].astype(jnp.int32)
    other = lax.rem(seat + 1, 16)
    sums = turned[pl.ds(pl.multiple_of(other * 8, 8), 8), :]
    sum0 = jnp.sum(sums[0:1, :], keepdims=True)
    sum1 = jnp.sum(sums[1:2, :], keepdims=True)
    rowabs = rowabs_ref[...]
    mean = jnp.sum(rowabs[:, 0:1], keepdims=True) * (1.0 / NODES)
    centre = mean + 0.5 + 4.0 * (sum1 / sum0)
    inverse = 1.0 / centre
    c_ref[...] = jnp.broadcast_to(centre, (8, 128))
    tiles = []
    for c in range(CAP):
        block = recv_ref[pl.ds(c, SENDERS, stride=ROWS), :]
        high = block.astype(BF16)
        low = (block - high.astype(F32)).astype(BF16)
        tiles.append(jnp.concatenate([high, low], axis=1))
    table = jnp.concatenate(tiles, axis=0)
    masked = []
    for x in range(2):
        masked.append([])
        for y in range(2):
            picks = []
            for c in range(CAP):
                hit = row_iota((BZ, SENDERS)) + (x * 2 + y) * BZ == where[c : c + 1, :]
                picks.append(hit.astype(F32).astype(BF16))
            pick = jnp.concatenate(picks, axis=1)
            both = jnp.dot(pick, table, preferred_element_type=F32)
            ordered = (both[:, :128] + both[:, 128:]).T
            rhs = ordered[:NODES]
            dens = ordered[NODES:]
            mask = mask_ref[0:1, column(x, y)]
            v_ref[:, column(x, y)] = rhs
            diag = rowabs[:, 0:1] + 0.5 + 4.0 * dens
            diag_ref[:, column(x, y)] = (diag - centre) * inverse
            maskc_ref[:, column(x, y)] = jnp.broadcast_to(mask * inverse, (8, BZ))
            masked[x].append(rhs * mask)
    store_edges(masked, ea_ref, eb_ref, oa_ref, ob_ref)


FIELD = pltpu.VMEM((NODES, N_COLS * BZ), F32)
EDGE = pltpu.VMEM((NODES, 2 * BZ), F32)


def in_specs(count):
    return [pl.BlockSpec(memory_space=pltpu.VMEM)] * count


def assemble(recv, mask, rowabs):
    return pl.pallas_call(
        assemble_kernel,
        name="assemble",
        in_specs=in_specs(3),
        out_specs=[pl.BlockSpec(memory_space=pltpu.VMEM)] * 8,
        out_shape=[FIELD, FIELD, pltpu.VMEM((8, N_COLS * BZ), F32), pltpu.VMEM((8, 128), F32), EDGE, EDGE, EDGE, EDGE],
        scratch_shapes=[pltpu.VMEM((128, 128), F32)],
        compiler_params=pltpu.CompilerParams(vmem_limit_bytes=16 << 20),
    )(vmem(recv), vmem(mask), vmem(rowabs))


def product(weights, source):
    high, low = split(source)
    stacked = jnp.concatenate([high, high, low], axis=0)
    return spread(jnp.dot(weights, stacked, preferred_element_type=F32))


def put_moments(order, mom_ref, mom_out, sq, cross):
    sq = jnp.sum(sq, keepdims=True)
    cross = jnp.sum(cross, keepdims=True)
    spot = lane_iota((1, 128))
    before = jnp.zeros((1, 128), F32) if mom_ref is None else mom_ref[0:1, :]
    mom = jnp.where(spot == 2 * order, sq, jnp.where(spot == 2 * order + 1, cross, before))
    mom_out[...] = jnp.broadcast_to(mom, mom_out.shape)


def sides_kernel(last, v_ref, mask_ref, ra_ref, rb_ref, ya_ref, yb_ref, w_ref, *rest):
    if last:
        corner_ref, diag_ref, maskc_ref, c_ref, mom_ref, o_ref, mom_out, high, low = rest
    else:
        o_ref, high, low = rest
    (x_low, x_high), (y_low, y_high) = parity_weights()
    halo, rise = {}, {}

    def at_rows(px, py):
        return pl.ds((px * 4 + py) * NODES, NODES)

    def put(px, py, src):
        high[at_rows(px, py), :], low[at_rows(px, py), :] = split(src)

    for x in range(2):
        for y in range(2):
            put(x + 1, y + 1, v_ref[:, column(x, y)] * mask_ref[0:1, column(x, y)])
    for k in range(2):
        at = pl.ds(k * BZ, BZ)
        halo[k] = (blend(x_low, ra_ref[:, at], rb_ref[:, at]), blend(x_high, ra_ref[:, at], rb_ref[:, at]))
        put(0, k + 1, halo[k][0])
        put(3, k + 1, halo[k][1])
        rise[k] = (blend(y_low, ya_ref[:, at], yb_ref[:, at]), blend(y_high, ya_ref[:, at], yb_ref[:, at]))
        put(k + 1, 0, rise[k][0])
        put(k + 1, 3, rise[k][1])
    nothing = jnp.zeros((NODES, BZ), BF16)
    for px in (0, 3):
        for py in (0, 3):
            high[at_rows(px, py), :] = nothing
            low[at_rows(px, py), :] = nothing
    sq = jnp.zeros((NODES, BZ), F32)
    cross = jnp.zeros((NODES, BZ), F32)
    for x in range(2):
        for y in range(2):
            full = jnp.zeros((6 * NODES, BZ), F32)
            half = jnp.zeros((3 * NODES, BZ), F32)
            for dx in range(3):
                rows = pl.ds(((x + dx) * 4 + y) * NODES, 3 * NODES)
                full = full + jnp.dot(w_ref[dx], high[rows, :], preferred_element_type=F32)
                half = half + jnp.dot(w_ref[dx, 0 : 3 * NODES, :], low[rows, :], preferred_element_type=F32)
            at = column(x, y)
            total = spread(full[: 3 * NODES] + full[3 * NODES :] + half)
            o_ref[:, at] = total
            if last:
                v = v_ref[:, at]
                sq = sq + v * v
                cross = cross + v * (diag_ref[:, at] * v - maskc_ref[0:1, at] * total)
    if not last:
        return
    energy = jnp.zeros((NODES, BZ), F32)
    for x in range(2):
        for y in range(2):
            energy = energy + halo[y][x] * product(corner_ref[(1 - x) * 2 + y], rise[x][y])
    cross = cross - energy * (1.0 / c_ref[0:1, 0:1])
    put_moments(2, mom_ref, mom_out, sq, cross)


def sides(operands, last):
    shapes = [FIELD] + ([pltpu.VMEM((SENDERS, 128), F32)] if last else [])
    return pl.pallas_call(
        functools.partial(sides_kernel, last),
        name="sides",
        in_specs=in_specs(len(operands)),
        out_specs=[pl.BlockSpec(memory_space=pltpu.VMEM)] * len(shapes),
        out_shape=shapes,
        scratch_shapes=[pltpu.VMEM((16 * NODES, BZ), BF16), pltpu.VMEM((16 * NODES, BZ), BF16)],
        compiler_params=pltpu.CompilerParams(vmem_limit_bytes=16 << 20),
        cost_estimate=pl.CostEstimate(flops=15 * 10**8, transcendentals=0, bytes_accessed=2 * 10**6),
    )(*[vmem(x) for x in operands])


def corners_kernel(order, last, sum_ref, v_ref, diag_ref, mask_ref, maskc_ref, ca_ref, cb_ref, corner_ref, *rest):
    rest = list(rest)
    mom_ref = rest.pop(0) if order and not last else None
    o_ref = rest.pop(0)
    x_pairs, y_pairs = parity_weights()
    sq = jnp.zeros((NODES, BZ), F32)
    cross = jnp.zeros((NODES, BZ), F32)
    masked = [[], []]
    for y in range(2):
        line = [blend(y_pairs[y], ca_ref[:, pl.ds(k * BZ, BZ)], cb_ref[:, pl.ds(k * BZ, BZ)]) for k in range(2)]
        for x in range(2):
            at = column(x, y)
            total = sum_ref[:, at] + product(corner_ref[x * 2 + y], blend(x_pairs[x], line[0], line[1]))
            v = v_ref[:, at]
            new = diag_ref[:, at] * v - maskc_ref[0:1, at] * total
            o_ref[:, at] = new
            if not last:
                masked[x].append(new * mask_ref[0:1, at])
                sq = sq + v * v
                cross = cross + v * new
    if not last:
        store_edges(masked, *rest[1:])
        put_moments(order, mom_ref, rest[0], sq, cross)


def corners(order, operands, last):
    shapes = [FIELD] + ([] if last else [pltpu.VMEM((8, 128), F32)] + [EDGE] * 4)
    return pl.pallas_call(
        functools.partial(corners_kernel, order, last),
        name="corners",
        in_specs=in_specs(len(operands)),
        out_specs=[pl.BlockSpec(memory_space=pltpu.VMEM)] * len(shapes),
        out_shape=shapes,
        compiler_params=pltpu.CompilerParams(vmem_limit_bytes=16 << 20),
        cost_estimate=pl.CostEstimate(flops=5 * 10**8, transcendentals=0, bytes_accessed=2 * 10**6),
    )(*[vmem(x) for x in operands])


def apply_stiffness(order, v, diag, mask, maskc, centre, edges, weights, corner, moments):
    last = order == 2
    ra, rb, ya, yb, ca, cb = exchange(lax.axis_index("grp"), *edges)
    operands = [v, mask, ra, rb, ya, yb, weights] + ([corner, diag, maskc, centre, moments] if last else [])
    part, *shared = sides(operands, last)
    operands = [part, v, diag, mask, maskc, ca, cb, corner]
    if last:
        return corners(order, operands, last)[0], shared[0], []
    new, moments, *edges = corners(order, operands + ([] if moments is None else [moments]), last)
    return new, moments, edges


def finish_kernel(mom_ref, c_ref, v0_ref, v1_ref, v2_ref, v3_ref, x_ref, r_ref):
    row = jnp.sum(mom_ref[...], axis=0, keepdims=True)
    lanes = lane_iota((1, 128))
    m = [jnp.sum(jnp.where(lanes == k, row, 0.0), keepdims=True) for k in range(6)]
    zero = jnp.zeros((1, 1), F32)
    one = jnp.ones((1, 1), F32)

    def inner(f, g):
        total = zero
        for i, a in enumerate(f):
            for j, b in enumerate(g):
                if a is not None and b is not None:
                    total = total + a * b * m[i + j]
        return total

    r = [one, None, None, None]
    p = [one, None, None, None]
    x = [None, None, None]
    norm = m[0]

    def plus(a, b):
        if a is None:
            return b
        return a if b is None else a + b

    for step in range(3):
        image = [plus(p[k], p[k - 1] if k else None) for k in range(4)]
        alpha = norm / inner(p, image)
        for k in range(3):
            if p[k] is not None:
                x[k] = plus(x[k], alpha * p[k])
        for k in range(4):
            if image[k] is not None:
                r[k] = plus(r[k], -(alpha * image[k]))
        if step < 2:
            new = inner(r, r)
            beta = new / norm
            p = [plus(r[k], None if p[k] is None else beta * p[k]) for k in range(4)]
            norm = new
    inverse = 1.0 / c_ref[0:1, 0:1]
    x = [value * inverse for value in x]
    for chunk in range(8):
        bx, by, zt = chunk // 4, chunk // 2 % 2, chunk % 2
        spot = bx * 4 + zt * 2 + by
        at = pl.ds(chunk * 128, 128)
        v0, v1, v2, v3 = v0_ref[:, at], v1_ref[:, at], v2_ref[:, at], v3_ref[:, at]
        x_ref[:, spot, :] = x[0] * v0 + x[1] * v1 + x[2] * v2
        r_ref[:, spot, :] = r[0] * v0 + r[1] * v1 + r[2] * v2 + r[3] * v3


def finish(moments, centre, fields):
    out = jax.ShapeDtypeStruct((NODES, 8, 128), F32)
    return pl.pallas_call(
        finish_kernel,
        name="finish",
        in_specs=[pl.BlockSpec(memory_space=pltpu.VMEM)] * 6,
        out_specs=[pl.BlockSpec(memory_space=pltpu.VMEM)] * 2,
        out_shape=[out, out],
        compiler_params=pltpu.CompilerParams(vmem_limit_bytes=16 << 20),
    )(moments, *[vmem(x) for x in (centre, *fields)])


def swap(axis, first):
    count = lax.axis_size(axis)
    return [(i, (i + 1 if (i - first) % 2 == 0 else i - 1) % count) for i in range(count)]


def odd_swap():
    slabs, grps = lax.axis_size("slab"), lax.axis_size("grp")
    pairs = []
    for s in range(slabs):
        for g in range(grps):
            if g in (0, grps - 1):
                pairs.append((s * grps + g, (s ^ 1) * grps + g))
            else:
                pairs.append((s * grps + g, s * grps + (g + 1 if g % 2 else g - 1)))
    return pairs


def exchange(grp, ea, eb, oa, ob):
    yb = lax.ppermute(ob, AXES, odd_swap())
    ra = lax.ppermute(ea, "slab", swap("slab", 0))
    rb = lax.ppermute(eb, "slab", swap("slab", 1))
    ya = lax.ppermute(oa, "grp", swap("grp", 0))
    up = grp % 2 == 0

    def line(upper):
        return jnp.concatenate([jnp.where(upper, r[:, BZ:], r[:, :BZ]) for r in (ra, rb)], axis=1)

    cb = lax.ppermute(line(jnp.logical_not(up)), AXES, odd_swap())
    ca = lax.ppermute(line(up), "grp", swap("grp", 0))
    return ra, rb, ya, yb, ca, cb


def on_device(samples, block_ids, tile_counts, occupied, coupling):
    payload = splat(samples, tile_counts, block_ids)
    recv = lax.all_to_all(payload.reshape(SENDERS, 1, ROWS * 128), AXES, split_axis=0, concat_axis=0, tiled=True)
    weights, corner, rowabs, mask = prepare(coupling, occupied)
    v, diag, maskc, centre, *edges = assemble(recv.reshape(SENDERS * ROWS, 128), mask, rowabs)
    fields = [v]
    moments = None
    for order in range(3):
        v, moments, edges = apply_stiffness(
            order, v, diag, mask, maskc, centre, edges, weights, corner, moments
        )
        fields.append(v)
    shared = lax.all_to_all(moments.reshape(SENDERS, 1, 128), AXES, split_axis=0, concat_axis=0, tiled=True)
    outs = finish(shared.reshape(SENDERS, 128), centre, fields)

    def settle(out):
        out = out.reshape(NODES, 2, 2, 2, 128)
        return jnp.transpose(out, (0, 1, 3, 2, 4)).reshape(NODES, 2, 2, BZ)

    return settle(outs[0]), settle(outs[1])


def solution(mesh):
    placed = (P(AXES, None, None), P(AXES), P(AXES), P("slab", "grp", None), P())
    return jax.shard_map(
        on_device,
        mesh=mesh,
        in_specs=placed,
        out_specs=(P(None, "slab", "grp", None), P(None, "slab", "grp", None)),
        check_vma=False,
    )
```
